32 devices in a mesh: fsdp: 8 (over z, core), ctx: 2 (over x), tp: 2 (over y).
Axes of the slice: x: 2, y: 2, z: 4, core: 2. Of those that a mesh axis runs over, the one named last changes fastest.
Arguments:
- tokens: bfloat16 [16, 1024, 1024], P('fsdp', 'ctx'), may hold values from -6 to 6
- picture_starts: int32 [16, 2], P('fsdp'), may hold values from 0 to 768, as said below
- ln1_gain: bfloat16 [1024], P('fsdp'), may hold values from 0.5 to 2
- ln1_shift: bfloat16 [1024], P('fsdp'), may hold values from -3 to 3
- w_qkv: bfloat16 [1024, 3, 1024], P('fsdp', None, 'tp'), may hold values from -0.1875 to 0.1875
- qv_bias: bfloat16 [2, 16, 64], P(None, 'tp', 'fsdp'), may hold values from -0.59765625 to 0.59765625
- w_proj: bfloat16 [1024, 1024], P('tp', 'fsdp'), may hold values from -1.5 to 1.5
- proj_bias: bfloat16 [1024], P('fsdp'), may hold values from -3 to 3
- ln2_gain: bfloat16 [1024], P('fsdp'), may hold values from 0.5 to 2
- ln2_shift: bfloat16 [1024], P('fsdp'), may hold values from -3 to 3
- w_fc1: bfloat16 [1024, 4096], P('fsdp', 'tp'), may hold values from -0.1875 to 0.1875
- fc1_bias: bfloat16 [64, 64], P('tp', 'fsdp'), may hold values from -3 to 3
- w_fc2: bfloat16 [4096, 1024], P('tp', 'fsdp'), may hold values from -0.09375 to 0.09375
- fc2_bias: bfloat16 [1024], P('fsdp'), may hold values from -3 to 3
- out_grad: bfloat16 [16, 1024, 1024], P('fsdp', 'ctx'), may hold values from -6 to 6
Outputs:
- output: bfloat16 [16, 1024, 1024], P('fsdp', 'ctx')
- grad_tokens: bfloat16 [16, 1024, 1024], P('fsdp', 'ctx')
- grad_ln1_gain: float32 [1024], P('fsdp')
- grad_ln1_shift: float32 [1024], P('fsdp')
- grad_w_qkv: float32 [1024, 3, 1024], P('fsdp', None, 'tp')
- grad_qv_bias: float32 [2, 16, 64], P(None, 'tp', 'fsdp')
- grad_w_proj: float32 [1024, 1024], P('tp', 'fsdp')
- grad_proj_bias: float32 [1024], P('fsdp')
- grad_ln2_gain: float32 [1024], P('fsdp')
- grad_ln2_shift: float32 [1024], P('fsdp')
- grad_w_fc1: float32 [1024, 4096], P('fsdp', 'tp')
- grad_fc1_bias: float32 [64, 64], P('tp', 'fsdp')
- grad_w_fc2: float32 [4096, 1024], P('tp', 'fsdp')
- grad_fc2_bias: float32 [1024], P('fsdp')
The draws below stay inside these ranges and needn't reach their ends.
Inputs may be any that keep to these rules, and one draw needn't show every extreme that they name: `picture_starts`: each start is a multiple of 256; the 2 starts of one sequence differ.
All inputs are finite; a program needn't handle non-finite values.
Results may differ from the reference program's by a relative error of at most 0.018.
Values may be sent and summed in bfloat16 or wider, within the bound.
No kernel may reach another device: no remote copies, remote signals or barrier semaphores. Data moves between devices by JAX's collectives and lax.ppermute only.
A program may use at most 640 MiB of HBM per device.

```python
import math
import jax
import jax.numpy as jnp
from jax import lax

D = 1024
HEADS = 16
HD = 64
FF = 4096
PIECE = 256
PICS = 2
LEN = 1024
SEQS = 16


def draw_picture_starts(key, part):
    block_count = LEN // PIECE
    row_keys = jax.random.split(key, SEQS)

    def shuffle(row_key):
        return jax.random.permutation(row_key, block_count)
    orders = jax.vmap(shuffle)(row_keys)[:, :PICS].astype(jnp.int32)
    forced = jax.random.randint(jax.random.fold_in(key, 7), (), 0, SEQS)
    fixed_row = ((jnp.arange(PICS) + block_count - 1) % block_count).astype(jnp.int32)
    row_ids = jnp.arange(SEQS)
    chosen = jnp.where((row_ids == forced)[:, None], fixed_row[None, :], orders)
    return (chosen * PIECE).astype(jnp.int32)


def levels(key, shape, shards, low, largest):
    level = 1.0
    for dim, blocks in shards:
        draws = jax.random.uniform(jax.random.fold_in(jax.random.fold_in(key, 6), dim), (blocks,), jnp.float32, low / len(shards), largest / len(shards))
        level = level * jnp.repeat(jnp.exp(draws), shape[dim] // blocks).reshape((-1,) + (1,) * (len(shape) - 1 - dim))
    return level


def bell_draw(stream_key, extent, width, bound, pieces=(), held_as=jnp.bfloat16):
    array = width * jax.random.normal(stream_key, extent, jnp.float32)
    if pieces:
        array = array * levels(stream_key, extent, pieces, -0.22, 0.18)
    return jnp.clip(array, -bound, bound).astype(held_as)


def setup_inputs(seed: int = 0) -> dict:
    arg_keys = jax.random.split(jax.random.key(seed), 16)
    tokens = bell_draw(arg_keys[0], (SEQS, LEN, D), 1.0, 6.0, ((0, 8), (1, 2)))
    picture_starts = draw_picture_starts(jax.random.fold_in(arg_keys[15], 71), 0)
    ln1_gain = jnp.clip(jnp.exp(math.log(2.0) - 1.3862944 * jax.random.uniform(arg_keys[2], (D,), jnp.float32) ** levels(arg_keys[2], (D,), ((0, 8),), -0.2, 0.2)), 0.5, 2.0).astype(jnp.bfloat16)
    ln1_shift = bell_draw(arg_keys[3], (D,), 0.5, 3.0, ((0, 8),))
    w_qkv = bell_draw(arg_keys[4], (D, 3, D), D ** -0.5, 0.1875, ((0, 8), (2, 2)))
    qv_bias = bell_draw(arg_keys[5], (2, HEADS, HD), 0.1, 0.59765625, ((1, 2), (2, 8)))
    w_proj = bell_draw(arg_keys[6], (D, D), (D // 64) ** -0.5, 1.5, ((0, 2), (1, 8)))
    proj_bias = bell_draw(arg_keys[7], (D,), 0.5, 3.0, ((0, 8),))
    ln2_gain = jnp.clip(jnp.exp(math.log(2.0) - 1.3862944 * jax.random.uniform(arg_keys[8], (D,), jnp.float32) ** levels(arg_keys[8], (D,), ((0, 8),), -0.2, 0.2)), 0.5, 2.0).astype(jnp.bfloat16)
    ln2_shift = bell_draw(arg_keys[9], (D,), 0.5, 3.0, ((0, 8),))
    w_fc1 = bell_draw(arg_keys[10], (D, FF), D ** -0.5, 0.1875, ((0, 8), (1, 2)))
    fc1_bias = bell_draw(arg_keys[11], (FF // HD, HD), 0.5, 3.0, ((0, 2), (1, 8)))
    w_fc2 = bell_draw(arg_keys[12], (FF, D), FF ** -0.5, 0.09375, ((0, 2), (1, 8)))
    fc2_bias = bell_draw(arg_keys[13], (D,), 0.5, 3.0, ((0, 8),))
    out_grad = bell_draw(arg_keys[14], (SEQS, LEN, D), 1.0, 6.0, ((0, 8), (1, 2)))
    return {"tokens": tokens, "picture_starts": picture_starts, "ln1_gain": ln1_gain, "ln1_shift": ln1_shift, "w_qkv": w_qkv, "qv_bias": qv_bias, "w_proj": w_proj, "proj_bias": proj_bias, "ln2_gain": ln2_gain, "ln2_shift": ln2_shift, "w_fc1": w_fc1, "fc1_bias": fc1_bias, "w_fc2": w_fc2, "fc2_bias": fc2_bias, "out_grad": out_grad}


@jax.custom_vjp
def low(v):
    return lax.optimization_barrier(v.astype(jnp.bfloat16)).astype(jnp.float32)

@jax.custom_vjp
def low_back(v):
    return v

def low_keep(v):
    return (low(v), None)

def low_pass(kept, grad):
    return (grad,)

def back_keep(v):
    return (v, None)

def back_low(kept, grad):
    return (low(grad),)
low.defvjp(low_keep, low_pass)
low_back.defvjp(back_keep, back_low)

def exact_dot(left_op, right_op):
    return jnp.dot(left_op, right_op, precision=lax.Precision.HIGHEST)

def layer_norm(values, gain_vec, shift_vec):
    average = lax.optimization_barrier(jnp.mean(values, axis=-1, keepdims=True))
    centred = values - average
    variance = lax.optimization_barrier(jnp.mean(centred * centred, axis=-1, keepdims=True))
    return centred * lax.rsqrt(variance + 1e-05) * gain_vec + shift_vec

def visible_mask(starts):
    positions = jnp.arange(LEN, dtype=jnp.int32)
    causal = positions[None, :] <= positions[:, None]
    blocks = positions // PIECE
    start_blocks = (starts // PIECE).astype(jnp.int32)
    picture = jnp.any(blocks[:, None] == start_blocks[None, :], axis=1)
    joined = (blocks[:, None] == blocks[None, :]) & picture[:, None]
    return causal | joined

def attend_one(packed):
    queries, key_rows, value_rows, starts = packed
    scores = jnp.einsum('qhd,khd->hqk', queries, key_rows, precision=lax.Precision.HIGHEST) * HD ** (-0.5)
    scores = low_back(scores)
    visible = visible_mask(starts)[None]
    masked = jnp.where(visible, scores, -1e+30)
    row_peak = lax.optimization_barrier(jnp.max(masked, axis=-1, keepdims=True))
    exponent = jnp.where(visible, jnp.exp(masked - row_peak), 0.0)
    attention_probs = exponent / lax.optimization_barrier(jnp.sum(exponent, axis=-1, keepdims=True))
    return jnp.einsum('hqk,khd->qhd', low(attention_probs), value_rows, precision=lax.Precision.HIGHEST)

def forward(float_args, picture_starts):
    tokens, ln1_gain, ln1_shift, w_qkv, qv_bias, w_proj, proj_bias, ln2_gain, ln2_shift, w_fc1, fc1_bias, w_fc2, fc2_bias = float_args
    flat_rows = tokens.reshape(SEQS * LEN, D)
    normed_one = low(layer_norm(flat_rows, ln1_gain, ln1_shift))
    projected = exact_dot(normed_one, w_qkv.reshape(D, 3 * D)).reshape(SEQS * LEN, 3, D)
    qv_rows = qv_bias.reshape(2, D)
    bias_rows = jnp.stack([qv_rows[0], jnp.zeros_like(qv_rows[0]), qv_rows[1]])
    triple = low_back(low(projected + bias_rows[None]))
    shaped = triple.reshape(SEQS, LEN, 3, HEADS, HD)
    attended = lax.map(jax.checkpoint(attend_one), (shaped[:, :, 0], shaped[:, :, 1], shaped[:, :, 2], picture_starts))
    head_out = low_back(low(attended.reshape(SEQS * LEN, D)))
    branch = low_back(exact_dot(head_out, w_proj) + proj_bias)
    residual = flat_rows + branch
    normed_two = low(layer_norm(residual, ln2_gain, ln2_shift))
    hidden_pre = low_back(exact_dot(normed_two, w_fc1) + fc1_bias.reshape(FF))
    active = low(jax.nn.gelu(hidden_pre, approximate=True))
    output = residual + exact_dot(active, w_fc2) + fc2_bias
    return output.reshape(SEQS, LEN, D)

def reference(tokens, picture_starts, ln1_gain, ln1_shift, w_qkv, qv_bias, w_proj, proj_bias, ln2_gain, ln2_shift, w_fc1, fc1_bias, w_fc2, fc2_bias, out_grad):
    float_args = tuple((element.astype(jnp.float32) for element in (tokens, ln1_gain, ln1_shift, w_qkv, qv_bias, w_proj, proj_bias, ln2_gain, ln2_shift, w_fc1, fc1_bias, w_fc2, fc2_bias)))

    def wrapped(*floats):
        return forward(floats, picture_starts)
    output, pullback = jax.vjp(wrapped, *float_args)
    gradients = pullback(out_grad.astype(jnp.float32))
    return (output.astype(jnp.bfloat16), gradients[0].astype(jnp.bfloat16), gradients[1], gradients[2], gradients[3], gradients[4], gradients[5], gradients[6], gradients[7], gradients[8], gradients[9], gradients[10], gradients[11], gradients[12])
```

```python
import jax
import jax.numpy as jnp
from jax import lax
from jax.experimental import pallas as pl
from jax.experimental.pallas import tpu as pltpu
from jax.sharding import PartitionSpec as P

HD = 64
PAIR = 2 * HD
PIECE = 256
SCALE = HD ** (-0.5)
KERNEL_VMEM = 48 * 1024 * 1024

epsilon = 1e-05
masked_value = -1e30


def layer_norm(values, gain_vec, shift_vec):
    average = jnp.mean(values, axis=-1, keepdims=True)
    centred = values - average
    variance = jnp.mean(centred * centred, axis=-1, keepdims=True)
    return centred * lax.rsqrt(variance + epsilon) * gain_vec + shift_vec


def gelu_tanh(values):
    return jax.nn.gelu(values, approximate=True)


NT = (((1,), (1,)), ((), ()))


def dot_nt(left, right):
    return lax.dot_general(left, right, NT, preferred_element_type=jnp.float32)


def dot_nn(left, right):
    return jnp.dot(left, right, preferred_element_type=jnp.float32)


def head_lanes(head):
    lanes = lax.broadcasted_iota(jnp.int32, (1, PAIR), 1)
    return (lanes >= head * HD) & (lanes < (head + 1) * HD)


def only_head(rows, head):
    return jnp.where(head_lanes(head), rows, jnp.zeros_like(rows))


def diagonal_mask(scores, joined):
    key_row = lax.broadcasted_iota(jnp.int32, scores.shape, 0)
    query_lane = lax.broadcasted_iota(jnp.int32, scores.shape, 1)
    return (key_row <= query_lane) | joined


def attention_forward_kernel(place, pictures, q_ref, k_ref, v_ref, out_ref, log_ref):
    rank = place[0]
    sequence = pl.program_id(0)
    local_len = q_ref.shape[1]
    blocks = local_len // PIECE
    own = pl.multiple_of(rank * local_len, local_len)
    key_own = k_ref[0, pl.ds(own, local_len), :]
    value_own = v_ref[0, pl.ds(own, local_len), :].T
    states = []
    scaled = []
    for head in range(2):
        for block in range(blocks):
            rows = slice(block * PIECE, (block + 1) * PIECE)
            query = only_head(q_ref[0, rows, :] * SCALE, head)
            scaled.append(query)
            joined = pictures[sequence, rank * blocks + block] > 0
            diagonal = dot_nt(key_own[rows], query)
            diagonal = jnp.where(diagonal_mask(diagonal, joined), diagonal, masked_value)
            peak = jnp.max(diagonal, axis=0, keepdims=True)
            value_head = value_own[head * HD : (head + 1) * HD]
            if block:
                before = dot_nt(key_own[: block * PIECE], query)
                peak = jnp.maximum(peak, jnp.max(before, axis=0, keepdims=True))
            weight = jnp.exp(diagonal - peak)
            total = jnp.sum(weight, axis=0, keepdims=True)
            gathered = dot_nn(value_head[:, rows], weight.astype(jnp.bfloat16))
            if block:
                weight = jnp.exp(before - peak)
                total = total + jnp.sum(weight, axis=0, keepdims=True)
                gathered = gathered + dot_nn(
                    value_head[:, : block * PIECE], weight.astype(jnp.bfloat16)
                )
            states.append((peak, total, gathered))

    def earlier(step, carried):
        start = pl.multiple_of(step * local_len, local_len)
        keys = k_ref[0, pl.ds(start, local_len), :]
        values = v_ref[0, pl.ds(start, local_len), :].T
        after = []
        for index, (peak, total, gathered) in enumerate(carried):
            head = index // blocks
            scores = dot_nt(keys, scaled[index])
            new_peak = jnp.maximum(peak, jnp.max(scores, axis=0, keepdims=True))
            shrink = jnp.exp(peak - new_peak)
            weight = jnp.exp(scores - new_peak)
            after.append(
                (
                    new_peak,
                    shrink * total + jnp.sum(weight, axis=0, keepdims=True),
                    shrink * gathered
                    + dot_nn(values[head * HD : (head + 1) * HD], weight.astype(jnp.bfloat16)),
                )
            )
        return after

    states = lax.fori_loop(0, rank, earlier, states)
    for block in range(blocks):
        rows = slice(block * PIECE, (block + 1) * PIECE)
        halves = []
        for head in range(2):
            peak, total, gathered = states[head * blocks + block]
            halves.append(gathered / total)
            log_ref[0, 0, head : head + 1, rows] = peak + jnp.log(total)
        out_ref[0, rows, :] = jnp.concatenate(halves, axis=0).T.astype(out_ref.dtype)


def attention_forward(triple, place, pictures, local_len):
    seq_count, full_len, triple_width = triple.shape
    local_width = triple_width // 3
    pairs = local_width // PAIR
    rows = seq_count * local_len
    return pl.pallas_call(
        attention_forward_kernel,
        grid_spec=pltpu.PrefetchScalarGridSpec(
            num_scalar_prefetch=2,
            grid=(seq_count, pairs),
            in_specs=[
                pl.BlockSpec((1, local_len, PAIR), lambda s, p, place, pics: (s, place[0], p)),
                pl.BlockSpec((1, full_len, PAIR), lambda s, p, place, pics: (s, 0, pairs + p)),
                pl.BlockSpec((1, full_len, PAIR), lambda s, p, place, pics: (s, 0, 2 * pairs + p)),
            ],
            out_specs=[
                pl.BlockSpec((1, local_len, PAIR), lambda s, p, place, pics: (s, 0, p)),
                pl.BlockSpec((1, 1, 2, local_len), lambda s, p, place, pics: (s, p, 0, 0)),
            ],
        ),
        out_shape=[
            jax.ShapeDtypeStruct((seq_count, local_len, local_width), jnp.bfloat16),
            jax.ShapeDtypeStruct((seq_count, pairs, 2, local_len), jnp.float32),
        ],
        compiler_params=pltpu.CompilerParams(vmem_limit_bytes=KERNEL_VMEM),
        cost_estimate=pl.CostEstimate(
            flops=4 * rows * full_len * local_width,
            bytes_accessed=2 * rows * 4 * local_width,
            transcendentals=rows * full_len * local_width // HD,
        ),
        name="attention_forward",
    )(place, pictures, triple, triple, triple)


def attention_backward_kernel(
    place, pictures, q_ref, k_ref, v_ref, out_ref, grad_ref, log_ref, triple_ref
):
    rank = place[0]
    ranks = place[1]
    sequence = pl.program_id(0)
    pair = pl.program_id(1)
    local_len = triple_ref.shape[1]
    local_width = triple_ref.shape[2] // 3
    blocks = local_len // PIECE
    own = pl.multiple_of(rank * local_len, local_len)

    def queries_at(start):
        queries = q_ref[0, pl.ds(start, local_len), :] * SCALE
        grads = grad_ref[0, pl.ds(start, local_len), :]
        products = grads.astype(jnp.float32) * out_ref[0, pl.ds(start, local_len), :].astype(
            jnp.float32
        )
        turned = products.T
        logs = log_ref[0, 0, :, pl.ds(start, local_len)]
        sides = []
        for head in range(2):
            delta = jnp.sum(turned[head * HD : (head + 1) * HD], axis=0, keepdims=True)
            sides.append(
                (
                    only_head(queries, head),
                    only_head(grads, head),
                    logs[head : head + 1],
                    delta,
                )
            )
        return sides

    def pieces(keys, values, query, grad, log, delta, mask=None):
        scores = dot_nt(keys, query)
        probs = jnp.exp(scores - log)
        if mask is not None:
            probs = jnp.where(mask(probs), probs, 0.0)
        grad_probs = dot_nt(values, grad)
        return probs, (probs * (grad_probs - delta)).astype(jnp.bfloat16)

    key_own = k_ref[0, pl.ds(own, local_len), :]
    value_own = v_ref[0, pl.ds(own, local_len), :]
    key_turned = key_own.T
    sides = queries_at(own)
    grad_keys = [None] * blocks
    grad_values = [None] * blocks
    grad_queries = []

    def add(total, part):
        return part if total is None else total + part

    for head in range(2):
        queries, grads, logs, deltas = sides[head]
        for block in range(blocks):
            rows = slice(block * PIECE, (block + 1) * PIECE)
            joined = pictures[sequence, rank * blocks + block] > 0
            grad_query = None
            for key_block in range(block + 1):
                key_rows = slice(key_block * PIECE, (key_block + 1) * PIECE)
                mask = (lambda p, j=joined: diagonal_mask(p, j)) if key_block == block else None
                probs, grad_scores = pieces(
                    key_own[key_rows],
                    value_own[key_rows],
                    queries[rows],
                    grads[rows],
                    logs[:, rows],
                    deltas[:, rows],
                    mask,
                )
                grad_values[key_block] = add(
                    grad_values[key_block], dot_nn(probs.astype(jnp.bfloat16), grads[rows])
                )
                grad_keys[key_block] = add(
                    grad_keys[key_block], dot_nn(grad_scores, queries[rows])
                )
                grad_query = add(
                    grad_query,
                    dot_nn(key_turned[head * HD : (head + 1) * HD, key_rows], grad_scores),
                )
            grad_queries.append(grad_query)

    def earlier(step, carried):
        start = pl.multiple_of(step * local_len, local_len)
        keys = k_ref[0, pl.ds(start, local_len), :]
        values = v_ref[0, pl.ds(start, local_len), :]
        turned = keys.T
        after = []
        for index, total in enumerate(carried):
            head, block = index // blocks, index % blocks
            rows = slice(block * PIECE, (block + 1) * PIECE)
            queries, grads, logs, deltas = sides[head]
            _, grad_scores = pieces(
                keys, values, queries[rows], grads[rows], logs[:, rows], deltas[:, rows]
            )
            after.append(total + dot_nn(turned[head * HD : (head + 1) * HD], grad_scores))
        return after

    grad_queries = lax.fori_loop(0, rank, earlier, grad_queries)
    for block in range(blocks):
        rows = slice(block * PIECE, (block + 1) * PIECE)
        both = jnp.concatenate([grad_queries[head * blocks + block] for head in range(2)], axis=0)
        triple_ref[0, rows, pl.ds(pl.multiple_of(pair * PAIR, PAIR), PAIR)] = (
            (both * SCALE).T.astype(triple_ref.dtype)
        )

    def later(step, carried):
        start = pl.multiple_of(step * local_len, local_len)
        sides = queries_at(start)
        keys_after, values_after = list(carried[0]), list(carried[1])
        for head in range(2):
            queries, grads, logs, deltas = sides[head]
            for block in range(blocks):
                rows = slice(block * PIECE, (block + 1) * PIECE)
                probs, grad_scores = pieces(
                    key_own[rows], value_own[rows], queries, grads, logs, deltas
                )
                values_after[block] = values_after[block] + dot_nn(
                    probs.astype(jnp.bfloat16), grads
                )
                keys_after[block] = keys_after[block] + dot_nn(grad_scores, queries)
        return keys_after, values_after

    grad_keys, grad_values = lax.fori_loop(rank + 1, ranks, later, (grad_keys, grad_values))
    for block in range(blocks):
        rows = slice(block * PIECE, (block + 1) * PIECE)
        for part, grads in ((1, grad_keys), (2, grad_values)):
            column = pl.multiple_of(part * local_width + pair * PAIR, PAIR)
            triple_ref[0, rows, pl.ds(column, PAIR)] = grads[block].astype(triple_ref.dtype)


def attention_backward(triple, attended, grad_heads, logs, place, pictures, local_len):
    seq_count, full_len, triple_width = triple.shape
    local_width = triple_width // 3
    pairs = local_width // PAIR
    rows = seq_count * local_len

    def full(offset):
        return pl.BlockSpec(
            (1, full_len, PAIR), lambda s, p, place, pics: (s, 0, offset * pairs + p)
        )

    return pl.pallas_call(
        attention_backward_kernel,
        grid_spec=pltpu.PrefetchScalarGridSpec(
            num_scalar_prefetch=2,
            grid=(seq_count, pairs),
            in_specs=[
                full(0),
                full(1),
                full(2),
                full(0),
                full(0),
                pl.BlockSpec((1, 1, 2, full_len), lambda s, p, place, pics: (s, p, 0, 0)),
            ],
            out_specs=pl.BlockSpec(
                (1, local_len, triple_width), lambda s, p, place, pics: (s, 0, 0)
            ),
        ),
        out_shape=jax.ShapeDtypeStruct((seq_count, local_len, triple_width), jnp.bfloat16),
        compiler_params=pltpu.CompilerParams(vmem_limit_bytes=KERNEL_VMEM),
        cost_estimate=pl.CostEstimate(
            flops=10 * rows * full_len * local_width,
            bytes_accessed=2 * rows * 12 * local_width,
            transcendentals=rows * full_len * local_width // HD,
        ),
        name="attention_backward",
    )(place, pictures, triple, triple, triple, attended, grad_heads, logs)


def gather_ctx(rows, axis):
    if lax.axis_size("ctx") != 2:
        return lax.all_gather(rows, "ctx", axis=axis, tiled=True)
    other = lax.ppermute(rows, "ctx", [(0, 1), (1, 0)])
    leading = lax.axis_index("ctx") == 0
    return jnp.concatenate(
        [jnp.where(leading, rows, other), jnp.where(leading, other, rows)], axis=axis
    )


def sum_tp(part):
    part = part.astype(jnp.bfloat16)
    if lax.axis_size("tp") != 2:
        return lax.psum(part, "tp").astype(jnp.float32)
    other = lax.ppermute(part, "tp", [(0, 1), (1, 0)])
    return part.astype(jnp.float32) + other.astype(jnp.float32)


def gather_fsdp(shard, axis):
    return lax.all_gather(shard, "fsdp", axis=axis, tiled=True)


def reduce_fsdp(gradient, axis):
    return lax.psum_scatter(
        gradient.astype(jnp.bfloat16), "fsdp", scatter_dimension=axis, tiled=True
    )


def body(
    tokens,
    picture_starts,
    ln1_gain,
    ln1_shift,
    w_qkv,
    qv_bias,
    w_proj,
    proj_bias,
    ln2_gain,
    ln2_shift,
    w_fc1,
    fc1_bias,
    w_fc2,
    fc2_bias,
    out_grad,
):
    seq_count, local_len, width = tokens.shape
    ranks = lax.axis_size("ctx")
    rank = lax.axis_index("ctx")
    full_len = ranks * local_len
    local_width = w_qkv.shape[2]
    rows = seq_count * local_len
    place = jnp.stack([rank, jnp.int32(ranks)]).astype(jnp.int32)
    piece_ids = jnp.arange(full_len // PIECE, dtype=jnp.int32)
    pictures = jnp.any(
        piece_ids[None, :, None] == (picture_starts // PIECE)[:, None, :], axis=2
    ).astype(jnp.int32)

    full_qkv = gather_fsdp(w_qkv.reshape(-1, 3 * local_width), 0)
    full_proj = gather_fsdp(w_proj, 1)
    full_fc1 = gather_fsdp(w_fc1, 0)
    full_fc2 = gather_fsdp(w_fc2, 1)
    vectors = lax.all_gather(
        jnp.stack([ln1_gain, ln1_shift, proj_bias, ln2_gain, ln2_shift, fc2_bias]),
        "fsdp",
        axis=1,
        tiled=True,
    ).astype(jnp.float32)
    gain_one, shift_one, bias_proj, gain_two, shift_two, bias_fc2 = vectors
    qv_rows = lax.all_gather(qv_bias, "fsdp", axis=2, tiled=True).reshape(2, -1)
    bias_fc1 = lax.all_gather(fc1_bias, "fsdp", axis=1, tiled=True).reshape(-1)
    qv_rows = qv_rows.astype(jnp.float32)
    bias_fc1 = bias_fc1.astype(jnp.float32)
    bias_qkv = jnp.concatenate([qv_rows[0], jnp.zeros_like(qv_rows[0]), qv_rows[1]])

    tokens_all = gather_ctx(tokens, 1)
    normed_all = layer_norm(tokens_all.astype(jnp.float32), gain_one, shift_one).astype(
        jnp.bfloat16
    )
    triple = jnp.einsum(
        "sld,de->sle", normed_all, full_qkv, preferred_element_type=jnp.float32
    )
    triple = (triple + bias_qkv).astype(jnp.bfloat16)
    attended, logs = attention_forward(triple, place, pictures, local_len)
    attended_all = gather_ctx(attended, 1)
    logs_all = gather_ctx(logs, 3)
    attended = attended.reshape(rows, local_width)
    flat_tokens = tokens.reshape(rows, width).astype(jnp.float32)
    part = jnp.dot(attended, full_proj, preferred_element_type=jnp.float32)
    residual = flat_tokens + (sum_tp(part) + bias_proj)
    normed_two = layer_norm(residual, gain_two, shift_two).astype(jnp.bfloat16)
    hidden_pre = jnp.dot(normed_two, full_fc1, preferred_element_type=jnp.float32) + bias_fc1
    active, gelu_pull = jax.vjp(gelu_tanh, hidden_pre)
    active = active.astype(jnp.bfloat16)
    feed_part = jnp.dot(active, full_fc2, preferred_element_type=jnp.float32)
    output = residual + sum_tp(feed_part) + bias_fc2

    grad_rows = out_grad.reshape(rows, width)
    grad_float = grad_rows.astype(jnp.float32)
    grad_active = jnp.einsum("td,fd->tf", grad_rows, full_fc2, preferred_element_type=jnp.float32)
    grad_hidden = gelu_pull(grad_active)[0].astype(jnp.bfloat16)
    back_two = jnp.einsum("tf,df->td", grad_hidden, full_fc1, preferred_element_type=jnp.float32)
    grad_normed_two = sum_tp(back_two)
    grad_fc2 = jnp.einsum("tf,td->fd", active, grad_rows, preferred_element_type=jnp.float32)
    grad_fc1 = jnp.einsum("td,tf->df", normed_two, grad_hidden, preferred_element_type=jnp.float32)
    shard_fc2 = reduce_fsdp(grad_fc2, 1)
    shard_fc1 = reduce_fsdp(grad_fc1, 0)
    norm_two_pull = jax.vjp(layer_norm, residual, gain_two, shift_two)[1]
    resid_part, grad_gain_two, grad_shift_two = norm_two_pull(grad_normed_two)
    grad_residual = grad_float + resid_part
    grad_branch = grad_residual.astype(jnp.bfloat16)
    grad_heads = jnp.einsum(
        "td,cd->tc", grad_branch, full_proj, preferred_element_type=jnp.float32
    ).astype(jnp.bfloat16)
    grad_heads_all = gather_ctx(grad_heads.reshape(seq_count, local_len, local_width), 1)
    grad_proj = jnp.einsum("tc,td->cd", attended, grad_branch, preferred_element_type=jnp.float32)
    shard_proj = reduce_fsdp(grad_proj, 1)
    grad_triple = attention_backward(
        triple, attended_all, grad_heads_all, logs_all, place, pictures, local_len
    ).reshape(rows, 3 * local_width)
    back_one = jnp.einsum("te,de->td", grad_triple, full_qkv, preferred_element_type=jnp.float32)
    grad_normed_one = sum_tp(back_one)
    normed_one = lax.dynamic_slice_in_dim(normed_all, rank * local_len, local_len, 1)
    grad_qkv = jnp.einsum(
        "td,te->de",
        normed_one.reshape(rows, width),
        grad_triple,
        preferred_element_type=jnp.float32,
    )
    shard_qkv = reduce_fsdp(grad_qkv, 0)
    norm_one_pull = jax.vjp(layer_norm, flat_tokens, gain_one, shift_one)[1]
    flat_part, grad_gain_one, grad_shift_one = norm_one_pull(grad_normed_one)
    grad_tokens = (grad_residual + flat_part).astype(jnp.bfloat16)

    triple_sums = jnp.sum(grad_triple.astype(jnp.float32), axis=0)
    grad_qv_bias = jnp.stack([triple_sums[:local_width], triple_sums[2 * local_width :]])
    small = [
        grad_gain_one,
        grad_shift_one,
        jnp.sum(grad_branch.astype(jnp.float32), axis=0),
        grad_gain_two,
        grad_shift_two,
        jnp.sum(grad_float, axis=0),
    ]
    small = reduce_fsdp(jnp.stack(small), 1)
    shard_qv = reduce_fsdp(grad_qv_bias.reshape(2, -1, HD), 2)
    grad_fc1_bias = jnp.sum(grad_hidden.astype(jnp.float32), axis=0).reshape(-1, HD)
    shard_fc1_bias = reduce_fsdp(grad_fc1_bias, 1)

    def finish(share):
        return lax.psum(share, "ctx").astype(jnp.float32)

    small = finish(small)
    return (
        output.astype(jnp.bfloat16).reshape(tokens.shape),
        grad_tokens.reshape(tokens.shape),
        small[0],
        small[1],
        finish(shard_qkv).reshape(-1, 3, local_width),
        finish(shard_qv),
        finish(shard_proj),
        small[2],
        small[3],
        small[4],
        finish(shard_fc1),
        finish(shard_fc1_bias),
        finish(shard_fc2),
        small[5],
    )


def solution(mesh):
    return jax.shard_map(
        body,
        mesh=mesh,
        in_specs=(
            P("fsdp", "ctx", None),
            P("fsdp", None),
            P("fsdp"),
            P("fsdp"),
            P("fsdp", None, "tp"),
            P(None, "tp", "fsdp"),
            P("tp", "fsdp"),
            P("fsdp"),
            P("fsdp"),
            P("fsdp"),
            P("fsdp", "tp"),
            P("tp", "fsdp"),
            P("tp", "fsdp"),
            P("fsdp"),
            P("fsdp", "ctx", None),
        ),
        out_specs=(
            P("fsdp", "ctx", None),
            P("fsdp", "ctx", None),
            P("fsdp"),
            P("fsdp"),
            P("fsdp", None, "tp"),
            P(None, "tp", "fsdp"),
            P("tp", "fsdp"),
            P("fsdp"),
            P("fsdp"),
            P("fsdp"),
            P("fsdp", "tp"),
            P("tp", "fsdp"),
            P("tp", "fsdp"),
            P("fsdp"),
        ),
        check_vma=False,
    )
```

```python
import jax
import jax.numpy as jnp
from jax import lax
from jax.experimental import pallas as pl
from jax.experimental.pallas import tpu as pltpu
from jax.sharding import PartitionSpec as P

HD = 64
PAIR = 2 * HD
PIECE = 256
SCALE = HD ** (-0.5)
KERNEL_VMEM = 56 * 1024 * 1024

epsilon = 1e-05
masked_value = -1e30


def layer_norm(values, gain_vec, shift_vec):
    average = jnp.mean(values, axis=-1, keepdims=True)
    centred = values - average
    variance = jnp.mean(centred * centred, axis=-1, keepdims=True)
    return centred * lax.rsqrt(variance + epsilon) * gain_vec + shift_vec


def gelu_tanh(values):
    return jax.nn.gelu(values, approximate=True)


NT = (((1,), (1,)), ((), ()))


def dot_nt(left, right):
    return lax.dot_general(left, right, NT, preferred_element_type=jnp.float32)


def dot_nn(left, right):
    return jnp.dot(left, right, preferred_element_type=jnp.float32)


def head_lanes(head):
    lanes = lax.broadcasted_iota(jnp.int32, (1, PAIR), 1)
    return (lanes >= head * HD) & (lanes < (head + 1) * HD)


def only_head(rows, head):
    return jnp.where(head_lanes(head), rows, jnp.zeros_like(rows))


def diagonal_mask(scores, joined):
    key_row = lax.broadcasted_iota(jnp.int32, scores.shape, 0)
    query_lane = lax.broadcasted_iota(jnp.int32, scores.shape, 1)
    return (key_row <= query_lane) | joined


def chunk_start(step, place, local_len, chunks):
    return 0 if chunks == 1 else pl.multiple_of(step * local_len, local_len)


def attention_forward_kernel(
    place, pictures, q_ref, k_ref, v_ref, k_far, v_far, out_ref, log_ref
):
    rank = place[0]
    sequence = place[2]
    local_len = q_ref.shape[1]
    blocks = local_len // PIECE
    chunks = k_far.shape[1] // local_len
    key_own = k_ref[0]
    value_own = v_ref[0].T
    states = []
    scaled = []
    for head in range(2):
        for block in range(blocks):
            rows = slice(block * PIECE, (block + 1) * PIECE)
            query = only_head(q_ref[0, rows, :] * SCALE, head)
            scaled.append(query)
            joined = pictures[sequence, rank * blocks + block] > 0
            diagonal = dot_nt(key_own[rows], query)
            diagonal = jnp.where(diagonal_mask(diagonal, joined), diagonal, masked_value)
            peak = jnp.max(diagonal, axis=0, keepdims=True)
            value_head = value_own[head * HD : (head + 1) * HD]
            if block:
                before = dot_nt(key_own[: block * PIECE], query)
                peak = jnp.maximum(peak, jnp.max(before, axis=0, keepdims=True))
            weight = jnp.exp(diagonal - peak)
            total = jnp.sum(weight, axis=0, keepdims=True)
            gathered = dot_nn(value_head[:, rows], weight.astype(jnp.bfloat16))
            if block:
                weight = jnp.exp(before - peak)
                total = total + jnp.sum(weight, axis=0, keepdims=True)
                gathered = gathered + dot_nn(
                    value_head[:, : block * PIECE], weight.astype(jnp.bfloat16)
                )
            states.append((peak, total, gathered))

    def earlier(step, carried):
        start = chunk_start(step, place, local_len, chunks)
        keys = k_far[0, pl.ds(start, local_len), :]
        values = v_far[0, pl.ds(start, local_len), :].T
        after = []
        for index, (peak, total, gathered) in enumerate(carried):
            head = index // blocks
            scores = dot_nt(keys, scaled[index])
            new_peak = jnp.maximum(peak, jnp.max(scores, axis=0, keepdims=True))
            shrink = jnp.exp(peak - new_peak)
            weight = jnp.exp(scores - new_peak)
            after.append(
                (
                    new_peak,
                    shrink * total + jnp.sum(weight, axis=0, keepdims=True),
                    shrink * gathered
                    + dot_nn(values[head * HD : (head + 1) * HD], weight.astype(jnp.bfloat16)),
                )
            )
        return after

    states = lax.fori_loop(0, rank, earlier, states)
    for block in range(blocks):
        rows = slice(block * PIECE, (block + 1) * PIECE)
        halves = []
        for head in range(2):
            peak, total, gathered = states[head * blocks + block]
            halves.append(gathered / total)
            log_ref[0, head : head + 1, rows] = peak + jnp.log(total)
        out_ref[rows, :] = jnp.concatenate(halves, axis=0).T.astype(out_ref.dtype)


def attention_forward(triple, far, place, pictures, index):
    place = jnp.concatenate([place, jnp.full((1,), index, jnp.int32)])
    _, local_len, triple_width = triple.shape
    far_len = far.shape[1]
    local_width = triple_width // 3
    pairs = local_width // PAIR

    def part(length, offset):
        return pl.BlockSpec(
            (1, length, PAIR), lambda p, place, pics: (index, 0, offset * pairs + p)
        )

    return pl.pallas_call(
        attention_forward_kernel,
        grid_spec=pltpu.PrefetchScalarGridSpec(
            num_scalar_prefetch=2,
            grid=(pairs,),
            in_specs=[
                part(local_len, 0),
                part(local_len, 1),
                part(local_len, 2),
                part(far_len, 1),
                part(far_len, 2),
            ],
            out_specs=[
                pl.BlockSpec((local_len, PAIR), lambda p, place, pics: (0, p)),
                pl.BlockSpec((1, 2, local_len), lambda p, place, pics: (p, 0, 0)),
            ],
        ),
        out_shape=[
            jax.ShapeDtypeStruct((local_len, local_width), jnp.bfloat16),
            jax.ShapeDtypeStruct((pairs, 2, local_len), jnp.float32),
        ],
        compiler_params=pltpu.CompilerParams(vmem_limit_bytes=KERNEL_VMEM),
        cost_estimate=pl.CostEstimate(flops=50000000000, bytes_accessed=0, transcendentals=0),
        name="attention_forward",
    )(place, pictures, triple, triple, triple, far, far)


def attention_backward_kernel(
    place,
    pictures,
    q_ref,
    k_ref,
    v_ref,
    out_ref,
    grad_ref,
    log_ref,
    q_far,
    k_far,
    v_far,
    out_far,
    grad_far,
    log_far,
    triple_ref,
):
    rank = place[0]
    ranks = place[1]
    sequence = place[2]
    pair = pl.program_id(0)
    local_len = triple_ref.shape[0]
    local_width = triple_ref.shape[1] // 3
    blocks = local_len // PIECE
    chunks = k_far.shape[1] // local_len

    def sides_of(queries, grads, outs, logs):
        turned = (grads.astype(jnp.float32) * outs.astype(jnp.float32)).T
        queries = queries * SCALE
        sides = []
        for head in range(2):
            delta = jnp.sum(turned[head * HD : (head + 1) * HD], axis=0, keepdims=True)
            sides.append(
                (
                    only_head(queries, head),
                    only_head(grads, head),
                    logs[head : head + 1],
                    delta,
                )
            )
        return sides

    def pieces(keys, values, query, grad, log, delta, mask=None):
        scores = dot_nt(keys, query)
        probs = jnp.exp(scores - log)
        if mask is not None:
            probs = jnp.where(mask(probs), probs, 0.0)
        grad_probs = dot_nt(values, grad)
        return probs, (probs * (grad_probs - delta)).astype(jnp.bfloat16)

    key_own = k_ref[0]
    value_own = v_ref[0]
    key_turned = key_own.T
    sides = sides_of(q_ref[0], grad_ref[...], out_ref[...], log_ref[0])
    grad_keys = [None] * blocks
    grad_values = [None] * blocks
    grad_queries = []

    def add(total, part):
        return part if total is None else total + part

    for head in range(2):
        queries, grads, logs, deltas = sides[head]
        for block in range(blocks):
            rows = slice(block * PIECE, (block + 1) * PIECE)
            joined = pictures[sequence, rank * blocks + block] > 0
            grad_query = None
            for key_block in range(block + 1):
                key_rows = slice(key_block * PIECE, (key_block + 1) * PIECE)
                mask = (lambda p, j=joined: diagonal_mask(p, j)) if key_block == block else None
                probs, grad_scores = pieces(
                    key_own[key_rows],
                    value_own[key_rows],
                    queries[rows],
                    grads[rows],
                    logs[:, rows],
                    deltas[:, rows],
                    mask,
                )
                grad_values[key_block] = add(
                    grad_values[key_block], dot_nn(probs.astype(jnp.bfloat16), grads[rows])
                )
                grad_keys[key_block] = add(
                    grad_keys[key_block], dot_nn(grad_scores, queries[rows])
                )
                grad_query = add(
                    grad_query,
                    dot_nn(key_turned[head * HD : (head + 1) * HD, key_rows], grad_scores),
                )
            grad_queries.append(grad_query)

    def earlier(step, carried):
        start = chunk_start(step, place, local_len, chunks)
        keys = k_far[0, pl.ds(start, local_len), :]
        values = v_far[0, pl.ds(start, local_len), :]
        turned = keys.T
        after = []
        for index, total in enumerate(carried):
            head, block = index // blocks, index % blocks
            rows = slice(block * PIECE, (block + 1) * PIECE)
            queries, grads, logs, deltas = sides[head]
            _, grad_scores = pieces(
                keys, values, queries[rows], grads[rows], logs[:, rows], deltas[:, rows]
            )
            after.append(total + dot_nn(turned[head * HD : (head + 1) * HD], grad_scores))
        return after

    grad_queries = lax.fori_loop(0, rank, earlier, grad_queries)
    for block in range(blocks):
        rows = slice(block * PIECE, (block + 1) * PIECE)
        both = jnp.concatenate([grad_queries[head * blocks + block] for head in range(2)], axis=0)
        triple_ref[rows, pl.ds(pl.multiple_of(pair * PAIR, PAIR), PAIR)] = (
            (both * SCALE).T.astype(triple_ref.dtype)
        )

    def later(step, carried):
        start = chunk_start(step, place, local_len, chunks)
        window = pl.ds(start, local_len)
        sides = sides_of(
            q_far[0, window, :], grad_far[window, :], out_far[window, :], log_far[0, :, window]
        )
        keys_after, values_after = list(carried[0]), list(carried[1])
        for head in range(2):
            queries, grads, logs, deltas = sides[head]
            for block in range(blocks):
                rows = slice(block * PIECE, (block + 1) * PIECE)
                probs, grad_scores = pieces(
                    key_own[rows], value_own[rows], queries, grads, logs, deltas
                )
                values_after[block] = values_after[block] + dot_nn(
                    probs.astype(jnp.bfloat16), grads
                )
                keys_after[block] = keys_after[block] + dot_nn(grad_scores, queries)
        return keys_after, values_after

    grad_keys, grad_values = lax.fori_loop(rank + 1, ranks, later, (grad_keys, grad_values))
    for block in range(blocks):
        rows = slice(block * PIECE, (block + 1) * PIECE)
        for part, grads in ((1, grad_keys), (2, grad_values)):
            column = pl.multiple_of(part * local_width + pair * PAIR, PAIR)
            triple_ref[rows, pl.ds(column, PAIR)] = grads[block].astype(triple_ref.dtype)


def attention_backward(own, other, place, pictures, index):
    place = jnp.concatenate([place, jnp.full((1,), index, jnp.int32)])
    _, local_len, triple_width = own[0].shape
    pairs = triple_width // (3 * PAIR)
    specs = []
    for length in (local_len, other[0].shape[1]):
        for offset in range(3):
            specs.append(
                pl.BlockSpec(
                    (1, length, PAIR),
                    lambda p, place, pics, offset=offset: (index, 0, offset * pairs + p),
                )
            )
        specs += [pl.BlockSpec((length, PAIR), lambda p, place, pics: (0, p))] * 2
        specs.append(pl.BlockSpec((1, 2, length), lambda p, place, pics: (p, 0, 0)))
    return pl.pallas_call(
        attention_backward_kernel,
        grid_spec=pltpu.PrefetchScalarGridSpec(
            num_scalar_prefetch=2,
            grid=(pairs,),
            in_specs=specs,
            out_specs=pl.BlockSpec((local_len, triple_width), lambda p, place, pics: (0, 0)),
        ),
        out_shape=jax.ShapeDtypeStruct((local_len, triple_width), jnp.bfloat16),
        compiler_params=pltpu.CompilerParams(vmem_limit_bytes=KERNEL_VMEM),
        cost_estimate=pl.CostEstimate(flops=50000000000, bytes_accessed=0, transcendentals=0),
        name="attention_backward",
    )(place, pictures, *([own[0]] * 3), *own[1:], *([other[0]] * 3), *other[1:])


def core_swap():
    return [(place, place ^ 1) for place in range(lax.axis_size("fsdp"))]


PAIR_SWAP = [(0, 1), (1, 0)]


def swap_core(rows):
    return lax.ppermute(rows, "fsdp", core_swap())


def swap_ctx(rows):
    return lax.ppermute(rows, "ctx", PAIR_SWAP)


def swap_tp(rows):
    return lax.ppermute(rows, "tp", PAIR_SWAP)


def exchange_chips(rows):
    fsdp = lax.axis_size("fsdp")
    groups = [list(range(core, fsdp, 2)) for core in range(2)]
    return lax.all_to_all(
        rows, "fsdp", split_axis=0, concat_axis=0, tiled=True, axis_index_groups=groups
    )


def pick(array, index, axis):
    return lax.dynamic_index_in_dim(array, index, axis, keepdims=False)


def after(value, *others):
    return lax.optimization_barrier((value, *others))[0]


def halves_of(shard):
    halves = 2 if lax.axis_size("ctx") == 2 else 1
    return shard.reshape(halves, -1, shard.shape[1])


def gather_chips(halves):
    chips = lax.axis_size("fsdp") // 2
    part = pick(halves, lax.axis_index("ctx"), 0) if halves.shape[0] == 2 else halves[0]
    return exchange_chips(jnp.broadcast_to(part, (chips, *part.shape)))


def gather_rest(bundle, bundles=None, *gate):
    bundles = bundles or [bundle, swap_core(bundle)]
    if lax.axis_size("ctx") == 2:
        across = after(swap_ctx(bundle), *gate)
        bundles = bundles + [across, swap_core(across)]
    return bundles


def kernel_call(kernel, scalars, arrays, in_specs, outs, out_specs, grid, name, scratch=(), flops=0):
    size = sum(array.size for array in arrays)
    return pl.pallas_call(
        kernel,
        grid_spec=pltpu.PrefetchScalarGridSpec(
            num_scalar_prefetch=len(scalars),
            grid=(grid,),
            in_specs=in_specs,
            out_specs=out_specs,
            scratch_shapes=list(scratch),
        ),
        out_shape=[jax.ShapeDtypeStruct(shape, dtype) for shape, dtype in outs],
        compiler_params=pltpu.CompilerParams(vmem_limit_bytes=KERNEL_VMEM),
        cost_estimate=pl.CostEstimate(flops=50000000000, bytes_accessed=0, transcendentals=0),
        name=name,
    )(*scalars, *arrays)


def owners(here, sides):
    for index in range(2 * sides):
        core = here[1] if index % 2 == 0 else 1 - here[1]
        yield core, ((here[2] if index < 2 else 1 - here[2]) if sides == 2 else 0)


def placed_rows(bundles, here, name):
    fsdp = lax.axis_size("fsdp")
    sides = len(bundles) // 2
    chips, height, width = bundles[0].shape
    chunk = 512

    def kernel(here, *refs):
        for index, (core, side) in enumerate(owners(here, sides)):
            for chip in range(chips):
                refs[-1][(2 * chip + core) * sides + side] = refs[index][chip]

    (result,) = kernel_call(
        kernel,
        [here],
        bundles,
        [pl.BlockSpec((chips, height, chunk), lambda i, here: (0, 0, i))] * (2 * sides),
        [((fsdp * sides, height, width), jnp.bfloat16)],
        [pl.BlockSpec((fsdp * sides, height, chunk), lambda i, here: (0, 0, i))],
        width // chunk,
        name,
    )
    return result.reshape(-1, width)


def placed_columns_plain(bundles, here):
    sides = []
    for mine, other in zip(bundles[::2], bundles[1::2]):
        first = jnp.where(here[1] == 0, mine, other)
        second = jnp.where(here[1] == 0, other, mine)
        both = jnp.stack([first, second], axis=1)
        sides.append(both.reshape(-1, *both.shape[2:]))
    if len(sides) == 2:
        sides = [
            jnp.where(here[2] == 0, sides[0], sides[1]),
            jnp.where(here[2] == 0, sides[1], sides[0]),
        ]
    fsdp, _, width = sides[0].shape
    return jnp.concatenate(sides, axis=1).transpose(1, 0, 2).reshape(-1, fsdp * width)


def weight_copies(bundles, target, here, columns):
    if len(bundles) == 1:
        yield bundles[0], target
        return
    sides = len(bundles) // 2
    for index, (core, side) in enumerate(owners(here, sides)):
        chips, _, width = bundles[index].shape
        height = target.shape[0] // (sides if columns else 2 * chips * sides)
        for chip in range(chips):
            block = 2 * chip + core
            source = bundles[index].at[chip, pl.ds(0, height)]
            if columns:
                across = pl.ds(pl.multiple_of(block * width, width), width)
                yield source, target.at[pl.ds(pl.multiple_of(side * height, height), height), across]
            else:
                row = pl.multiple_of((block * sides + side) * height, height)
                yield source, target.at[pl.ds(row, height)]


UNITS = 1024
TILE = 16
ROOT = 0.7978845608028654
CUBIC = 0.044715


def feed_kernel(counts, columns, here, *refs):
    own_ref, tp_ref, tokens_ref, grad_ref, vector_ref, bias_ref = refs[:6]
    at = 6
    bundles = []
    for count in counts:
        bundles.append(refs[at : at + count])
        at += count
    residual_ref, normed_ref, active_ref, hidden_ref, feed_ref, back_ref, sum_ref, proj_ref = refs[
        at : at + 8
    ]
    proj, first, second, feed, back, hidden_pre, grad_active, semaphores = refs[at + 8 :]
    step = pl.program_id(0)
    copies = []
    for group, target, across in zip(bundles, (proj, first, second), columns):
        copies.append(
            [
                (source, place, across)
                for source, place in weight_copies(group, target, here, across)
            ]
        )
    made, number = [], 0
    for group in copies:
        made.append([])
        for source, place, _ in group:
            made[-1].append(pltpu.make_async_copy(source, place, semaphores.at[number]))
            number += 1
    rows = proj.shape[0] // 2
    kept = pltpu.make_async_copy(
        proj.at[pl.ds(pl.multiple_of(here[3] * rows, rows), rows)],
        proj_ref,
        semaphores.at[number],
    )

    @pl.when(step == 0)
    def _():
        for group in made:
            for copy in group:
                copy.start()
        for copy in made[0]:
            copy.wait()
        kept.start()
        leading = here[3] == 0
        low = jnp.where(leading, own_ref[...], tp_ref[...])
        high = jnp.where(leading, tp_ref[...], own_ref[...])
        feed[...] = dot_nn(low, proj[:rows]) + dot_nn(high, proj[rows:])
        for start in range(0, feed.shape[0], TILE):
            lines = slice(start, start + TILE)
            residual = tokens_ref[0, lines].astype(jnp.float32) + feed[lines] + vector_ref[0:1]
            residual_ref[lines] = residual
            unit, _ = centred_rows(residual)
            normed_ref[lines] = (unit * vector_ref[1:2] + vector_ref[2:3]).astype(
                normed_ref.dtype
            )
        for copy in made[1]:
            copy.wait()

    units = pl.ds(pl.multiple_of(step * UNITS, UNITS), UNITS)
    hidden_pre[...] = dot_nn(normed_ref[...], first[:, units])

    @pl.when(step == 0)
    def _():
        for copy in made[2]:
            copy.wait()
        kept.wait()

    grad_active[...] = dot_nt(grad_ref[0], second[units])
    totals = jnp.zeros((TILE, UNITS), jnp.float32)
    for start in range(0, feed.shape[0], TILE):
        lines = slice(start, start + TILE)
        hidden = hidden_pre[lines] + bias_ref[...]
        square = hidden * hidden
        bent = jnp.tanh(hidden * (ROOT + ROOT * CUBIC * square))
        share = 0.5 + 0.5 * bent
        active_ref[lines] = (hidden * share).astype(jnp.bfloat16)
        slope = share + hidden * (1.0 - bent * bent) * (
            0.5 * ROOT + 1.5 * ROOT * CUBIC * square
        )
        grad_hidden = (grad_active[lines] * slope).astype(jnp.bfloat16)
        hidden_ref[lines] = grad_hidden
        totals = totals + grad_hidden.astype(jnp.float32)
    sum_ref[...] = jnp.sum(totals, axis=0, keepdims=True)
    active = active_ref[...]
    feed_part = dot_nn(active, second[units])
    back_part = dot_nt(hidden_ref[...], first[:, units])

    @pl.when(step == 0)
    def _():
        feed[...] = feed_part
        back[...] = back_part

    @pl.when(step > 0)
    def _():
        feed[...] += feed_part
        back[...] += back_part

    @pl.when(step == pl.num_programs(0) - 1)
    def _():
        feed_ref[...] = feed[...].astype(feed_ref.dtype)
        back_ref[...] = back[...].astype(back_ref.dtype)


def feed_forward(own, tp, tokens, out_grad, vectors, bias, weights, here, index):
    local_len, local_width = own.shape
    width = tokens.shape[2]
    units = bias.shape[1]
    columns = (True, False, True)
    counts = tuple(len(group) for group in weights)
    copies = sum(1 if count == 1 else count * group[0].shape[0] for count, group in zip(counts, weights))
    whole = lambda shape: pl.BlockSpec(shape, lambda j, here: (0,) * len(shape))
    row = pl.BlockSpec((1, local_len, width), lambda j, here: (index, 0, 0))
    block = pl.BlockSpec((local_len, UNITS), lambda j, here: (0, j))
    line = pl.BlockSpec((1, UNITS), lambda j, here: (0, j))
    flat = [array for group in weights for array in group]
    half, full = jnp.bfloat16, jnp.float32
    return kernel_call(
        lambda *refs: feed_kernel(counts, columns, *refs),
        [here],
        [own, tp, tokens, out_grad, vectors, bias] + flat,
        [whole(own.shape), whole(own.shape), row, row, whole(vectors.shape), line]
        + [pl.BlockSpec(memory_space=pl.ANY)] * len(flat),
        [
            ((local_len, width), full),
            ((local_len, width), half),
            ((local_len, units), half),
            ((local_len, units), half),
            ((local_len, width), half),
            ((local_len, width), half),
            ((1, units), full),
            ((local_width, width), half),
        ],
        [whole((local_len, width)), whole((local_len, width)), block, block]
        + [whole((local_len, width)), whole((local_len, width)), line]
        + [pl.BlockSpec(memory_space=pl.ANY)],
        units // UNITS,
        "feed_forward",
        [
            pltpu.VMEM((2 * local_width, width), half),
            pltpu.VMEM((width, units), half),
            pltpu.VMEM((units, width), half),
            pltpu.VMEM((local_len, width), full),
            pltpu.VMEM((local_len, width), full),
            pltpu.VMEM((local_len, UNITS), full),
            pltpu.VMEM((local_len, UNITS), full),
            pltpu.SemaphoreType.DMA((copies + 1,)),
        ],
        flops=8 * local_len * width * units,
    )


ROWS = 256


def centred_rows(rows):
    average = jnp.mean(rows, axis=-1, keepdims=True)
    centred = rows - average
    spread = lax.rsqrt(jnp.mean(centred * centred, axis=-1, keepdims=True) + epsilon)
    return centred * spread, spread


def through_norm(grads, unit, spread, gain):
    scaled = grads * gain
    return spread * (
        scaled
        - jnp.mean(scaled, axis=-1, keepdims=True)
        - unit * jnp.mean(scaled * unit, axis=-1, keepdims=True)
    )


def accumulate(ref, totals):
    total = jnp.concatenate([jnp.sum(lines, axis=0, keepdims=True) for lines in totals])

    @pl.when(pl.program_id(0) == 0)
    def _():
        ref[...] = total

    @pl.when(pl.program_id(0) > 0)
    def _():
        ref[...] += total


def tiles_of(count):
    return [slice(start, start + TILE) for start in range(0, count, TILE)]


def norm_two_kernel(
    here, own_ref, tp_ref, residual_ref, grad_ref, vector_ref, proj_ref, branch_ref, heads_ref, sum_ref
):
    totals = [jnp.zeros((TILE, own_ref.shape[1]), jnp.float32)] * 3
    for lines in tiles_of(own_ref.shape[0]):
        grads = own_ref[lines].astype(jnp.float32) + tp_ref[lines].astype(jnp.float32)
        unit, spread = centred_rows(residual_ref[lines])
        total = grad_ref[0, lines].astype(jnp.float32) + through_norm(
            grads, unit, spread, vector_ref[1:2]
        )
        branch = total.astype(jnp.bfloat16)
        branch_ref[lines] = branch
        totals = [
            totals[0] + grads * unit,
            totals[1] + grads,
            totals[2] + branch.astype(jnp.float32),
        ]
    heads_ref[...] = dot_nt(branch_ref[...], proj_ref[...]).astype(heads_ref.dtype)
    accumulate(sum_ref, totals)


def norm_two_backward(own, tp, residual, out_grad, vectors, proj, here, index):
    local_len, width = own.shape
    local_width = proj.shape[0]
    whole = lambda shape: pl.BlockSpec(shape, lambda i, here: (0,) * len(shape))
    row = pl.BlockSpec((ROWS, width), lambda i, here: (i, 0))
    return kernel_call(
        norm_two_kernel,
        [here],
        [own, tp, residual, out_grad, vectors, proj],
        [row, row, row, pl.BlockSpec((1, ROWS, width), lambda i, here: (index, i, 0))]
        + [whole(vectors.shape), whole(proj.shape)],
        [
            ((local_len, width), jnp.bfloat16),
            ((local_len, local_width), jnp.bfloat16),
            ((3, width), jnp.float32),
        ],
        [row, pl.BlockSpec((ROWS, local_width), lambda i, here: (i, 0)), whole((3, width))],
        local_len // ROWS,
        "norm_two_backward",
        flops=2 * local_len * width * local_width,
    )


def qkv_back_kernel(here, grad_ref, tokens_ref, weight_ref, back_ref, sum_ref, triple_ref, back):
    back[...] = dot_nt(grad_ref[...], weight_ref[...])
    totals = [jnp.zeros((TILE, back.shape[1]), jnp.float32)] * 2
    triple = jnp.zeros((TILE, grad_ref.shape[1]), jnp.float32)
    for lines in tiles_of(back.shape[0]):
        part = back[lines]
        back_ref[lines] = part.astype(back_ref.dtype)
        unit, _ = centred_rows(tokens_ref[0, lines].astype(jnp.float32))
        totals = [totals[0] + part * unit, totals[1] + part]
        triple = triple + grad_ref[lines].astype(jnp.float32)
    accumulate(sum_ref, totals)
    accumulate(triple_ref, [triple])


def qkv_backward(grad_triple, tokens, weight, here, index):
    local_len, triple_width = grad_triple.shape
    width = tokens.shape[2]
    whole = lambda shape: pl.BlockSpec(shape, lambda i, here: (0,) * len(shape))
    return kernel_call(
        qkv_back_kernel,
        [here],
        [grad_triple, tokens, weight],
        [
            pl.BlockSpec((ROWS, triple_width), lambda i, here: (i, 0)),
            pl.BlockSpec((1, ROWS, width), lambda i, here: (index, i, 0)),
            whole(weight.shape),
        ],
        [
            ((local_len, width), jnp.bfloat16),
            ((2, width), jnp.float32),
            ((1, triple_width), jnp.float32),
        ],
        [
            pl.BlockSpec((ROWS, width), lambda i, here: (i, 0)),
            whole((2, width)),
            whole((1, triple_width)),
        ],
        local_len // ROWS,
        "qkv_backward",
        [pltpu.VMEM((ROWS, width), jnp.float32)],
        flops=2 * local_len * width * triple_width,
    )


def norm_one_kernel(here, own_ref, tp_ref, tokens_ref, residual_ref, vector_ref, out_ref):
    for lines in tiles_of(own_ref.shape[0]):
        grads = own_ref[lines].astype(jnp.float32) + tp_ref[lines].astype(jnp.float32)
        unit, spread = centred_rows(tokens_ref[0, lines].astype(jnp.float32))
        out_ref[lines] = (
            residual_ref[lines].astype(jnp.float32)
            + through_norm(grads, unit, spread, vector_ref[3:4])
        ).astype(out_ref.dtype)


def norm_one_backward(own, tp, tokens, residual, vectors, here, index):
    local_len, width = own.shape
    row = pl.BlockSpec((ROWS, width), lambda i, here: (i, 0))
    return kernel_call(
        norm_one_kernel,
        [here],
        [own, tp, tokens, residual, vectors],
        [row, row, pl.BlockSpec((1, ROWS, width), lambda i, here: (index, i, 0)), row]
        + [pl.BlockSpec(vectors.shape, lambda i, here: (0, 0))],
        [((local_len, width), jnp.bfloat16)],
        [row],
        local_len // ROWS,
        "norm_one_backward",
    )[0]


CHUNK = 512


def gradient_kernel(plan, here, *refs):
    chips, groups, extra = plan
    step = pl.program_id(0)
    refs = list(refs)
    turned = refs.pop()
    mark = refs.pop()
    outs = [refs.pop(-2), refs.pop()]
    mark[...] = jnp.zeros_like(mark)
    rows = outs[0].shape[2] - extra
    at = 0
    for first, last, sequences in groups:
        lefts = refs[at : at + 2 * sequences * chips]
        rights = refs[at + 2 * sequences * chips : at + sequences * (2 * chips + 1)]
        at += sequences * (2 * chips + 1)

        @pl.when(step == first)
        def _():
            for index, left in enumerate(lefts):
                which, rest = divmod(index, sequences * chips)
                sequence, chip = divmod(rest, chips)
                block = left.shape[2]
                turned[which, sequence, chip * block : (chip + 1) * block] = left[0].T

        @pl.when((step >= first) & (step < last))
        def _():
            for which in range(2):
                total = dot_nn(turned[which, 0], rights[0][...])
                for sequence in range(1, sequences):
                    total += dot_nn(turned[which, sequence], rights[sequence][...])
                total = total.reshape(chips, 2, rows, -1)
                outs[which][:, :, :rows] = total.astype(jnp.bfloat16)

    if extra:
        for which in range(2):
            small = refs[at + which][...].astype(jnp.bfloat16)
            outs[which][:, 0, rows:] = small
            outs[which][:, 1, rows:] = jnp.zeros_like(small)


def gradient_plain(groups, here, small):
    chips = lax.axis_size("fsdp") // 2
    columns = []
    for lefts, rights in groups:
        total = 0.0
        for (array, lead), right in zip(lefts, rights):
            total = total + lax.dot_general(
                array[lead], right, (((0,), (0,)), ((), ())), preferred_element_type=jnp.float32
            )
        columns.append(total)
    whole = jnp.concatenate(columns, axis=1)
    whole = whole.reshape(chips, 2, 2, -1, whole.shape[1])
    if small is not None:
        whole = jnp.concatenate([whole, jnp.stack([small, jnp.zeros_like(small)], 2)], axis=3)
    whole = whole.astype(jnp.bfloat16)
    sent = pick(whole, 1 - here[1], 1)
    return sent, pick(whole, here[1], 1), sent


def gradient_blocks(groups, here, name, small=None):
    chips = lax.axis_size("fsdp") // 2
    if groups[0][0][0][0].shape[2] % (2 * chips * PAIR):
        return gradient_plain(groups, here, small)
    arrays, specs, plan = [], [], []
    at = 0
    for lefts, rights in groups:
        first, last = at, at + rights[0].shape[1] // CHUNK
        at = last
        plan.append((first, last, len(rights)))
        tokens = rights[0].shape[0]
        for own in (0, 1):
            for array, lead in lefts:
                block = array.shape[2] // (2 * chips)
                for chip in range(chips):
                    arrays.append(array)
                    specs.append(
                        pl.BlockSpec(
                            (1, tokens, block),
                            lambda i, here, lead=lead, chip=chip, own=own: (
                                lead,
                                0,
                                2 * chip + (here[1] if own else 1 - here[1]),
                            ),
                        )
                    )
        for right in rights:
            arrays.append(right)
            specs.append(
                pl.BlockSpec(
                    (tokens, CHUNK),
                    lambda i, here, first=first, last=last: (
                        0,
                        jnp.clip(i, first, last - 1) - first,
                    ),
                )
            )
    half = block // 2
    extra = 0
    if small is not None:
        extra = EXTRA
        for own in (0, 1):
            arrays.append(pick(small, here[1] if own else 1 - here[1], 1))
            specs.append(pl.BlockSpec((chips, EXTRA, CHUNK), lambda i, here: (0, 0, i)))
    whole = pl.BlockSpec((chips, 2, half + extra, CHUNK), lambda i, here: (0, 0, 0, i))
    plan = (chips, plan, extra)
    return kernel_call(
        lambda *refs: gradient_kernel(plan, *refs),
        [here],
        arrays,
        specs,
        [((chips, 2, half + extra, at * CHUNK), jnp.bfloat16)] * 2 + [((8, PAIR), jnp.float32)],
        [whole, whole, pl.BlockSpec((8, PAIR), lambda i, here: (0, 0))],
        at,
        name,
        [pltpu.VMEM((2, len(groups[0][1]), chips * block, tokens), jnp.bfloat16)],
    )


def cross_ctx(sent, kept, gate):
    received = after(swap_core(sent), gate)
    if lax.axis_size("ctx") != 2:
        total = kept.astype(jnp.float32) + received.astype(jnp.float32)
        return total.reshape(kept.shape[0], -1, kept.shape[3]), sent, None
    side = lax.axis_index("ctx")
    mine, away = [
        pick(kept, which, 1).astype(jnp.float32) + pick(received, which, 1).astype(jnp.float32)
        for which in (side, 1 - side)
    ]
    away = away.astype(jnp.bfloat16)
    return mine, away, swap_ctx(away)


def cross_chips(crossing, gate):
    mine, _, coming = crossing
    if coming is not None:
        mine = mine + after(coming, gate).astype(jnp.float32)
    mine = mine.astype(jnp.bfloat16)
    return mine, exchange_chips(mine)


def spread_chips(parts):
    return jnp.sum(parts.astype(jnp.float32), axis=0).astype(jnp.bfloat16)


def spread_end(total, halves):
    if lax.axis_size("ctx") != 2:
        return lax.psum(total, "ctx").reshape(halves, -1, total.shape[1])
    other = swap_ctx(total)
    leading = lax.axis_index("ctx") == 0
    return jnp.stack([jnp.where(leading, total, other), jnp.where(leading, other, total)])


def other_ctx(rows, axis):
    if lax.axis_size("ctx") != 2:
        return lax.all_gather(rows, "ctx", axis=axis, tiled=True)
    return swap_ctx(rows)


def other_tokens(tokens, gate):
    seq_count = tokens.shape[0]
    if lax.axis_size("ctx") != 2 or lax.axis_size("tp") != 2 or seq_count % 2:
        return other_ctx(tokens, 1)
    side = lax.axis_index("tp")
    halves = tokens.reshape(2, seq_count // 2, *tokens.shape[1:])
    mine = after(swap_ctx(pick(halves, side, 0)), gate)
    theirs = swap_tp(mine)
    return jnp.concatenate(
        [jnp.where(side == 0, mine, theirs), jnp.where(side == 0, theirs, mine)]
    )


EXTRA = 16


def body(
    tokens,
    picture_starts,
    ln1_gain,
    ln1_shift,
    w_qkv,
    qv_bias,
    w_proj,
    proj_bias,
    ln2_gain,
    ln2_shift,
    w_fc1,
    fc1_bias,
    w_fc2,
    fc2_bias,
    out_grad,
):
    seq_count, local_len, width = tokens.shape
    fsdp = lax.axis_size("fsdp")
    chips = fsdp // 2
    ranks = lax.axis_size("ctx")
    rank = lax.axis_index("ctx")
    full_len = ranks * local_len
    local_width = w_qkv.shape[2]
    local_heads = local_width // HD
    units = w_fc1.shape[1]
    sequences = range(seq_count)
    spot = lax.axis_index("fsdp")
    side = lax.axis_index("tp")
    here = jnp.stack([spot // 2, spot % 2, rank, side]).astype(jnp.int32)
    place = jnp.stack([rank, jnp.int32(ranks)]).astype(jnp.int32)
    piece_ids = jnp.arange(full_len // PIECE, dtype=jnp.int32)
    pictures = jnp.any(
        piece_ids[None, :, None] == (picture_starts // PIECE)[:, None, :], axis=2
    ).astype(jnp.int32)

    block = ln1_gain.shape[0]
    qv_size, fc1_size = qv_bias.size, fc1_bias.size
    qv_lines = qv_size // block
    small = jnp.concatenate(
        [
            jnp.stack([ln1_gain, ln1_shift, proj_bias, ln2_gain, ln2_shift, fc2_bias]),
            qv_bias.reshape(-1, block),
            fc1_bias.reshape(-1, block),
        ]
    )
    small = jnp.pad(small, ((0, EXTRA - small.shape[0]), (0, 0)))
    qkv_bundle = gather_chips(halves_of(w_qkv.reshape(-1, 3 * local_width)))
    far_proj = swap_tp(w_proj)
    proj_halves = halves_of(
        jnp.concatenate(
            [jnp.where(side == 0, w_proj, far_proj), jnp.where(side == 0, far_proj, w_proj)]
        )
    )
    small = jnp.broadcast_to(small, (proj_halves.shape[0], *small.shape))
    proj_halves = jnp.concatenate([proj_halves, small], axis=1)
    proj_bundle = gather_chips(after(proj_halves, qkv_bundle))
    far_tokens = other_tokens(tokens, proj_bundle)
    fc1_bundle = gather_chips(after(halves_of(w_fc1), proj_bundle))
    full_qkv = placed_rows(gather_rest(qkv_bundle), here, "place_qkv")
    proj_bundles = [proj_bundle, swap_core(proj_bundle)]

    first = jnp.where(spot % 2 == 0, proj_bundles[0], proj_bundles[1])[:, -EXTRA:]
    second = jnp.where(spot % 2 == 0, proj_bundles[1], proj_bundles[0])[:, -EXTRA:]
    smalls = jnp.stack([first, second], axis=1).reshape(fsdp, EXTRA, block).astype(jnp.float32)
    vectors = [smalls[:, i].reshape(-1) for i in range(6)]
    gain_one, shift_one, bias_proj, gain_two, shift_two, bias_fc2 = vectors
    qv_rows = smalls[:, 6 : 6 + qv_lines].reshape(fsdp, 2, local_heads, HD // fsdp)
    qv_rows = qv_rows.transpose(1, 2, 0, 3).reshape(2, local_width)
    bias_fc1 = smalls[:, 6 + qv_lines : 6 + qv_lines + fc1_size // block]
    bias_fc1 = bias_fc1.reshape(fsdp, units // HD, HD // fsdp).transpose(1, 0, 2).reshape(1, -1)
    bias_qkv = jnp.concatenate([qv_rows[0], jnp.zeros_like(qv_rows[0]), qv_rows[1]])
    lines = jnp.stack([bias_proj, gain_two, shift_two, gain_one])

    def project(rows):
        normed = layer_norm(rows.astype(jnp.float32), gain_one, shift_one).astype(jnp.bfloat16)
        result = jnp.einsum("sld,de->sle", normed, full_qkv, preferred_element_type=jnp.float32)
        return normed, (result + bias_qkv).astype(jnp.bfloat16)

    normed_one, triple = project(tokens)
    _, far_triple = project(far_tokens)
    fc2_bundle = gather_chips(after(halves_of(w_fc2), fc1_bundle))
    fc1_bundles = gather_rest(fc1_bundle)
    proj_bundles = gather_rest(proj_bundle, proj_bundles)
    attended, logs = [], []
    for index in sequences:
        gate = [attended[-1], fc2_bundle, *fc1_bundles[1:3]] if index else proj_bundles[2:3]
        heads, log = attention_forward(triple, far_triple, after(place, *gate), pictures, index)
        attended.append(heads)
        logs.append(log)
    tp_attended = [after(swap_tp(heads), attended[-1]) for heads in attended]
    fc2_bundles = gather_rest(fc2_bundle, None, attended[-1])
    all_attended = jnp.stack(attended)
    weights = [proj_bundles, fc1_bundles, fc2_bundles]
    if block % PAIR:
        weights = [
            [placed_columns_plain([b[:, :-EXTRA] for b in proj_bundles], here)],
            fc1_bundles,
            [placed_columns_plain(fc2_bundles, here)],
        ]
    far_attended = other_ctx(after(all_attended, weights[2][-1]), 1)
    far_logs = other_ctx(after(jnp.stack(logs), weights[2][-1]), 3)
    residuals, normed_two, actives, hidden_grads, feeds, backs, swapped_twos = [], [], [], [], [], [], []
    hidden_sums = 0.0
    for index in sequences:
        gate = [backs[-1], far_attended, far_logs] if index else []
        residual, normed, active, hidden_grad, feed, back, hidden_sum, own_proj = feed_forward(
            attended[index],
            after(tp_attended[index], *backs[-1:]),
            tokens,
            out_grad,
            lines,
            bias_fc1,
            weights,
            after(here, *gate),
            index,
        )
        residuals.append(residual)
        normed_two.append(normed)
        actives.append(active)
        hidden_grads.append(hidden_grad)
        feeds.append(feed)
        backs.append(back)
        swapped_twos.append(swap_tp(back))
        hidden_sums = hidden_sums + hidden_sum[0]

    fc2_groups = [([(out_grad, s) for s in sequences], actives)]
    fc1_groups = [([(normed[None], 0) for normed in normed_two], hidden_grads)]
    branches, head_grads, far_head_grads = [], [], []
    two_sums = 0.0
    gate = backs[-1]
    for index in sequences:
        branch, head_grad, two_sum = norm_two_backward(
            backs[index],
            swapped_twos[index],
            residuals[index],
            out_grad,
            lines,
            own_proj,
            after(here, gate),
            index,
        )
        branches.append(branch)
        head_grads.append(head_grad)
        far_head_grads.append(other_ctx(head_grad, 0))
        two_sums = two_sums + two_sum
        if index == 0:
            blocks_fc2 = gradient_blocks(fc2_groups, after(here, head_grad), "grad_fc2")
            blocks_fc1 = gradient_blocks(fc1_groups, after(here, blocks_fc2[2]), "grad_fc1")
            cross_fc2 = cross_ctx(*blocks_fc2[:2], blocks_fc1[2])
            gate = cross_fc2[1]
    cross_fc1 = cross_ctx(*blocks_fc1[:2], head_grads[-1])

    grad_triples, back_ones, swapped_ones, outputs = [], [], [], []
    one_sums, triple_sums = 0.0, 0.0
    gate = cross_fc1[1]
    for index in sequences:
        if index == 0:
            feed = after(feeds[0], gate)
            swapped_feed = swap_tp(feed)
        grad_triple = attention_backward(
            (triple, attended[index], head_grads[index], logs[index]),
            (far_triple, far_attended[index], far_head_grads[index], far_logs[index]),
            after(place, gate),
            pictures,
            index,
        )
        gate = grad_triple
        if index == 0:
            gate, arrived_fc2 = cross_chips(cross_fc2, grad_triple)
        if index == seq_count - 1:
            total_fc2 = spread_chips(after(arrived_fc2, grad_triple))
            gate, arrived_fc1 = cross_chips(cross_fc1, total_fc2)
        back_one, one_sum, triple_sum = qkv_backward(
            grad_triple, tokens, full_qkv, after(here, gate), index
        )
        gate = back_one
        grad_triples.append(grad_triple)
        back_ones.append(back_one)
        swapped_ones.append(swap_tp(back_one))
        one_sums = one_sums + one_sum
        triple_sums = triple_sums + triple_sum[0]

    def finish_output(index, mine, theirs):
        total = mine.astype(jnp.float32) + theirs.astype(jnp.float32)
        outputs.append((residuals[index] + total + bias_fc2).astype(jnp.bfloat16))

    finish_output(0, feed, after(swapped_feed, back_ones[-1]))
    last_feeds = [after(feeds[index], back_ones[-1]) for index in range(1, seq_count)]
    last_swapped = [swap_tp(feed) for feed in last_feeds]

    out_sums = jnp.sum(out_grad.astype(jnp.float32), axis=(0, 1))
    grad_qv = jnp.concatenate([triple_sums[:local_width], triple_sums[2 * local_width :]])
    vectors = [one_sums[0], one_sums[1], two_sums[2], two_sums[0], two_sums[1], out_sums]
    packed = jnp.concatenate(
        [vector.reshape(fsdp, block) for vector in vectors]
        + [
            grad_qv.reshape(2, local_heads, fsdp, HD // fsdp)
            .transpose(2, 0, 1, 3)
            .reshape(fsdp, -1),
            hidden_sums.reshape(-1, fsdp, HD // fsdp).transpose(1, 0, 2).reshape(fsdp, -1),
        ],
        axis=1,
    )
    last_width = 3 * local_width + local_width
    packed = jnp.pad(packed[:, None], ((0, 0), (0, EXTRA - 1), (0, last_width - packed.shape[1])))
    packed = packed.reshape(chips, 2, EXTRA, last_width)
    last_groups = [
        ([(normed_one, s) for s in sequences], grad_triples),
        ([(branch[None], 0) for branch in branches], attended),
    ]
    def norm_one(index, gate):
        return norm_one_backward(
            back_ones[index],
            swapped_ones[index],
            tokens,
            branches[index],
            lines,
            after(here, gate),
            index,
        )

    blocks_last = gradient_blocks(last_groups, after(here, back_ones[-1]), "grad_last", packed)
    grad_tokens = [norm_one(0, blocks_last[2])]
    cross_last = cross_ctx(*blocks_last[:2], grad_tokens[0])
    for index in range(1, seq_count):
        grad_tokens.append(norm_one(index, cross_last[1]))
    total_fc1 = spread_chips(after(arrived_fc1, grad_tokens[-1]))
    for index in range(1, seq_count):
        finish_output(index, last_feeds[index - 1], after(last_swapped[index - 1], total_fc1))
    _, arrived_last = cross_chips(cross_last, total_fc1)
    sums_fc2 = spread_end(total_fc2, 2)
    sums_fc1 = spread_end(total_fc1, 2)
    sums_last = spread_end(spread_chips(arrived_last), 2)
    small = sums_last[0, -EXTRA]
    norm_one = small[: 2 * block]
    norm_one = norm_one.astype(jnp.float32) + swap_tp(norm_one).astype(jnp.float32)
    small = small.astype(jnp.float32)
    vectors = [norm_one[:block], norm_one[block:]]
    vectors += [small[i * block : (i + 1) * block] for i in range(2, 6)]
    shard_qv = small[6 * block : 6 * block + qv_size].reshape(qv_bias.shape)
    shard_fc1_bias = small[6 * block + qv_size :][:fc1_size].reshape(fc1_bias.shape)
    sums_last = sums_last[:, : block // 2].reshape(block, -1).astype(jnp.float32)
    return (
        jnp.stack(outputs),
        jnp.stack(grad_tokens),
        vectors[0],
        vectors[1],
        sums_last[:, : 3 * local_width].reshape(-1, 3, local_width),
        shard_qv,
        sums_last[:, 3 * local_width :].T,
        vectors[2],
        vectors[3],
        vectors[4],
        sums_fc1.reshape(block, -1).astype(jnp.float32),
        shard_fc1_bias,
        sums_fc2.reshape(block, -1).astype(jnp.float32).T,
        vectors[5],
    )


def solution(mesh):
    return jax.shard_map(
        body,
        mesh=mesh,
        in_specs=(
            P("fsdp", "ctx", None),
            P("fsdp", None),
            P("fsdp"),
            P("fsdp"),
            P("fsdp", None, "tp"),
            P(None, "tp", "fsdp"),
            P("tp", "fsdp"),
            P("fsdp"),
            P("fsdp"),
            P("fsdp"),
            P("fsdp", "tp"),
            P("tp", "fsdp"),
            P("tp", "fsdp"),
            P("fsdp"),
            P("fsdp", "ctx", None),
        ),
        out_specs=(
            P("fsdp", "ctx", None),
            P("fsdp", "ctx", None),
            P("fsdp"),
            P("fsdp"),
            P("fsdp", None, "tp"),
            P(None, "tp", "fsdp"),
            P("tp", "fsdp"),
            P("fsdp"),
            P("fsdp"),
            P("fsdp"),
            P("fsdp", "tp"),
            P("tp", "fsdp"),
            P("tp", "fsdp"),
            P("fsdp"),
        ),
        check_vma=False,
    )
```

```python
import jax
import jax.numpy as jnp
from jax import lax
from jax.experimental import pallas as pl
from jax.experimental.pallas import tpu as pltpu
from jax.sharding import PartitionSpec as P

HD = 64
PAIR = 2 * HD
PIECE = 256
SCALE = HD ** (-0.5)
KERNEL_VMEM = 56 * 1024 * 1024

epsilon = 1e-05
masked_value = -1e30


def layer_norm(values, gain_vec, shift_vec):
    average = jnp.mean(values, axis=-1, keepdims=True)
    centred = values - average
    variance = jnp.mean(centred * centred, axis=-1, keepdims=True)
    return centred * lax.rsqrt(variance + epsilon) * gain_vec + shift_vec


def gelu_tanh(values):
    return jax.nn.gelu(values, approximate=True)


NT = (((1,), (1,)), ((), ()))


def dot_nt(left, right):
    return lax.dot_general(left, right, NT, preferred_element_type=jnp.float32)


def dot_nn(left, right):
    return jnp.dot(left, right, preferred_element_type=jnp.float32)


def head_lanes(head):
    lanes = lax.broadcasted_iota(jnp.int32, (1, PAIR), 1)
    return (lanes >= head * HD) & (lanes < (head + 1) * HD)


def only_head(rows, head):
    return jnp.where(head_lanes(head), rows, jnp.zeros_like(rows))


def diagonal_mask(scores, joined):
    key_row = lax.broadcasted_iota(jnp.int32, scores.shape, 0)
    query_lane = lax.broadcasted_iota(jnp.int32, scores.shape, 1)
    return (key_row <= query_lane) | joined


def chunk_start(step, place, local_len, chunks):
    return 0 if chunks == 1 else pl.multiple_of(step * local_len, local_len)


SCORE_TILE = 32


def score_tiles(count):
    return [slice(start, start + SCORE_TILE) for start in range(0, count, SCORE_TILE)]


def folded(rows, combine):
    parts = [rows[start : start + 8] for start in range(0, rows.shape[0], 8)]
    while len(parts) > 1:
        parts = [
            combine(parts[i], parts[i + 1]) if i + 1 < len(parts) else parts[i]
            for i in range(0, len(parts), 2)
        ]
    return parts[0]


def attention_forward_kernel(
    place, pictures, q_ref, k_ref, v_ref, k_far, v_far, out_ref, log_ref, scores, weights, values
):
    rank = place[0]
    sequence = place[2]
    local_len = q_ref.shape[1]
    blocks = local_len // PIECE
    chunks = k_far.shape[1] // local_len
    values[...] = v_ref[0].T
    states = [(head, block) for head in range(2) for block in range(blocks)]
    scaled, peaks = [], []
    for index, (head, block) in enumerate(states):
        query = only_head(q_ref[0, block * PIECE : (block + 1) * PIECE, :] * SCALE, head)
        scaled.append(query)
        joined = pictures[sequence, rank * blocks + block] > 0
        count = (block + 1) * PIECE
        scores[index, :count] = dot_nt(k_ref[0, :count], query)
        peak = jnp.full((8, PIECE), masked_value, jnp.float32)
        for tile in score_tiles(count):
            part = scores[index, tile]
            if tile.start >= block * PIECE:
                key_row = lax.broadcasted_iota(jnp.int32, part.shape, 0) + (
                    tile.start - block * PIECE
                )
                lane = lax.broadcasted_iota(jnp.int32, part.shape, 1)
                part = jnp.where((key_row <= lane) | joined, part, masked_value)
                scores[index, tile] = part
            peak = jnp.maximum(peak, folded(part, jnp.maximum))
        peaks.append(peak)

    def far_scores(step, carried):
        keys = k_far[0, pl.ds(chunk_start(step, place, local_len, chunks), local_len), :]
        base = pl.multiple_of((step + 1) * local_len, local_len)
        after = []
        for index, peak in enumerate(carried):
            part = dot_nt(keys, scaled[index])
            scores[index, pl.ds(base, local_len)] = part
            for tile in score_tiles(local_len):
                peak = jnp.maximum(peak, folded(part[tile], jnp.maximum))
            after.append(peak)
        return after

    peaks = lax.fori_loop(0, rank, far_scores, peaks)
    peaks = [jnp.max(peak, axis=0, keepdims=True) for peak in peaks]
    gathered = []
    for index, (head, block) in enumerate(states):
        count = (block + 1) * PIECE
        total = jnp.zeros((8, PIECE), jnp.float32)
        for tile in score_tiles(count):
            weight = jnp.exp(scores[index, tile] - peaks[index])
            total = total + folded(weight, jnp.add)
            weights[index, tile] = weight.astype(jnp.bfloat16)
        gathered.append(
            (total, dot_nn(values[head * HD : (head + 1) * HD, :count], weights[index, :count]))
        )

    def far_values(step, carried):
        base = pl.multiple_of((step + 1) * local_len, local_len)
        far = v_far[0, pl.ds(chunk_start(step, place, local_len, chunks), local_len), :].T
        after = []
        for index, (total, sums) in enumerate(carried):
            head = states[index][0]
            for tile in score_tiles(local_len):
                weight = jnp.exp(
                    scores[index, pl.ds(base + tile.start, SCORE_TILE)] - peaks[index]
                )
                total = total + folded(weight, jnp.add)
                weights[index, tile] = weight.astype(jnp.bfloat16)
            sums = sums + dot_nn(far[head * HD : (head + 1) * HD], weights[index])
            after.append((total, sums))
        return after

    gathered = lax.fori_loop(0, rank, far_values, gathered)
    for block in range(blocks):
        rows = slice(block * PIECE, (block + 1) * PIECE)
        halves = []
        for head in range(2):
            index = head * blocks + block
            total = jnp.sum(gathered[index][0], axis=0, keepdims=True)
            halves.append(gathered[index][1] / total)
            log_ref[0, head : head + 1, rows] = peaks[index] + jnp.log(total)
        out_ref[rows, :] = jnp.concatenate(halves, axis=0).T.astype(out_ref.dtype)


def attention_forward(triple, far, place, pictures, index):
    place = jnp.concatenate([place, jnp.full((1,), index, jnp.int32)])
    _, local_len, triple_width = triple.shape
    far_len = far.shape[1]
    local_width = triple_width // 3
    pairs = local_width // PAIR

    def part(length, offset):
        return pl.BlockSpec(
            (1, length, PAIR), lambda p, place, pics: (index, 0, offset * pairs + p)
        )

    return pl.pallas_call(
        attention_forward_kernel,
        grid_spec=pltpu.PrefetchScalarGridSpec(
            num_scalar_prefetch=2,
            grid=(pairs,),
            in_specs=[
                part(local_len, 0),
                part(local_len, 1),
                part(local_len, 2),
                part(far_len, 1),
                part(far_len, 2),
            ],
            out_specs=[
                pl.BlockSpec((local_len, PAIR), lambda p, place, pics: (0, p)),
                pl.BlockSpec((1, 2, local_len), lambda p, place, pics: (p, 0, 0)),
            ],
            scratch_shapes=[
                pltpu.VMEM((2 * local_len // PIECE, local_len + far_len, PIECE), jnp.float32),
                pltpu.VMEM((2 * local_len // PIECE, local_len, PIECE), jnp.bfloat16),
                pltpu.VMEM((PAIR, local_len), jnp.bfloat16),
            ],
        ),
        out_shape=[
            jax.ShapeDtypeStruct((local_len, local_width), jnp.bfloat16),
            jax.ShapeDtypeStruct((pairs, 2, local_len), jnp.float32),
        ],
        compiler_params=pltpu.CompilerParams(vmem_limit_bytes=KERNEL_VMEM),
        cost_estimate=pl.CostEstimate(flops=50000000000, bytes_accessed=0, transcendentals=0),
        name="attention_forward",
    )(place, pictures, triple, triple, triple, far, far)


def attention_backward_kernel(
    place,
    pictures,
    q_ref,
    k_ref,
    v_ref,
    out_ref,
    grad_ref,
    log_ref,
    q_far,
    k_far,
    v_far,
    out_far,
    grad_far,
    log_far,
    triple_ref,
):
    rank = place[0]
    ranks = place[1]
    sequence = place[2]
    pair = pl.program_id(0)
    local_len = triple_ref.shape[0]
    local_width = triple_ref.shape[1] // 3
    blocks = local_len // PIECE
    chunks = k_far.shape[1] // local_len

    def sides_of(queries, grads, outs, logs):
        turned = (grads.astype(jnp.float32) * outs.astype(jnp.float32)).T
        queries = queries * SCALE
        sides = []
        for head in range(2):
            delta = jnp.sum(turned[head * HD : (head + 1) * HD], axis=0, keepdims=True)
            sides.append(
                (
                    only_head(queries, head),
                    only_head(grads, head),
                    logs[head : head + 1],
                    delta,
                )
            )
        return sides

    def pieces(keys, values, query, grad, log, delta, mask=None):
        scores = dot_nt(keys, query)
        probs = jnp.exp(scores - log)
        if mask is not None:
            probs = jnp.where(mask(probs), probs, 0.0)
        grad_probs = dot_nt(values, grad)
        return probs, (probs * (grad_probs - delta)).astype(jnp.bfloat16)

    key_own = k_ref[0]
    value_own = v_ref[0]
    key_turned = key_own.T
    sides = sides_of(q_ref[0], grad_ref[...], out_ref[...], log_ref[0])
    grad_keys = [None] * blocks
    grad_values = [None] * blocks
    grad_queries = []

    def add(total, part):
        return part if total is None else total + part

    for head in range(2):
        queries, grads, logs, deltas = sides[head]
        for block in range(blocks):
            rows = slice(block * PIECE, (block + 1) * PIECE)
            joined = pictures[sequence, rank * blocks + block] > 0
            grad_query = None
            for key_block in range(block + 1):
                key_rows = slice(key_block * PIECE, (key_block + 1) * PIECE)
                mask = (lambda p, j=joined: diagonal_mask(p, j)) if key_block == block else None
                probs, grad_scores = pieces(
                    key_own[key_rows],
                    value_own[key_rows],
                    queries[rows],
                    grads[rows],
                    logs[:, rows],
                    deltas[:, rows],
                    mask,
                )
                grad_values[key_block] = add(
                    grad_values[key_block], dot_nn(probs.astype(jnp.bfloat16), grads[rows])
                )
                grad_keys[key_block] = add(
                    grad_keys[key_block], dot_nn(grad_scores, queries[rows])
                )
                grad_query = add(
                    grad_query,
                    dot_nn(key_turned[head * HD : (head + 1) * HD, key_rows], grad_scores),
                )
            grad_queries.append(grad_query)

    def earlier(step, carried):
        start = chunk_start(step, place, local_len, chunks)
        keys = k_far[0, pl.ds(start, local_len), :]
        values = v_far[0, pl.ds(start, local_len), :]
        turned = keys.T
        after = []
        for index, total in enumerate(carried):
            head, block = index // blocks, index % blocks
            rows = slice(block * PIECE, (block + 1) * PIECE)
            queries, grads, logs, deltas = sides[head]
            _, grad_scores = pieces(
                keys, values, queries[rows], grads[rows], logs[:, rows], deltas[:, rows]
            )
            after.append(total + dot_nn(turned[head * HD : (head + 1) * HD], grad_scores))
        return after

    grad_queries = lax.fori_loop(0, rank, earlier, grad_queries)
    for block in range(blocks):
        rows = slice(block * PIECE, (block + 1) * PIECE)
        both = jnp.concatenate([grad_queries[head * blocks + block] for head in range(2)], axis=0)
        triple_ref[rows, pl.ds(pl.multiple_of(pair * PAIR, PAIR), PAIR)] = (
            (both * SCALE).T.astype(triple_ref.dtype)
        )

    def later(step, carried):
        start = chunk_start(step, place, local_len, chunks)
        window = pl.ds(start, local_len)
        sides = sides_of(
            q_far[0, window, :], grad_far[window, :], out_far[window, :], log_far[0, :, window]
        )
        keys_after, values_after = list(carried[0]), list(carried[1])
        for head in range(2):
            queries, grads, logs, deltas = sides[head]
            for block in range(blocks):
                rows = slice(block * PIECE, (block + 1) * PIECE)
                probs, grad_scores = pieces(
                    key_own[rows], value_own[rows], queries, grads, logs, deltas
                )
                values_after[block] = values_after[block] + dot_nn(
                    probs.astype(jnp.bfloat16), grads
                )
                keys_after[block] = keys_after[block] + dot_nn(grad_scores, queries)
        return keys_after, values_after

    grad_keys, grad_values = lax.fori_loop(rank + 1, ranks, later, (grad_keys, grad_values))
    for block in range(blocks):
        rows = slice(block * PIECE, (block + 1) * PIECE)
        for part, grads in ((1, grad_keys), (2, grad_values)):
            column = pl.multiple_of(part * local_width + pair * PAIR, PAIR)
            triple_ref[rows, pl.ds(column, PAIR)] = grads[block].astype(triple_ref.dtype)


def attention_backward(own, other, place, pictures, index):
    place = jnp.concatenate([place, jnp.full((1,), index, jnp.int32)])
    _, local_len, triple_width = own[0].shape
    pairs = triple_width // (3 * PAIR)
    specs = []
    for length in (local_len, other[0].shape[1]):
        for offset in range(3):
            specs.append(
                pl.BlockSpec(
                    (1, length, PAIR),
                    lambda p, place, pics, offset=offset: (index, 0, offset * pairs + p),
                )
            )
        specs += [pl.BlockSpec((length, PAIR), lambda p, place, pics: (0, p))] * 2
        specs.append(pl.BlockSpec((1, 2, length), lambda p, place, pics: (p, 0, 0)))
    return pl.pallas_call(
        attention_backward_kernel,
        grid_spec=pltpu.PrefetchScalarGridSpec(
            num_scalar_prefetch=2,
            grid=(pairs,),
            in_specs=specs,
            out_specs=pl.BlockSpec((local_len, triple_width), lambda p, place, pics: (0, 0)),
        ),
        out_shape=jax.ShapeDtypeStruct((local_len, triple_width), jnp.bfloat16),
        compiler_params=pltpu.CompilerParams(vmem_limit_bytes=KERNEL_VMEM),
        cost_estimate=pl.CostEstimate(flops=50000000000, bytes_accessed=0, transcendentals=0),
        name="attention_backward",
    )(place, pictures, *([own[0]] * 3), *own[1:], *([other[0]] * 3), *other[1:])


def core_swap():
    return [(place, place ^ 1) for place in range(lax.axis_size("fsdp"))]


PAIR_SWAP = [(0, 1), (1, 0)]


def swap_core(rows):
    return lax.ppermute(rows, "fsdp", core_swap())


def swap_ctx(rows):
    return lax.ppermute(rows, "ctx", PAIR_SWAP)


def swap_tp(rows):
    return lax.ppermute(rows, "tp", PAIR_SWAP)


def exchange_chips(rows):
    fsdp = lax.axis_size("fsdp")
    groups = [list(range(core, fsdp, 2)) for core in range(2)]
    return lax.all_to_all(
        rows, "fsdp", split_axis=0, concat_axis=0, tiled=True, axis_index_groups=groups
    )


def pick(array, index, axis):
    return lax.dynamic_index_in_dim(array, index, axis, keepdims=False)


def after(value, *others):
    return lax.optimization_barrier((value, *others))[0]


def halves_of(shard):
    halves = 2 if lax.axis_size("ctx") == 2 else 1
    return shard.reshape(halves, -1, shard.shape[1])


def gather_chips(halves):
    chips = lax.axis_size("fsdp") // 2
    part = pick(halves, lax.axis_index("ctx"), 0) if halves.shape[0] == 2 else halves[0]
    return exchange_chips(jnp.broadcast_to(part, (chips, *part.shape)))


def chip_shift(step):
    chips = lax.axis_size("fsdp") // 2
    return [
        (2 * chip + core, 2 * ((chip + step) % chips) + core)
        for chip in range(chips)
        for core in range(2)
    ]


def shift_chips(halves):
    part = pick(halves, lax.axis_index("ctx"), 0) if halves.shape[0] == 2 else halves[0]
    chips = lax.axis_size("fsdp") // 2
    return [part] + [lax.ppermute(part, "fsdp", chip_shift(step)) for step in range(1, chips)]


def gather_rest(bundle, *gate, near=None):
    bundles = [bundle, swap_core(bundle) if near is None else near]
    if lax.axis_size("ctx") == 2:
        across = after(swap_ctx(bundle), *gate)
        bundles += [across, swap_core(across)]
    return bundles


def kernel_call(kernel, scalars, arrays, in_specs, outs, out_specs, grid, name, scratch=(), flops=0):
    size = sum(array.size for array in arrays)
    return pl.pallas_call(
        kernel,
        grid_spec=pltpu.PrefetchScalarGridSpec(
            num_scalar_prefetch=len(scalars),
            grid=(grid,),
            in_specs=in_specs,
            out_specs=out_specs,
            scratch_shapes=list(scratch),
        ),
        out_shape=[jax.ShapeDtypeStruct(shape, dtype) for shape, dtype in outs],
        compiler_params=pltpu.CompilerParams(vmem_limit_bytes=KERNEL_VMEM),
        cost_estimate=pl.CostEstimate(flops=50000000000, bytes_accessed=0, transcendentals=0),
        name=name,
    )(*scalars, *arrays)


def owners(here, sides):
    for index in range(2 * sides):
        core = here[1] if index % 2 == 0 else 1 - here[1]
        yield core, ((here[2] if index < 2 else 1 - here[2]) if sides == 2 else 0)


def placed_rows(bundles, here, name, extra):
    fsdp = lax.axis_size("fsdp")
    sides = len(bundles) // 2
    chips, total, width = bundles[0].shape
    height = total - extra
    chunk = 512

    def kernel(here, *refs):
        for index, (core, side) in enumerate(owners(here, sides)):
            for chip in range(chips):
                refs[-1][(2 * chip + core) * sides + side] = refs[index][chip, :height]

    (result,) = kernel_call(
        kernel,
        [here],
        bundles,
        [pl.BlockSpec((chips, total, chunk), lambda i, here: (0, 0, i))] * (2 * sides),
        [((fsdp * sides, height, width), jnp.bfloat16)],
        [pl.BlockSpec((fsdp * sides, height, chunk), lambda i, here: (0, 0, i))],
        width // chunk,
        name,
    )
    return result.reshape(-1, width)


def placed_columns_plain(bundles, here):
    sides = []
    for mine, other in zip(bundles[::2], bundles[1::2]):
        first = jnp.where(here[1] == 0, mine, other)
        second = jnp.where(here[1] == 0, other, mine)
        both = jnp.stack([first, second], axis=1)
        sides.append(both.reshape(-1, *both.shape[2:]))
    if len(sides) == 2:
        sides = [
            jnp.where(here[2] == 0, sides[0], sides[1]),
            jnp.where(here[2] == 0, sides[1], sides[0]),
        ]
    fsdp, _, width = sides[0].shape
    return jnp.concatenate(sides, axis=1).transpose(1, 0, 2).reshape(-1, fsdp * width)


def weight_copies(bundles, target, here, columns, shifted=False):
    if len(bundles) == 1:
        yield bundles[0], target
        return
    sides = len(bundles) // 2
    for index, (core, side) in enumerate(owners(here, sides)):
        chips, _, width = bundles[index].shape
        height = target.shape[0] // (sides if columns else 2 * chips * sides)
        for chip in range(chips):
            source = bundles[index].at[chip, pl.ds(0, height)]
            block = 2 * (lax.rem(here[0] + chips - chip, chips) if shifted else chip) + core
            if columns:
                across = pl.ds(pl.multiple_of(block * width, width), width)
                yield source, target.at[pl.ds(pl.multiple_of(side * height, height), height), across]
            else:
                row = pl.multiple_of((block * sides + side) * height, height)
                yield source, target.at[pl.ds(row, height)]


UNITS = 1024
TILE = 16
ROOT = 0.7978845608028654
CUBIC = 0.044715


def feed_kernel(counts, here, *refs):
    own_ref, tp_ref, tokens_ref, grad_ref, vector_ref, bias_ref = refs[:6]
    at = 6
    bundles = []
    for count in counts:
        bundles.append(refs[at : at + count])
        at += count
    residual_ref, normed_ref, active_ref, hidden_ref, feed_ref, back_ref, sum_ref, proj_ref = refs[
        at : at + 8
    ]
    proj, first, second, feed, back, hidden_pre, grad_active, semaphores = refs[at + 8 :]
    step = pl.program_id(0)
    copies = [
        weight_copies(bundles[0], proj, here, True),
        weight_copies(bundles[1], first, here, False),
        weight_copies(bundles[2], second, here, True, True),
    ]
    made, number = [], 0
    for group in copies:
        made.append([])
        for source, place in group:
            made[-1].append(pltpu.make_async_copy(source, place, semaphores.at[number]))
            number += 1
    rows = proj.shape[0] // 2
    kept = pltpu.make_async_copy(
        proj.at[pl.ds(pl.multiple_of(here[3] * rows, rows), rows)],
        proj_ref,
        semaphores.at[number],
    )

    @pl.when(step == 0)
    def _():
        for group in made:
            for copy in group:
                copy.start()
        for copy in made[0]:
            copy.wait()
        kept.start()
        leading = here[3] == 0
        low = jnp.where(leading, own_ref[...], tp_ref[...])
        high = jnp.where(leading, tp_ref[...], own_ref[...])
        feed[...] = dot_nn(low, proj[:rows]) + dot_nn(high, proj[rows:])
        for start in range(0, feed.shape[0], TILE):
            lines = slice(start, start + TILE)
            residual = tokens_ref[0, lines].astype(jnp.float32) + feed[lines] + vector_ref[0:1]
            residual_ref[lines] = residual
            unit, _ = centred_rows(residual)
            normed_ref[lines] = (unit * vector_ref[1:2] + vector_ref[2:3]).astype(
                normed_ref.dtype
            )
        for copy in made[1]:
            copy.wait()

    units = pl.ds(pl.multiple_of(step * UNITS, UNITS), UNITS)
    hidden_pre[...] = dot_nn(normed_ref[...], first[:, units])

    @pl.when(step == 0)
    def _():
        for copy in made[2]:
            copy.wait()
        kept.wait()

    grad_active[...] = dot_nt(grad_ref[0], second[units])
    totals = jnp.zeros((TILE, UNITS), jnp.float32)
    for start in range(0, feed.shape[0], TILE):
        lines = slice(start, start + TILE)
        hidden = hidden_pre[lines] + bias_ref[...]
        square = hidden * hidden
        bent = jnp.tanh(hidden * (ROOT + ROOT * CUBIC * square))
        share = 0.5 + 0.5 * bent
        active_ref[lines] = (hidden * share).astype(jnp.bfloat16)
        slope = share + hidden * (1.0 - bent * bent) * (
            0.5 * ROOT + 1.5 * ROOT * CUBIC * square
        )
        grad_hidden = (grad_active[lines] * slope).astype(jnp.bfloat16)
        hidden_ref[lines] = grad_hidden
        totals = totals + grad_hidden.astype(jnp.float32)
    sum_ref[...] = jnp.sum(totals, axis=0, keepdims=True)
    active = active_ref[...]
    feed_part = dot_nn(active, second[units])
    back_part = dot_nt(hidden_ref[...], first[:, units])

    @pl.when(step == 0)
    def _():
        feed[...] = feed_part
        back[...] = back_part

    @pl.when(step > 0)
    def _():
        feed[...] += feed_part
        back[...] += back_part

    @pl.when(step == pl.num_programs(0) - 1)
    def _():
        feed_ref[...] = feed[...].astype(feed_ref.dtype)
        back_ref[...] = back[...].astype(back_ref.dtype)


def feed_forward(own, tp, tokens, out_grad, vectors, bias, weights, here, index):
    local_len, local_width = own.shape
    width = tokens.shape[2]
    units = bias.shape[1]
    counts = tuple(len(group) for group in weights)
    copies = sum(1 if len(group) == 1 else len(group) * group[0].shape[0] for group in weights)
    whole = lambda shape: pl.BlockSpec(shape, lambda j, here: (0,) * len(shape))
    row = pl.BlockSpec((1, local_len, width), lambda j, here: (index, 0, 0))
    block = pl.BlockSpec((local_len, UNITS), lambda j, here: (0, j))
    line = pl.BlockSpec((1, UNITS), lambda j, here: (0, j))
    flat = [array for group in weights for array in group]
    half, full = jnp.bfloat16, jnp.float32
    return kernel_call(
        lambda *refs: feed_kernel(counts, *refs),
        [here],
        [own, tp, tokens, out_grad, vectors, bias] + flat,
        [whole(own.shape), whole(own.shape), row, row, whole(vectors.shape), line]
        + [pl.BlockSpec(memory_space=pl.ANY)] * len(flat),
        [
            ((local_len, width), full),
            ((local_len, width), half),
            ((local_len, units), half),
            ((local_len, units), half),
            ((local_len, width), half),
            ((local_len, width), half),
            ((1, units), full),
            ((local_width, width), half),
        ],
        [whole((local_len, width)), whole((local_len, width)), block, block]
        + [whole((local_len, width)), whole((local_len, width)), line]
        + [pl.BlockSpec(memory_space=pl.ANY)],
        units // UNITS,
        "feed_forward",
        [
            pltpu.VMEM((2 * local_width, width), half),
            pltpu.VMEM((width, units), half),
            pltpu.VMEM((units, width), half),
            pltpu.VMEM((local_len, width), full),
            pltpu.VMEM((local_len, width), full),
            pltpu.VMEM((local_len, UNITS), full),
            pltpu.VMEM((local_len, UNITS), full),
            pltpu.SemaphoreType.DMA((copies + 1,)),
        ],
        flops=8 * local_len * width * units,
    )


ROWS = 256


def centred_rows(rows):
    average = jnp.mean(rows, axis=-1, keepdims=True)
    centred = rows - average
    spread = lax.rsqrt(jnp.mean(centred * centred, axis=-1, keepdims=True) + epsilon)
    return centred * spread, spread


def through_norm(grads, unit, spread, gain):
    scaled = grads * gain
    return spread * (
        scaled
        - jnp.mean(scaled, axis=-1, keepdims=True)
        - unit * jnp.mean(scaled * unit, axis=-1, keepdims=True)
    )


def accumulate(ref, totals):
    total = jnp.concatenate([jnp.sum(lines, axis=0, keepdims=True) for lines in totals])

    @pl.when(pl.program_id(0) == 0)
    def _():
        ref[...] = total

    @pl.when(pl.program_id(0) > 0)
    def _():
        ref[...] += total


def tiles_of(count):
    return [slice(start, start + TILE) for start in range(0, count, TILE)]


def norm_two_kernel(
    here, own_ref, tp_ref, residual_ref, grad_ref, vector_ref, proj_ref, branch_ref, heads_ref, sum_ref
):
    totals = [jnp.zeros((TILE, own_ref.shape[1]), jnp.float32)] * 3
    for lines in tiles_of(own_ref.shape[0]):
        grads = own_ref[lines].astype(jnp.float32) + tp_ref[lines].astype(jnp.float32)
        unit, spread = centred_rows(residual_ref[lines])
        total = grad_ref[0, lines].astype(jnp.float32) + through_norm(
            grads, unit, spread, vector_ref[1:2]
        )
        branch = total.astype(jnp.bfloat16)
        branch_ref[lines] = branch
        totals = [
            totals[0] + grads * unit,
            totals[1] + grads,
            totals[2] + branch.astype(jnp.float32),
        ]
    heads_ref[...] = dot_nt(branch_ref[...], proj_ref[...]).astype(heads_ref.dtype)
    accumulate(sum_ref, totals)


def norm_two_backward(own, tp, residual, out_grad, vectors, proj, here, index):
    local_len, width = own.shape
    local_width = proj.shape[0]
    whole = lambda shape: pl.BlockSpec(shape, lambda i, here: (0,) * len(shape))
    row = pl.BlockSpec((ROWS, width), lambda i, here: (i, 0))
    return kernel_call(
        norm_two_kernel,
        [here],
        [own, tp, residual, out_grad, vectors, proj],
        [row, row, row, pl.BlockSpec((1, ROWS, width), lambda i, here: (index, i, 0))]
        + [whole(vectors.shape), whole(proj.shape)],
        [
            ((local_len, width), jnp.bfloat16),
            ((local_len, local_width), jnp.bfloat16),
            ((3, width), jnp.float32),
        ],
        [row, pl.BlockSpec((ROWS, local_width), lambda i, here: (i, 0)), whole((3, width))],
        local_len // ROWS,
        "norm_two_backward",
        flops=2 * local_len * width * local_width,
    )


def qkv_back_kernel(here, grad_ref, tokens_ref, weight_ref, back_ref, sum_ref, triple_ref, back):
    back[...] = dot_nt(grad_ref[...], weight_ref[...])
    totals = [jnp.zeros((TILE, back.shape[1]), jnp.float32)] * 2
    triple = jnp.zeros((TILE, grad_ref.shape[1]), jnp.float32)
    for lines in tiles_of(back.shape[0]):
        part = back[lines]
        back_ref[lines] = part.astype(back_ref.dtype)
        unit, _ = centred_rows(tokens_ref[0, lines].astype(jnp.float32))
        totals = [totals[0] + part * unit, totals[1] + part]
        triple = triple + grad_ref[lines].astype(jnp.float32)
    accumulate(sum_ref, totals)
    accumulate(triple_ref, [triple])


def qkv_backward(grad_triple, tokens, weight, here, index):
    local_len, triple_width = grad_triple.shape
    width = tokens.shape[2]
    whole = lambda shape: pl.BlockSpec(shape, lambda i, here: (0,) * len(shape))
    return kernel_call(
        qkv_back_kernel,
        [here],
        [grad_triple, tokens, weight],
        [
            pl.BlockSpec((ROWS, triple_width), lambda i, here: (i, 0)),
            pl.BlockSpec((1, ROWS, width), lambda i, here: (index, i, 0)),
            whole(weight.shape),
        ],
        [
            ((local_len, width), jnp.bfloat16),
            ((2, width), jnp.float32),
            ((1, triple_width), jnp.float32),
        ],
        [
            pl.BlockSpec((ROWS, width), lambda i, here: (i, 0)),
            whole((2, width)),
            whole((1, triple_width)),
        ],
        local_len // ROWS,
        "qkv_backward",
        [pltpu.VMEM((ROWS, width), jnp.float32)],
        flops=2 * local_len * width * triple_width,
    )


def norm_one_kernel(here, own_ref, tp_ref, tokens_ref, residual_ref, vector_ref, out_ref):
    for lines in tiles_of(own_ref.shape[0]):
        grads = own_ref[lines].astype(jnp.float32) + tp_ref[lines].astype(jnp.float32)
        unit, spread = centred_rows(tokens_ref[0, lines].astype(jnp.float32))
        out_ref[lines] = (
            residual_ref[lines].astype(jnp.float32)
            + through_norm(grads, unit, spread, vector_ref[3:4])
        ).astype(out_ref.dtype)


def norm_one_backward(own, tp, tokens, residual, vectors, here, index):
    local_len, width = own.shape
    row = pl.BlockSpec((ROWS, width), lambda i, here: (i, 0))
    return kernel_call(
        norm_one_kernel,
        [here],
        [own, tp, tokens, residual, vectors],
        [row, row, pl.BlockSpec((1, ROWS, width), lambda i, here: (index, i, 0)), row]
        + [pl.BlockSpec(vectors.shape, lambda i, here: (0, 0))],
        [((local_len, width), jnp.bfloat16)],
        [row],
        local_len // ROWS,
        "norm_one_backward",
    )[0]


CHUNK = 512


def gradient_kernel(plan, here, *refs):
    chips, groups = plan
    step = pl.program_id(0)
    refs = list(refs)
    turned = refs.pop()
    outs = [refs.pop(-2), refs.pop()]
    rows = outs[0].shape[2]
    at = 0
    for first, last, sequences in groups:
        lefts = refs[at : at + 2 * sequences * chips]
        rights = refs[at + 2 * sequences * chips : at + sequences * (2 * chips + 1)]
        at += sequences * (2 * chips + 1)

        @pl.when(step == first)
        def _():
            for index, left in enumerate(lefts):
                which, rest = divmod(index, sequences * chips)
                sequence, chip = divmod(rest, chips)
                block = left.shape[2]
                turned[which, sequence, chip * block : (chip + 1) * block] = left[0].T

        @pl.when((step >= first) & (step < last))
        def _():
            for which in range(2):
                total = dot_nn(turned[which, 0], rights[0][...])
                for sequence in range(1, sequences):
                    total += dot_nn(turned[which, sequence], rights[sequence][...])
                total = total.astype(jnp.bfloat16).reshape(chips, 2, rows, -1)
                for half in range(2):
                    outs[which][half] = total[:, half]


def gradient_plain(groups, here):
    chips = lax.axis_size("fsdp") // 2
    columns = []
    for lefts, rights in groups:
        total = 0.0
        for (array, lead), right in zip(lefts, rights):
            total = total + lax.dot_general(
                array[lead], right, (((0,), (0,)), ((), ())), preferred_element_type=jnp.float32
            )
        columns.append(total)
    whole = jnp.concatenate(columns, axis=1)
    whole = whole.astype(jnp.bfloat16).reshape(chips, 2, 2, -1, whole.shape[1])
    whole = whole.transpose(2, 1, 0, 3, 4)
    return pick(whole, 1 - here[1], 1), pick(whole, here[1], 1)


def gradient_blocks(groups, here, name):
    chips = lax.axis_size("fsdp") // 2
    if groups[0][0][0][0].shape[2] % (2 * chips * PAIR):
        return gradient_plain(groups, here)
    arrays, specs, plan = [], [], []
    at = 0
    for lefts, rights in groups:
        first, last = at, at + rights[0].shape[1] // CHUNK
        at = last
        plan.append((first, last, len(rights)))
        tokens = rights[0].shape[0]
        for own in (0, 1):
            for array, lead in lefts:
                block = array.shape[2] // (2 * chips)
                for chip in range(chips):
                    arrays.append(array)
                    specs.append(
                        pl.BlockSpec(
                            (1, tokens, block),
                            lambda i, here, lead=lead, chip=chip, own=own: (
                                lead,
                                0,
                                2 * chip + (here[1] if own else 1 - here[1]),
                            ),
                        )
                    )
        for right in rights:
            arrays.append(right)
            specs.append(
                pl.BlockSpec(
                    (tokens, CHUNK),
                    lambda i, here, first=first, last=last: (
                        0,
                        jnp.clip(i, first, last - 1) - first,
                    ),
                )
            )
    half = block // 2
    whole = pl.BlockSpec((2, chips, half, CHUNK), lambda i, here: (0, 0, 0, i))
    plan = (chips, plan)
    return kernel_call(
        lambda *refs: gradient_kernel(plan, *refs),
        [here],
        arrays,
        specs,
        [((2, chips, half, at * CHUNK), jnp.bfloat16)] * 2,
        [whole, whole],
        at,
        name,
        [pltpu.VMEM((2, len(groups[0][1]), chips * block, tokens), jnp.bfloat16)],
    )


def cross_ctx(sent, kept, gate, small=None):
    received = after(swap_core(sent), gate)
    halves = [None, None]
    side = lax.axis_index("ctx")
    for which in range(2):
        index = (which + side) % 2
        total = pick(kept, index, 0).astype(jnp.float32) + pick(received, index, 0).astype(
            jnp.float32
        )
        if small is not None:
            total = jnp.concatenate([total, jnp.where(index == 0, small, 0.0)], axis=1)
        halves[which] = total
    if lax.axis_size("ctx") != 2:
        low = jnp.where(side % 2 == 0, halves[0], halves[1])
        high = jnp.where(side % 2 == 0, halves[1], halves[0])
        return jnp.concatenate([low, high], axis=1), sent, None
    away = halves[1].astype(jnp.bfloat16)
    return halves[0], away, swap_ctx(away)


def cross_chips(crossing, gate):
    mine, _, coming = crossing
    if coming is not None:
        mine = mine + after(coming, gate).astype(jnp.float32)
    mine = mine.astype(jnp.bfloat16)
    return mine, exchange_chips(mine)


def spread_chips(parts):
    return jnp.sum(parts.astype(jnp.float32), axis=0).astype(jnp.bfloat16)


def spread_end(total, halves):
    if lax.axis_size("ctx") != 2:
        return lax.psum(total, "ctx").reshape(halves, -1, total.shape[1])
    other = swap_ctx(total)
    leading = lax.axis_index("ctx") == 0
    return jnp.stack([jnp.where(leading, total, other), jnp.where(leading, other, total)])


def other_ctx(rows, axis):
    if lax.axis_size("ctx") != 2:
        return lax.all_gather(rows, "ctx", axis=axis, tiled=True)
    return swap_ctx(rows)


def other_tokens(tokens, gate):
    seq_count = tokens.shape[0]
    if lax.axis_size("ctx") != 2 or lax.axis_size("tp") != 2 or seq_count % 2:
        return other_ctx(tokens, 1)
    side = lax.axis_index("tp")
    halves = tokens.reshape(2, seq_count // 2, *tokens.shape[1:])
    mine = after(swap_ctx(pick(halves, side, 0)), gate)
    theirs = swap_tp(mine)
    return jnp.concatenate(
        [jnp.where(side == 0, mine, theirs), jnp.where(side == 0, theirs, mine)]
    )


EXTRA = 16


def body(
    tokens,
    picture_starts,
    ln1_gain,
    ln1_shift,
    w_qkv,
    qv_bias,
    w_proj,
    proj_bias,
    ln2_gain,
    ln2_shift,
    w_fc1,
    fc1_bias,
    w_fc2,
    fc2_bias,
    out_grad,
):
    seq_count, local_len, width = tokens.shape
    fsdp = lax.axis_size("fsdp")
    chips = fsdp // 2
    ranks = lax.axis_size("ctx")
    rank = lax.axis_index("ctx")
    full_len = ranks * local_len
    local_width = w_qkv.shape[2]
    local_heads = local_width // HD
    units = w_fc1.shape[1]
    sequences = range(seq_count)
    spot = lax.axis_index("fsdp")
    side = lax.axis_index("tp")
    here = jnp.stack([spot // 2, spot % 2, rank, side]).astype(jnp.int32)
    place = jnp.stack([rank, jnp.int32(ranks)]).astype(jnp.int32)
    piece_ids = jnp.arange(full_len // PIECE, dtype=jnp.int32)
    pictures = jnp.any(
        piece_ids[None, :, None] == (picture_starts // PIECE)[:, None, :], axis=2
    ).astype(jnp.int32)

    block = ln1_gain.shape[0]
    qv_size, fc1_size = qv_bias.size, fc1_bias.size
    qv_lines = qv_size // block
    small = jnp.concatenate(
        [
            jnp.stack([ln1_gain, ln1_shift, proj_bias, ln2_gain, ln2_shift, fc2_bias]),
            qv_bias.reshape(-1, block),
            fc1_bias.reshape(-1, block),
        ]
    )
    small = jnp.pad(small, ((0, EXTRA - small.shape[0]), (0, 0)))
    qkv_bundle = gather_chips(halves_of(w_qkv.reshape(-1, 3 * local_width)))
    far_proj = swap_tp(w_proj)
    proj_halves = halves_of(
        jnp.concatenate(
            [jnp.where(side == 0, w_proj, far_proj), jnp.where(side == 0, far_proj, w_proj)]
        )
    )
    small = jnp.broadcast_to(small, (proj_halves.shape[0], *small.shape))
    proj_halves = jnp.concatenate([proj_halves, small], axis=1)
    proj_bundle = gather_chips(after(proj_halves, qkv_bundle))
    fc2_pieces = shift_chips(halves_of(w_fc2))
    fc1_bundle = gather_chips(after(halves_of(w_fc1), proj_bundle))
    far_tokens = other_tokens(tokens, proj_bundle)
    full_qkv = placed_rows(gather_rest(qkv_bundle), here, "place_qkv", 0)
    mine = swap_core(proj_bundle)

    first = jnp.where(spot % 2 == 0, proj_bundle, mine)[:, -EXTRA:]
    second = jnp.where(spot % 2 == 0, mine, proj_bundle)[:, -EXTRA:]
    smalls = jnp.stack([first, second], axis=1).reshape(fsdp, EXTRA, block).astype(jnp.float32)
    vectors = [smalls[:, i].reshape(-1) for i in range(6)]
    gain_one, shift_one, bias_proj, gain_two, shift_two, bias_fc2 = vectors
    qv_rows = smalls[:, 6 : 6 + qv_lines].reshape(fsdp, 2, local_heads, HD // fsdp)
    qv_rows = qv_rows.transpose(1, 2, 0, 3).reshape(2, local_width)
    bias_fc1 = smalls[:, 6 + qv_lines : 6 + qv_lines + fc1_size // block]
    bias_fc1 = bias_fc1.reshape(fsdp, units // HD, HD // fsdp).transpose(1, 0, 2).reshape(1, -1)
    bias_qkv = jnp.concatenate([qv_rows[0], jnp.zeros_like(qv_rows[0]), qv_rows[1]])
    lines = jnp.stack([bias_proj, gain_two, shift_two, gain_one])

    def project(rows):
        normed = layer_norm(rows.astype(jnp.float32), gain_one, shift_one).astype(jnp.bfloat16)
        result = jnp.einsum("sld,de->sle", normed, full_qkv, preferred_element_type=jnp.float32)
        return normed, (result + bias_qkv).astype(jnp.bfloat16)

    normed_one, triple = project(tokens)
    _, far_triple = project(far_tokens)
    proj_bundles = gather_rest(proj_bundle, triple, near=mine)
    fc2_bundle = jnp.stack(after(tuple(fc2_pieces), full_qkv))
    fc1_near = swap_core(fc1_bundle)
    attended, logs = [], []
    for index in sequences:
        gate = [attended[-1], fc1_near] if index else [fc2_bundle, proj_bundles[-1]]
        heads, log = attention_forward(triple, far_triple, after(place, *gate), pictures, index)
        attended.append(heads)
        logs.append(log)
    tp_attended = [after(swap_tp(heads), attended[-1]) for heads in attended]
    fc1_bundles = gather_rest(fc1_bundle, attended[-1], near=fc1_near)
    fc2_bundles = gather_rest(fc2_bundle, *tp_attended)
    all_attended = jnp.stack(attended)
    weights = [proj_bundles, fc1_bundles, fc2_bundles]
    if block % PAIR:
        order = lax.rem(here[0] + chips - jnp.arange(chips, dtype=jnp.int32), chips)
        weights = [
            [placed_columns_plain([b[:, :-EXTRA] for b in proj_bundles], here)],
            fc1_bundles,
            [placed_columns_plain([b[order] for b in fc2_bundles], here)],
        ]
    far_attended = other_ctx(after(all_attended, fc2_bundles[-1]), 1)
    far_logs = other_ctx(after(jnp.stack(logs), fc2_bundles[-1]), 3)
    residuals, normed_two, actives, hidden_grads, feeds, backs, swapped_twos = [], [], [], [], [], [], []
    hidden_sums = 0.0
    for index in sequences:
        gate = [backs[-1], far_attended, far_logs] if index else []
        residual, normed, active, hidden_grad, feed, back, hidden_sum, own_proj = feed_forward(
            attended[index],
            after(tp_attended[index], *backs[-1:]),
            tokens,
            out_grad,
            lines,
            bias_fc1,
            weights,
            after(here, *gate),
            index,
        )
        residuals.append(residual)
        normed_two.append(normed)
        actives.append(active)
        hidden_grads.append(hidden_grad)
        feeds.append(feed)
        backs.append(back)
        swapped_twos.append(swap_tp(back))
        hidden_sums = hidden_sums + hidden_sum[0]

    fc2_groups = [([(out_grad, s) for s in sequences], actives)]
    fc1_groups = [([(normed[None], 0) for normed in normed_two], hidden_grads)]
    branches, head_grads, far_head_grads = [], [], []
    two_sums = 0.0
    gate = backs[-1]
    for index in sequences:
        branch, head_grad, two_sum = norm_two_backward(
            backs[index],
            swapped_twos[index],
            residuals[index],
            out_grad,
            lines,
            own_proj,
            after(here, gate),
            index,
        )
        branches.append(branch)
        head_grads.append(head_grad)
        far_head_grads.append(other_ctx(head_grad, 0))
        two_sums = two_sums + two_sum
        if index == 0:
            blocks_fc2 = gradient_blocks(fc2_groups, after(here, head_grad), "grad_fc2")
            gate = blocks_fc2[1]
    cross_fc2 = cross_ctx(*blocks_fc2, head_grads[-1])
    fc1_groups.append(([(branch[None], 0) for branch in branches], attended))
    blocks_fc1 = gradient_blocks(fc1_groups, after(here, cross_fc2[1]), "grad_fc1_proj")

    grad_triples, back_ones, swapped_ones, outputs = [], [], [], []
    one_sums, triple_sums = 0.0, 0.0
    gate = (blocks_fc1[1],)
    for index in sequences:
        if index == 0:
            feed = after(feeds[0], *gate)
            swapped_feed = swap_tp(feed)
        grad_triple = attention_backward(
            (triple, attended[index], head_grads[index], logs[index]),
            (far_triple, far_attended[index], far_head_grads[index], far_logs[index]),
            after(place, *gate),
            pictures,
            index,
        )
        gate = (grad_triple,)
        if index == 0:
            gate, arrived_fc2 = cross_chips(cross_fc2, grad_triple)
            cross_fc1 = cross_ctx(*blocks_fc1, gate)
            gate = (cross_fc1[1],)
        grad_triples.append(grad_triple)
        if index == seq_count - 1:
            total_fc2 = spread_chips(after(arrived_fc2, grad_triple))
            part_fc1, arrived_fc1 = cross_chips(cross_fc1, total_fc2)
            last_groups = [([(normed_one, s) for s in sequences], grad_triples)]
            blocks_last = gradient_blocks(last_groups, after(here, part_fc1), "grad_last")
            gate = (blocks_last[1], *swapped_ones)
        back_one, one_sum, triple_sum = qkv_backward(
            grad_triple, tokens, full_qkv, after(here, *gate), index
        )
        gate = (back_one, swapped_feed)
        back_ones.append(back_one)
        swapped_ones.append(swap_tp(back_one))
        one_sums = one_sums + one_sum
        triple_sums = triple_sums + triple_sum[0]

    def finish_output(index, mine, theirs):
        total = mine.astype(jnp.float32) + theirs.astype(jnp.float32)
        outputs.append((residuals[index] + total + bias_fc2).astype(jnp.bfloat16))

    finish_output(0, feed, after(swapped_feed, back_ones[-1]))

    out_sums = jnp.sum(out_grad.astype(jnp.float32), axis=(0, 1))
    grad_qv = jnp.concatenate([triple_sums[:local_width], triple_sums[2 * local_width :]])
    vectors = [one_sums[0], one_sums[1], two_sums[2], two_sums[0], two_sums[1], out_sums]
    packed = jnp.concatenate(
        [vector.reshape(fsdp, block) for vector in vectors]
        + [
            grad_qv.reshape(2, local_heads, fsdp, HD // fsdp)
            .transpose(2, 0, 1, 3)
            .reshape(fsdp, -1),
            hidden_sums.reshape(-1, fsdp, HD // fsdp).transpose(1, 0, 2).reshape(fsdp, -1),
        ],
        axis=1,
    )
    last_width = 3 * local_width
    packed = jnp.pad(packed[:, None], ((0, 0), (0, EXTRA - 1), (0, last_width - packed.shape[1])))
    packed = packed.reshape(chips, 2, EXTRA, last_width).astype(jnp.bfloat16)
    core = spot % 2
    small = pick(packed, core, 1).astype(jnp.float32) + swap_core(
        pick(packed, 1 - core, 1)
    ).astype(jnp.float32)
    def norm_one(index, gate):
        return norm_one_backward(
            back_ones[index],
            swapped_ones[index],
            tokens,
            branches[index],
            lines,
            after(here, gate),
            index,
        )

    total_fc1 = spread_chips(after(arrived_fc1, back_ones[-1]))
    cross_last = cross_ctx(*blocks_last, back_ones[-1], small)
    grad_tokens = [norm_one(0, cross_last[1])]
    part_last, arrived_last = cross_chips(cross_last, grad_tokens[0])
    for index in range(1, seq_count):
        grad_tokens.append(norm_one(index, part_last))
    for index in range(1, seq_count):
        feed = after(feeds[index], part_last)
        finish_output(index, feed, swap_tp(feed))
    sums_fc2 = spread_end(after(total_fc2, part_last), 2)
    sums_fc1 = spread_end(after(total_fc1, part_last), 2)
    sums_last = spread_end(spread_chips(arrived_last), 2)
    small = sums_last[0, -EXTRA]
    norm_one = small[: 2 * block]
    norm_one = norm_one.astype(jnp.float32) + swap_tp(norm_one).astype(jnp.float32)
    small = small.astype(jnp.float32)
    vectors = [norm_one[:block], norm_one[block:]]
    vectors += [small[i * block : (i + 1) * block] for i in range(2, 6)]
    shard_qv = small[6 * block : 6 * block + qv_size].reshape(qv_bias.shape)
    shard_fc1_bias = small[6 * block + qv_size :][:fc1_size].reshape(fc1_bias.shape)
    sums_last = sums_last[:, : block // 2].reshape(block, -1).astype(jnp.float32)
    sums_fc1 = sums_fc1.reshape(block, -1).astype(jnp.float32)
    return (
        jnp.stack(outputs),
        jnp.stack(grad_tokens),
        vectors[0],
        vectors[1],
        sums_last.reshape(-1, 3, local_width),
        shard_qv,
        sums_fc1[:, units:].T,
        vectors[2],
        vectors[3],
        vectors[4],
        sums_fc1[:, :units],
        shard_fc1_bias,
        sums_fc2.reshape(block, -1).astype(jnp.float32).T,
        vectors[5],
    )


def solution(mesh):
    return jax.shard_map(
        body,
        mesh=mesh,
        in_specs=(
            P("fsdp", "ctx", None),
            P("fsdp", None),
            P("fsdp"),
            P("fsdp"),
            P("fsdp", None, "tp"),
            P(None, "tp", "fsdp"),
            P("tp", "fsdp"),
            P("fsdp"),
            P("fsdp"),
            P("fsdp"),
            P("fsdp", "tp"),
            P("tp", "fsdp"),
            P("tp", "fsdp"),
            P("fsdp"),
            P("fsdp", "ctx", None),
        ),
        out_specs=(
            P("fsdp", "ctx", None),
            P("fsdp", "ctx", None),
            P("fsdp"),
            P("fsdp"),
            P("fsdp", None, "tp"),
            P(None, "tp", "fsdp"),
            P("tp", "fsdp"),
            P("fsdp"),
            P("fsdp"),
            P("fsdp"),
            P("fsdp", "tp"),
            P("tp", "fsdp"),
            P("tp", "fsdp"),
            P("fsdp"),
        ),
        check_vma=False,
    )
```

```python
import jax
import jax.numpy as jnp
from jax import lax
from jax.experimental import pallas as pl
from jax.experimental.pallas import tpu as pltpu
from jax.sharding import PartitionSpec as P

HD = 64
PAIR = 2 * HD
PIECE = 256
SCALE = HD ** (-0.5)
KERNEL_VMEM = 56 * 1024 * 1024

epsilon = 1e-05
masked_value = -1e30


def layer_norm(values, gain_vec, shift_vec):
    average = jnp.mean(values, axis=-1, keepdims=True)
    centred = values - average
    variance = jnp.mean(centred * centred, axis=-1, keepdims=True)
    return centred * lax.rsqrt(variance + epsilon) * gain_vec + shift_vec


NT = (((1,), (1,)), ((), ()))


def dot_nt(left, right):
    return lax.dot_general(left, right, NT, preferred_element_type=jnp.float32)


def dot_nn(left, right):
    return jnp.dot(left, right, preferred_element_type=jnp.float32)


def head_lanes(head):
    lanes = lax.broadcasted_iota(jnp.int32, (1, PAIR), 1)
    return (lanes >= head * HD) & (lanes < (head + 1) * HD)


def only_head(rows, head):
    return jnp.where(head_lanes(head), rows, jnp.zeros_like(rows))


def diagonal_mask(scores, joined):
    key_row = lax.broadcasted_iota(jnp.int32, scores.shape, 0)
    query_lane = lax.broadcasted_iota(jnp.int32, scores.shape, 1)
    return (key_row <= query_lane) | joined


def chunk_start(step, place, local_len, chunks):
    return 0 if chunks == 1 else pl.multiple_of(step * local_len, local_len)


SCORE_TILE = 32


def score_tiles(count):
    return [slice(start, start + SCORE_TILE) for start in range(0, count, SCORE_TILE)]


def folded(rows, combine):
    parts = [rows[start : start + 8] for start in range(0, rows.shape[0], 8)]
    while len(parts) > 1:
        parts = [
            combine(parts[i], parts[i + 1]) if i + 1 < len(parts) else parts[i]
            for i in range(0, len(parts), 2)
        ]
    return parts[0]


def attention_forward_kernel(
    place, pictures, q_ref, k_ref, v_ref, k_far, v_far, out_ref, log_ref, scores, weights, values
):
    rank = place[0]
    sequence = place[2]
    local_len = q_ref.shape[1]
    blocks = local_len // PIECE
    chunks = k_far.shape[1] // local_len
    values[...] = v_ref[0].T
    states = [(head, block) for head in range(2) for block in range(blocks)]
    scaled, peaks = [], []
    for index, (head, block) in enumerate(states):
        query = only_head(q_ref[0, block * PIECE : (block + 1) * PIECE, :] * SCALE, head)
        scaled.append(query)
        joined = pictures[sequence, rank * blocks + block] > 0
        count = (block + 1) * PIECE
        scores[index, :count] = dot_nt(k_ref[0, :count], query)
        peak = jnp.full((8, PIECE), masked_value, jnp.float32)
        for tile in score_tiles(count):
            part = scores[index, tile]
            if tile.start >= block * PIECE:
                key_row = lax.broadcasted_iota(jnp.int32, part.shape, 0) + (
                    tile.start - block * PIECE
                )
                lane = lax.broadcasted_iota(jnp.int32, part.shape, 1)
                part = jnp.where((key_row <= lane) | joined, part, masked_value)
                scores[index, tile] = part
            peak = jnp.maximum(peak, folded(part, jnp.maximum))
        peaks.append(peak)

    def far_scores(step, carried):
        keys = k_far[0, pl.ds(chunk_start(step, place, local_len, chunks), local_len), :]
        base = pl.multiple_of((step + 1) * local_len, local_len)
        after = []
        for index, peak in enumerate(carried):
            part = dot_nt(keys, scaled[index])
            scores[index, pl.ds(base, local_len)] = part
            for tile in score_tiles(local_len):
                peak = jnp.maximum(peak, folded(part[tile], jnp.maximum))
            after.append(peak)
        return after

    peaks = lax.fori_loop(0, rank, far_scores, peaks)
    peaks = [jnp.max(peak, axis=0, keepdims=True) for peak in peaks]
    gathered = []
    for index, (head, block) in enumerate(states):
        count = (block + 1) * PIECE
        total = jnp.zeros((8, PIECE), jnp.float32)
        for tile in score_tiles(count):
            weight = jnp.exp(scores[index, tile] - peaks[index])
            total = total + folded(weight, jnp.add)
            weights[index, tile] = weight.astype(jnp.bfloat16)
        gathered.append(
            (total, dot_nn(values[head * HD : (head + 1) * HD, :count], weights[index, :count]))
        )

    def far_values(step, carried):
        base = pl.multiple_of((step + 1) * local_len, local_len)
        far = v_far[0, pl.ds(chunk_start(step, place, local_len, chunks), local_len), :].T
        after = []
        for index, (total, sums) in enumerate(carried):
            head = states[index][0]
            for tile in score_tiles(local_len):
                weight = jnp.exp(
                    scores[index, pl.ds(base + tile.start, SCORE_TILE)] - peaks[index]
                )
                total = total + folded(weight, jnp.add)
                weights[index, tile] = weight.astype(jnp.bfloat16)
            sums = sums + dot_nn(far[head * HD : (head + 1) * HD], weights[index])
            after.append((total, sums))
        return after

    gathered = lax.fori_loop(0, rank, far_values, gathered)
    for block in range(blocks):
        rows = slice(block * PIECE, (block + 1) * PIECE)
        halves = []
        for head in range(2):
            index = head * blocks + block
            total = jnp.sum(gathered[index][0], axis=0, keepdims=True)
            halves.append(gathered[index][1] / total)
            log_ref[0, head : head + 1, rows] = peaks[index] + jnp.log(total)
        out_ref[rows, :] = jnp.concatenate(halves, axis=0).T.astype(out_ref.dtype)


def attention_forward(triple, far, place, pictures, index):
    place = jnp.concatenate([place, jnp.full((1,), index, jnp.int32)])
    _, local_len, triple_width = triple.shape
    far_len = far.shape[1]
    local_width = triple_width // 3
    pairs = local_width // PAIR

    def part(length, offset):
        return pl.BlockSpec(
            (1, length, PAIR), lambda p, place, pics: (index, 0, offset * pairs + p)
        )

    return pl.pallas_call(
        attention_forward_kernel,
        grid_spec=pltpu.PrefetchScalarGridSpec(
            num_scalar_prefetch=2,
            grid=(pairs,),
            in_specs=[
                part(local_len, 0),
                part(local_len, 1),
                part(local_len, 2),
                part(far_len, 1),
                part(far_len, 2),
            ],
            out_specs=[
                pl.BlockSpec((local_len, PAIR), lambda p, place, pics: (0, p)),
                pl.BlockSpec((1, 2, local_len), lambda p, place, pics: (p, 0, 0)),
            ],
            scratch_shapes=[
                pltpu.VMEM((2 * local_len // PIECE, local_len + far_len, PIECE), jnp.float32),
                pltpu.VMEM((2 * local_len // PIECE, local_len, PIECE), jnp.bfloat16),
                pltpu.VMEM((PAIR, local_len), jnp.bfloat16),
            ],
        ),
        out_shape=[
            jax.ShapeDtypeStruct((local_len, local_width), jnp.bfloat16),
            jax.ShapeDtypeStruct((pairs, 2, local_len), jnp.float32),
        ],
        compiler_params=pltpu.CompilerParams(vmem_limit_bytes=KERNEL_VMEM),
        cost_estimate=pl.CostEstimate(flops=50000000000, bytes_accessed=0, transcendentals=0),
        name="attention_forward",
    )(place, pictures, triple, triple, triple, far, far)


def attention_backward_kernel(
    place,
    pictures,
    q_ref,
    k_ref,
    v_ref,
    out_ref,
    grad_ref,
    log_ref,
    q_far,
    k_far,
    v_far,
    out_far,
    grad_far,
    log_far,
    triple_ref,
):
    rank = place[0]
    ranks = place[1]
    sequence = place[2]
    pair = pl.program_id(0)
    local_len = triple_ref.shape[0]
    local_width = triple_ref.shape[1] // 3
    blocks = local_len // PIECE
    chunks = k_far.shape[1] // local_len

    def sides_of(queries, grads, outs, logs):
        turned = (grads.astype(jnp.float32) * outs.astype(jnp.float32)).T
        queries = queries * SCALE
        sides = []
        for head in range(2):
            delta = jnp.sum(turned[head * HD : (head + 1) * HD], axis=0, keepdims=True)
            sides.append(
                (
                    only_head(queries, head),
                    only_head(grads, head),
                    logs[head : head + 1],
                    delta,
                )
            )
        return sides

    def pieces(keys, values, query, grad, log, delta, mask=None):
        scores = dot_nt(keys, query)
        probs = jnp.exp(scores - log)
        if mask is not None:
            probs = jnp.where(mask(probs), probs, 0.0)
        grad_probs = dot_nt(values, grad)
        return probs, (probs * (grad_probs - delta)).astype(jnp.bfloat16)

    key_own = k_ref[0]
    value_own = v_ref[0]
    key_turned = key_own.T
    sides = sides_of(q_ref[0], grad_ref[...], out_ref[...], log_ref[0])
    grad_keys = [None] * blocks
    grad_values = [None] * blocks
    grad_queries = []

    def add(total, part):
        return part if total is None else total + part

    for head in range(2):
        queries, grads, logs, deltas = sides[head]
        for block in range(blocks):
            rows = slice(block * PIECE, (block + 1) * PIECE)
            joined = pictures[sequence, rank * blocks + block] > 0
            grad_query = None
            for key_block in range(block + 1):
                key_rows = slice(key_block * PIECE, (key_block + 1) * PIECE)
                mask = (lambda p, j=joined: diagonal_mask(p, j)) if key_block == block else None
                probs, grad_scores = pieces(
                    key_own[key_rows],
                    value_own[key_rows],
                    queries[rows],
                    grads[rows],
                    logs[:, rows],
                    deltas[:, rows],
                    mask,
                )
                grad_values[key_block] = add(
                    grad_values[key_block], dot_nn(probs.astype(jnp.bfloat16), grads[rows])
                )
                grad_keys[key_block] = add(
                    grad_keys[key_block], dot_nn(grad_scores, queries[rows])
                )
                grad_query = add(
                    grad_query,
                    dot_nn(key_turned[head * HD : (head + 1) * HD, key_rows], grad_scores),
                )
            grad_queries.append(grad_query)

    def earlier(step, carried):
        start = chunk_start(step, place, local_len, chunks)
        keys = k_far[0, pl.ds(start, local_len), :]
        values = v_far[0, pl.ds(start, local_len), :]
        turned = keys.T
        after = []
        for index, total in enumerate(carried):
            head, block = index // blocks, index % blocks
            rows = slice(block * PIECE, (block + 1) * PIECE)
            queries, grads, logs, deltas = sides[head]
            _, grad_scores = pieces(
                keys, values, queries[rows], grads[rows], logs[:, rows], deltas[:, rows]
            )
            after.append(total + dot_nn(turned[head * HD : (head + 1) * HD], grad_scores))
        return after

    grad_queries = lax.fori_loop(0, rank, earlier, grad_queries)
    for block in range(blocks):
        rows = slice(block * PIECE, (block + 1) * PIECE)
        both = jnp.concatenate([grad_queries[head * blocks + block] for head in range(2)], axis=0)
        triple_ref[rows, pl.ds(pl.multiple_of(pair * PAIR, PAIR), PAIR)] = (
            (both * SCALE).T.astype(triple_ref.dtype)
        )

    def later(step, carried):
        start = chunk_start(step, place, local_len, chunks)
        window = pl.ds(start, local_len)
        sides = sides_of(
            q_far[0, window, :], grad_far[window, :], out_far[window, :], log_far[0, :, window]
        )
        keys_after, values_after = list(carried[0]), list(carried[1])
        for head in range(2):
            queries, grads, logs, deltas = sides[head]
            for block in range(blocks):
                rows = slice(block * PIECE, (block + 1) * PIECE)
                probs, grad_scores = pieces(
                    key_own[rows], value_own[rows], queries, grads, logs, deltas
                )
                values_after[block] = values_after[block] + dot_nn(
                    probs.astype(jnp.bfloat16), grads
                )
                keys_after[block] = keys_after[block] + dot_nn(grad_scores, queries)
        return keys_after, values_after

    grad_keys, grad_values = lax.fori_loop(rank + 1, ranks, later, (grad_keys, grad_values))
    for block in range(blocks):
        rows = slice(block * PIECE, (block + 1) * PIECE)
        for part, grads in ((1, grad_keys), (2, grad_values)):
            column = pl.multiple_of(part * local_width + pair * PAIR, PAIR)
            triple_ref[rows, pl.ds(column, PAIR)] = grads[block].astype(triple_ref.dtype)


def attention_backward(own, other, place, pictures, index):
    place = jnp.concatenate([place, jnp.full((1,), index, jnp.int32)])
    _, local_len, triple_width = own[0].shape
    pairs = triple_width // (3 * PAIR)
    specs = []
    for length in (local_len, other[0].shape[1]):
        for offset in range(3):
            specs.append(
                pl.BlockSpec(
                    (1, length, PAIR),
                    lambda p, place, pics, offset=offset: (index, 0, offset * pairs + p),
                )
            )
        specs += [pl.BlockSpec((length, PAIR), lambda p, place, pics: (0, p))] * 2
        specs.append(pl.BlockSpec((1, 2, length), lambda p, place, pics: (p, 0, 0)))
    return pl.pallas_call(
        attention_backward_kernel,
        grid_spec=pltpu.PrefetchScalarGridSpec(
            num_scalar_prefetch=2,
            grid=(pairs,),
            in_specs=specs,
            out_specs=pl.BlockSpec((local_len, triple_width), lambda p, place, pics: (0, 0)),
        ),
        out_shape=jax.ShapeDtypeStruct((local_len, triple_width), jnp.bfloat16),
        compiler_params=pltpu.CompilerParams(vmem_limit_bytes=KERNEL_VMEM),
        cost_estimate=pl.CostEstimate(flops=50000000000, bytes_accessed=0, transcendentals=0),
        name="attention_backward",
    )(place, pictures, *([own[0]] * 3), *own[1:], *([other[0]] * 3), *other[1:])


def core_swap():
    return [(place, place ^ 1) for place in range(lax.axis_size("fsdp"))]


PAIR_SWAP = [(0, 1), (1, 0)]


def swap_core(rows):
    return lax.ppermute(rows, "fsdp", core_swap())


def swap_ctx(rows):
    return lax.ppermute(rows, "ctx", PAIR_SWAP)


def swap_tp(rows):
    return lax.ppermute(rows, "tp", PAIR_SWAP)


def exchange_chips(rows):
    fsdp = lax.axis_size("fsdp")
    groups = [list(range(core, fsdp, 2)) for core in range(2)]
    return lax.all_to_all(
        rows, "fsdp", split_axis=0, concat_axis=0, tiled=True, axis_index_groups=groups
    )


def pick(array, index, axis):
    return lax.dynamic_index_in_dim(array, index, axis, keepdims=False)


def after(value, *others):
    return lax.optimization_barrier((value, *others))[0]


def halves_of(shard):
    halves = 2 if lax.axis_size("ctx") == 2 else 1
    return shard.reshape(halves, -1, shard.shape[1])


def gather_chips(halves):
    chips = lax.axis_size("fsdp") // 2
    part = pick(halves, lax.axis_index("ctx"), 0) if halves.shape[0] == 2 else halves[0]
    return exchange_chips(jnp.broadcast_to(part, (chips, *part.shape)))


def chip_shift(step):
    chips = lax.axis_size("fsdp") // 2
    return [
        (2 * chip + core, 2 * ((chip + step) % chips) + core)
        for chip in range(chips)
        for core in range(2)
    ]


def shift_chips(halves):
    part = pick(halves, lax.axis_index("ctx"), 0) if halves.shape[0] == 2 else halves[0]
    chips = lax.axis_size("fsdp") // 2
    return [part] + [lax.ppermute(part, "fsdp", chip_shift(step)) for step in range(1, chips)]


def gather_rest(bundle, *gate, near=None):
    bundles = [bundle, swap_core(bundle) if near is None else near]
    if lax.axis_size("ctx") == 2:
        across = after(swap_ctx(bundle), *gate)
        bundles += [across, swap_core(across)]
    return bundles


def kernel_call(kernel, scalars, arrays, in_specs, outs, out_specs, grid, name, scratch=(), flops=0):
    size = sum(array.size for array in arrays)
    return pl.pallas_call(
        kernel,
        grid_spec=pltpu.PrefetchScalarGridSpec(
            num_scalar_prefetch=len(scalars),
            grid=(grid,),
            in_specs=in_specs,
            out_specs=out_specs,
            scratch_shapes=list(scratch),
        ),
        out_shape=[jax.ShapeDtypeStruct(shape, dtype) for shape, dtype in outs],
        compiler_params=pltpu.CompilerParams(vmem_limit_bytes=KERNEL_VMEM),
        cost_estimate=pl.CostEstimate(flops=50000000000, bytes_accessed=0, transcendentals=0),
        name=name,
    )(*scalars, *arrays)


def owners(here, sides):
    for index in range(2 * sides):
        core = here[1] if index % 2 == 0 else 1 - here[1]
        yield core, ((here[2] if index < 2 else 1 - here[2]) if sides == 2 else 0)


def placed_rows(bundles, here, name, extra):
    fsdp = lax.axis_size("fsdp")
    sides = len(bundles) // 2
    chips, total, width = bundles[0].shape
    height = total - extra
    chunk = 512

    def kernel(here, *refs):
        for index, (core, side) in enumerate(owners(here, sides)):
            for chip in range(chips):
                refs[-1][(2 * chip + core) * sides + side] = refs[index][chip, :height]

    (result,) = kernel_call(
        kernel,
        [here],
        bundles,
        [pl.BlockSpec((chips, total, chunk), lambda i, here: (0, 0, i))] * (2 * sides),
        [((fsdp * sides, height, width), jnp.bfloat16)],
        [pl.BlockSpec((fsdp * sides, height, chunk), lambda i, here: (0, 0, i))],
        width // chunk,
        name,
    )
    return result.reshape(-1, width)


def placed_columns_plain(bundles, here):
    sides = []
    for mine, other in zip(bundles[::2], bundles[1::2]):
        first = jnp.where(here[1] == 0, mine, other)
        second = jnp.where(here[1] == 0, other, mine)
        both = jnp.stack([first, second], axis=1)
        sides.append(both.reshape(-1, *both.shape[2:]))
    if len(sides) == 2:
        sides = [
            jnp.where(here[2] == 0, sides[0], sides[1]),
            jnp.where(here[2] == 0, sides[1], sides[0]),
        ]
    fsdp, _, width = sides[0].shape
    return jnp.concatenate(sides, axis=1).transpose(1, 0, 2).reshape(-1, fsdp * width)


def weight_copies(bundles, target, here, columns, shifted=False):
    if len(bundles) == 1:
        yield bundles[0], target
        return
    sides = len(bundles) // 2
    for index, (core, side) in enumerate(owners(here, sides)):
        chips, _, width = bundles[index].shape
        height = target.shape[0] // (sides if columns else 2 * chips * sides)
        for chip in range(chips):
            source = bundles[index].at[chip, pl.ds(0, height)]
            block = 2 * (lax.rem(here[0] + chips - chip, chips) if shifted else chip) + core
            if columns:
                across = pl.ds(pl.multiple_of(block * width, width), width)
                yield source, target.at[pl.ds(pl.multiple_of(side * height, height), height), across]
            else:
                row = pl.multiple_of((block * sides + side) * height, height)
                yield source, target.at[pl.ds(row, height)]


UNITS = 1024
TILE = 16
ROOT = 0.7978845608028654
CUBIC = 0.044715


def feed_kernel(counts, here, *refs):
    own_ref, tp_ref, tokens_ref, grad_ref, vector_ref, bias_ref = refs[:6]
    at = 6
    bundles = []
    for count in counts:
        bundles.append(refs[at : at + count])
        at += count
    residual_ref, normed_ref, active_ref, hidden_ref, feed_ref, back_ref, sum_ref, proj_ref = refs[
        at : at + 8
    ]
    proj, first, second, feed, back, hidden_pre, grad_active, semaphores = refs[at + 8 :]
    step = pl.program_id(0)
    copies = [
        weight_copies(bundles[0], proj, here, True),
        weight_copies(bundles[1], first, here, False),
        weight_copies(bundles[2], second, here, True, True),
    ]
    made, number = [], 0
    for group in copies:
        made.append([])
        for source, place in group:
            made[-1].append(pltpu.make_async_copy(source, place, semaphores.at[number]))
            number += 1
    rows = proj.shape[0] // 2
    kept = pltpu.make_async_copy(
        proj.at[pl.ds(pl.multiple_of(here[3] * rows, rows), rows)],
        proj_ref,
        semaphores.at[number],
    )

    @pl.when(step == 0)
    def _():
        for group in made:
            for copy in group:
                copy.start()
        for copy in made[0]:
            copy.wait()
        kept.start()
        leading = here[3] == 0
        low = jnp.where(leading, own_ref[...], tp_ref[...])
        high = jnp.where(leading, tp_ref[...], own_ref[...])
        feed[...] = dot_nn(low, proj[:rows]) + dot_nn(high, proj[rows:])
        for start in range(0, feed.shape[0], TILE):
            lines = slice(start, start + TILE)
            residual = tokens_ref[0, lines].astype(jnp.float32) + feed[lines] + vector_ref[0:1]
            residual_ref[lines] = residual
            unit, _ = centred_rows(residual)
            normed_ref[lines] = (unit * vector_ref[1:2] + vector_ref[2:3]).astype(
                normed_ref.dtype
            )
        for copy in made[1]:
            copy.wait()

    units = pl.ds(pl.multiple_of(step * UNITS, UNITS), UNITS)
    hidden_pre[...] = dot_nn(normed_ref[...], first[:, units])

    @pl.when(step == 0)
    def _():
        for copy in made[2]:
            copy.wait()
        kept.wait()

    grad_active[...] = dot_nt(grad_ref[0], second[units])
    totals = jnp.zeros((TILE, UNITS), jnp.float32)
    for start in range(0, feed.shape[0], TILE):
        lines = slice(start, start + TILE)
        hidden = hidden_pre[lines] + bias_ref[...]
        square = hidden * hidden
        bent = jnp.tanh(hidden * (ROOT + ROOT * CUBIC * square))
        share = 0.5 + 0.5 * bent
        active_ref[lines] = (hidden * share).astype(jnp.bfloat16)
        slope = share + hidden * (1.0 - bent * bent) * (
            0.5 * ROOT + 1.5 * ROOT * CUBIC * square
        )
        grad_hidden = (grad_active[lines] * slope).astype(jnp.bfloat16)
        hidden_ref[lines] = grad_hidden
        totals = totals + grad_hidden.astype(jnp.float32)
    sum_ref[...] = jnp.sum(totals, axis=0, keepdims=True)
    active = active_ref[...]
    feed_part = dot_nn(active, second[units])
    back_part = dot_nt(hidden_ref[...], first[:, units])

    @pl.when(step == 0)
    def _():
        feed[...] = feed_part
        back[...] = back_part

    @pl.when(step > 0)
    def _():
        feed[...] += feed_part
        back[...] += back_part

    @pl.when(step == pl.num_programs(0) - 1)
    def _():
        feed_ref[...] = feed[...].astype(feed_ref.dtype)
        back_ref[...] = back[...].astype(back_ref.dtype)


def feed_forward(own, tp, tokens, out_grad, vectors, bias, weights, here, index):
    local_len, local_width = own.shape
    width = tokens.shape[2]
    units = bias.shape[1]
    counts = tuple(len(group) for group in weights)
    copies = sum(1 if len(group) == 1 else len(group) * group[0].shape[0] for group in weights)
    whole = lambda shape: pl.BlockSpec(shape, lambda j, here: (0,) * len(shape))
    row = pl.BlockSpec((1, local_len, width), lambda j, here: (index, 0, 0))
    block = pl.BlockSpec((local_len, UNITS), lambda j, here: (0, j))
    line = pl.BlockSpec((1, UNITS), lambda j, here: (0, j))
    flat = [array for group in weights for array in group]
    half, full = jnp.bfloat16, jnp.float32
    return kernel_call(
        lambda *refs: feed_kernel(counts, *refs),
        [here],
        [own, tp, tokens, out_grad, vectors, bias] + flat,
        [whole(own.shape), whole(own.shape), row, row, whole(vectors.shape), line]
        + [pl.BlockSpec(memory_space=pl.ANY)] * len(flat),
        [
            ((local_len, width), full),
            ((local_len, width), half),
            ((local_len, units), half),
            ((local_len, units), half),
            ((local_len, width), half),
            ((local_len, width), half),
            ((1, units), full),
            ((local_width, width), half),
        ],
        [whole((local_len, width)), whole((local_len, width)), block, block]
        + [whole((local_len, width)), whole((local_len, width)), line]
        + [pl.BlockSpec(memory_space=pl.ANY)],
        units // UNITS,
        "feed_forward",
        [
            pltpu.VMEM((2 * local_width, width), half),
            pltpu.VMEM((width, units), half),
            pltpu.VMEM((units, width), half),
            pltpu.VMEM((local_len, width), full),
            pltpu.VMEM((local_len, width), full),
            pltpu.VMEM((local_len, UNITS), full),
            pltpu.VMEM((local_len, UNITS), full),
            pltpu.SemaphoreType.DMA((copies + 1,)),
        ],
        flops=8 * local_len * width * units,
    )


ROWS = 256


def centred_rows(rows):
    average = jnp.mean(rows, axis=-1, keepdims=True)
    centred = rows - average
    spread = lax.rsqrt(jnp.mean(centred * centred, axis=-1, keepdims=True) + epsilon)
    return centred * spread, spread


def through_norm(grads, unit, spread, gain):
    scaled = grads * gain
    return spread * (
        scaled
        - jnp.mean(scaled, axis=-1, keepdims=True)
        - unit * jnp.mean(scaled * unit, axis=-1, keepdims=True)
    )


def accumulate(ref, totals):
    total = jnp.concatenate([jnp.sum(lines, axis=0, keepdims=True) for lines in totals])

    @pl.when(pl.program_id(0) == 0)
    def _():
        ref[...] = total

    @pl.when(pl.program_id(0) > 0)
    def _():
        ref[...] += total


def tiles_of(count):
    return [slice(start, start + TILE) for start in range(0, count, TILE)]


def norm_two_kernel(
    here, own_ref, tp_ref, residual_ref, grad_ref, vector_ref, proj_ref, branch_ref, heads_ref, sum_ref
):
    totals = [jnp.zeros((TILE, own_ref.shape[1]), jnp.float32)] * 3
    for lines in tiles_of(own_ref.shape[0]):
        grads = own_ref[lines].astype(jnp.float32) + tp_ref[lines].astype(jnp.float32)
        unit, spread = centred_rows(residual_ref[lines])
        total = grad_ref[0, lines].astype(jnp.float32) + through_norm(
            grads, unit, spread, vector_ref[1:2]
        )
        branch = total.astype(jnp.bfloat16)
        branch_ref[lines] = branch
        totals = [
            totals[0] + grads * unit,
            totals[1] + grads,
            totals[2] + branch.astype(jnp.float32),
        ]
    heads_ref[...] = dot_nt(branch_ref[...], proj_ref[...]).astype(heads_ref.dtype)
    accumulate(sum_ref, totals)


def norm_two_backward(own, tp, residual, out_grad, vectors, proj, here, index):
    local_len, width = own.shape
    local_width = proj.shape[0]
    whole = lambda shape: pl.BlockSpec(shape, lambda i, here: (0,) * len(shape))
    row = pl.BlockSpec((ROWS, width), lambda i, here: (i, 0))
    return kernel_call(
        norm_two_kernel,
        [here],
        [own, tp, residual, out_grad, vectors, proj],
        [row, row, row, pl.BlockSpec((1, ROWS, width), lambda i, here: (index, i, 0))]
        + [whole(vectors.shape), whole(proj.shape)],
        [
            ((local_len, width), jnp.bfloat16),
            ((local_len, local_width), jnp.bfloat16),
            ((3, width), jnp.float32),
        ],
        [row, pl.BlockSpec((ROWS, local_width), lambda i, here: (i, 0)), whole((3, width))],
        local_len // ROWS,
        "norm_two_backward",
        flops=2 * local_len * width * local_width,
    )


def qkv_back_kernel(here, grad_ref, tokens_ref, weight_ref, back_ref, sum_ref, triple_ref, back):
    back[...] = dot_nt(grad_ref[...], weight_ref[...])
    totals = [jnp.zeros((TILE, back.shape[1]), jnp.float32)] * 2
    triple = jnp.zeros((TILE, grad_ref.shape[1]), jnp.float32)
    for lines in tiles_of(back.shape[0]):
        part = back[lines]
        back_ref[lines] = part.astype(back_ref.dtype)
        unit, _ = centred_rows(tokens_ref[0, lines].astype(jnp.float32))
        totals = [totals[0] + part * unit, totals[1] + part]
        triple = triple + grad_ref[lines].astype(jnp.float32)
    accumulate(sum_ref, totals)
    accumulate(triple_ref, [triple])


def qkv_backward(grad_triple, tokens, weight, here, index):
    local_len, triple_width = grad_triple.shape
    width = tokens.shape[2]
    whole = lambda shape: pl.BlockSpec(shape, lambda i, here: (0,) * len(shape))
    return kernel_call(
        qkv_back_kernel,
        [here],
        [grad_triple, tokens, weight],
        [
            pl.BlockSpec((ROWS, triple_width), lambda i, here: (i, 0)),
            pl.BlockSpec((1, ROWS, width), lambda i, here: (index, i, 0)),
            whole(weight.shape),
        ],
        [
            ((local_len, width), jnp.bfloat16),
            ((2, width), jnp.float32),
            ((1, triple_width), jnp.float32),
        ],
        [
            pl.BlockSpec((ROWS, width), lambda i, here: (i, 0)),
            whole((2, width)),
            whole((1, triple_width)),
        ],
        local_len // ROWS,
        "qkv_backward",
        [pltpu.VMEM((ROWS, width), jnp.float32)],
        flops=2 * local_len * width * triple_width,
    )


def norm_one_kernel(here, own_ref, tp_ref, tokens_ref, residual_ref, vector_ref, out_ref):
    for lines in tiles_of(own_ref.shape[0]):
        grads = own_ref[lines].astype(jnp.float32) + tp_ref[lines].astype(jnp.float32)
        unit, spread = centred_rows(tokens_ref[0, lines].astype(jnp.float32))
        out_ref[lines] = (
            residual_ref[lines].astype(jnp.float32)
            + through_norm(grads, unit, spread, vector_ref[3:4])
        ).astype(out_ref.dtype)


def norm_one_backward(own, tp, tokens, residual, vectors, here, index):
    local_len, width = own.shape
    row = pl.BlockSpec((ROWS, width), lambda i, here: (i, 0))
    return kernel_call(
        norm_one_kernel,
        [here],
        [own, tp, tokens, residual, vectors],
        [row, row, pl.BlockSpec((1, ROWS, width), lambda i, here: (index, i, 0)), row]
        + [pl.BlockSpec(vectors.shape, lambda i, here: (0, 0))],
        [((local_len, width), jnp.bfloat16)],
        [row],
        local_len // ROWS,
        "norm_one_backward",
    )[0]


CHUNK = 512


def gradient_kernel(plan, here, *refs):
    chips, groups = plan
    step = pl.program_id(0)
    refs = list(refs)
    turned = refs.pop()
    outs = [refs.pop(-2), refs.pop()]
    rows = outs[0].shape[2]
    at = 0
    for first, last, sequences in groups:
        lefts = refs[at : at + 2 * sequences * chips]
        rights = refs[at + 2 * sequences * chips : at + sequences * (2 * chips + 1)]
        at += sequences * (2 * chips + 1)

        @pl.when(step == first)
        def _():
            for index, left in enumerate(lefts):
                which, rest = divmod(index, sequences * chips)
                sequence, chip = divmod(rest, chips)
                block = left.shape[2]
                turned[which, sequence, chip * block : (chip + 1) * block] = left[0].T

        @pl.when((step >= first) & (step < last))
        def _():
            for which in range(2):
                total = dot_nn(turned[which, 0], rights[0][...])
                for sequence in range(1, sequences):
                    total += dot_nn(turned[which, sequence], rights[sequence][...])
                total = total.astype(jnp.bfloat16).reshape(chips, 2, rows, -1)
                for half in range(2):
                    outs[which][half] = total[:, half]


def gradient_plain(groups, here):
    chips = lax.axis_size("fsdp") // 2
    columns = []
    for lefts, rights in groups:
        total = 0.0
        for (array, lead), right in zip(lefts, rights):
            total = total + lax.dot_general(
                array[lead], right, (((0,), (0,)), ((), ())), preferred_element_type=jnp.float32
            )
        columns.append(total)
    whole = jnp.concatenate(columns, axis=1)
    whole = whole.astype(jnp.bfloat16).reshape(chips, 2, 2, -1, whole.shape[1])
    whole = whole.transpose(2, 1, 0, 3, 4)
    return pick(whole, 1 - here[1], 1), pick(whole, here[1], 1)


def gradient_blocks(groups, here, name):
    chips = lax.axis_size("fsdp") // 2
    if groups[0][0][0][0].shape[2] % (2 * chips * PAIR):
        return gradient_plain(groups, here)
    arrays, specs, plan = [], [], []
    at = 0
    for lefts, rights in groups:
        first, last = at, at + rights[0].shape[1] // CHUNK
        at = last
        plan.append((first, last, len(rights)))
        tokens = rights[0].shape[0]
        for own in (0, 1):
            for array, lead in lefts:
                block = array.shape[2] // (2 * chips)
                for chip in range(chips):
                    arrays.append(array)
                    specs.append(
                        pl.BlockSpec(
                            (1, tokens, block),
                            lambda i, here, lead=lead, chip=chip, own=own: (
                                lead,
                                0,
                                2 * chip + (here[1] if own else 1 - here[1]),
                            ),
                        )
                    )
        for right in rights:
            arrays.append(right)
            specs.append(
                pl.BlockSpec(
                    (tokens, CHUNK),
                    lambda i, here, first=first, last=last: (
                        0,
                        jnp.clip(i, first, last - 1) - first,
                    ),
                )
            )
    half = block // 2
    whole = pl.BlockSpec((2, chips, half, CHUNK), lambda i, here: (0, 0, 0, i))
    plan = (chips, plan)
    return kernel_call(
        lambda *refs: gradient_kernel(plan, *refs),
        [here],
        arrays,
        specs,
        [((2, chips, half, at * CHUNK), jnp.bfloat16)] * 2,
        [whole, whole],
        at,
        name,
        [pltpu.VMEM((2, len(groups[0][1]), chips * block, tokens), jnp.bfloat16)],
    )


def cross_ctx(sent, kept, gate):
    received = after(swap_core(sent), gate)
    halves = [None, None]
    side = lax.axis_index("ctx")
    for which in range(2):
        index = (which + side) % 2
        total = pick(kept, index, 0).astype(jnp.float32) + pick(received, index, 0).astype(
            jnp.float32
        )
        halves[which] = total
    if lax.axis_size("ctx") != 2:
        low = jnp.where(side % 2 == 0, halves[0], halves[1])
        high = jnp.where(side % 2 == 0, halves[1], halves[0])
        return jnp.concatenate([low, high], axis=1), sent, None
    away = halves[1].astype(jnp.bfloat16)
    return halves[0], away, swap_ctx(away)


def cross_chips(crossing, gate):
    mine, _, coming = crossing
    if coming is not None:
        mine = mine + after(coming, gate).astype(jnp.float32)
    mine = mine.astype(jnp.bfloat16)
    return mine, exchange_chips(mine)


def sum_lines(lines, spot):
    chips = lines.shape[0]
    chip, core = spot // 2, spot % 2
    lines = lines.astype(jnp.bfloat16)
    near = swap_core(pick(lines, 1 - core, 1)).astype(jnp.float32)
    lines = (pick(lines, core, 1).astype(jnp.float32) + near).astype(jnp.bfloat16)
    if lax.axis_size("ctx") == 2:
        both = lines.astype(jnp.float32) + swap_ctx(lines).astype(jnp.float32)
    else:
        both = lax.psum(lines, "ctx").astype(jnp.float32)
    lines = both.astype(jnp.bfloat16)
    total = pick(lines, chip, 0).astype(jnp.float32)
    for step in range(1, chips):
        sent = pick(lines, (chip + step) % chips, 0)
        total = total + lax.ppermute(sent, "fsdp", chip_shift(step)).astype(jnp.float32)
    return total


def spread_chips(parts):
    return jnp.sum(parts.astype(jnp.float32), axis=0).astype(jnp.bfloat16)


def spread_end(total, halves):
    if lax.axis_size("ctx") != 2:
        return lax.psum(total, "ctx").reshape(halves, -1, total.shape[1])
    other = swap_ctx(total)
    leading = lax.axis_index("ctx") == 0
    return jnp.stack([jnp.where(leading, total, other), jnp.where(leading, other, total)])


def other_ctx(rows, axis):
    if lax.axis_size("ctx") != 2:
        return lax.all_gather(rows, "ctx", axis=axis, tiled=True)
    return swap_ctx(rows)


def other_tokens(tokens, gate):
    seq_count = tokens.shape[0]
    if lax.axis_size("ctx") != 2 or lax.axis_size("tp") != 2 or seq_count % 2:
        return other_ctx(tokens, 1)
    side = lax.axis_index("tp")
    halves = tokens.reshape(2, seq_count // 2, *tokens.shape[1:])
    mine = after(swap_ctx(pick(halves, side, 0)), gate)
    theirs = swap_tp(mine)
    return jnp.concatenate(
        [jnp.where(side == 0, mine, theirs), jnp.where(side == 0, theirs, mine)]
    )


EXTRA = 16


def body(
    tokens,
    picture_starts,
    ln1_gain,
    ln1_shift,
    w_qkv,
    qv_bias,
    w_proj,
    proj_bias,
    ln2_gain,
    ln2_shift,
    w_fc1,
    fc1_bias,
    w_fc2,
    fc2_bias,
    out_grad,
):
    seq_count, local_len, width = tokens.shape
    fsdp = lax.axis_size("fsdp")
    chips = fsdp // 2
    ranks = lax.axis_size("ctx")
    rank = lax.axis_index("ctx")
    full_len = ranks * local_len
    local_width = w_qkv.shape[2]
    local_heads = local_width // HD
    units = w_fc1.shape[1]
    sequences = range(seq_count)
    spot = lax.axis_index("fsdp")
    side = lax.axis_index("tp")
    here = jnp.stack([spot // 2, spot % 2, rank, side]).astype(jnp.int32)
    place = jnp.stack([rank, jnp.int32(ranks)]).astype(jnp.int32)
    piece_ids = jnp.arange(full_len // PIECE, dtype=jnp.int32)
    pictures = jnp.any(
        piece_ids[None, :, None] == (picture_starts // PIECE)[:, None, :], axis=2
    ).astype(jnp.int32)

    block = ln1_gain.shape[0]
    qv_size, fc1_size = qv_bias.size, fc1_bias.size
    qv_lines = qv_size // block
    small = jnp.concatenate(
        [
            jnp.stack([ln1_gain, ln1_shift, proj_bias, ln2_gain, ln2_shift, fc2_bias]),
            qv_bias.reshape(-1, block),
            fc1_bias.reshape(-1, block),
        ]
    )
    small = jnp.pad(small, ((0, EXTRA - small.shape[0]), (0, 0)))
    qkv_bundle = gather_chips(halves_of(w_qkv.reshape(-1, 3 * local_width)))
    far_proj = swap_tp(w_proj)
    proj_halves = halves_of(
        jnp.concatenate(
            [jnp.where(side == 0, w_proj, far_proj), jnp.where(side == 0, far_proj, w_proj)]
        )
    )
    small = jnp.broadcast_to(small, (proj_halves.shape[0], *small.shape))
    proj_halves = jnp.concatenate([proj_halves, small], axis=1)
    proj_bundle = gather_chips(after(proj_halves, qkv_bundle))
    fc2_pieces = shift_chips(after(halves_of(w_fc2), qkv_bundle))
    fc1_bundle = gather_chips(after(halves_of(w_fc1), proj_bundle))
    far_tokens = other_tokens(tokens, qkv_bundle)
    full_qkv = placed_rows(gather_rest(qkv_bundle), here, "place_qkv", 0)
    mine = swap_core(proj_bundle)

    first = jnp.where(spot % 2 == 0, proj_bundle, mine)[:, -EXTRA:]
    second = jnp.where(spot % 2 == 0, mine, proj_bundle)[:, -EXTRA:]
    smalls = jnp.stack([first, second], axis=1).reshape(fsdp, EXTRA, block).astype(jnp.float32)
    vectors = [smalls[:, i].reshape(-1) for i in range(6)]
    gain_one, shift_one, bias_proj, gain_two, shift_two, bias_fc2 = vectors
    qv_rows = smalls[:, 6 : 6 + qv_lines].reshape(fsdp, 2, local_heads, HD // fsdp)
    qv_rows = qv_rows.transpose(1, 2, 0, 3).reshape(2, local_width)
    bias_fc1 = smalls[:, 6 + qv_lines : 6 + qv_lines + fc1_size // block]
    bias_fc1 = bias_fc1.reshape(fsdp, units // HD, HD // fsdp).transpose(1, 0, 2).reshape(1, -1)
    bias_qkv = jnp.concatenate([qv_rows[0], jnp.zeros_like(qv_rows[0]), qv_rows[1]])
    lines = jnp.stack([bias_proj, gain_two, shift_two, gain_one])

    def project(rows):
        normed = layer_norm(rows.astype(jnp.float32), gain_one, shift_one).astype(jnp.bfloat16)
        result = jnp.einsum("sld,de->sle", normed, full_qkv, preferred_element_type=jnp.float32)
        return normed, (result + bias_qkv).astype(jnp.bfloat16)

    normed_one, triple = project(tokens)
    _, far_triple = project(far_tokens)
    proj_bundles = gather_rest(proj_bundle, triple, near=mine)
    fc2_bundle = jnp.stack(after(tuple(fc2_pieces), full_qkv))
    fc1_near = swap_core(fc1_bundle)
    attended, logs = [], []
    for index in sequences:
        gate = [attended[-1], fc1_near] if index else [fc2_bundle, proj_bundles[-1]]
        heads, log = attention_forward(triple, far_triple, after(place, *gate), pictures, index)
        attended.append(heads)
        logs.append(log)
    tp_attended = [swap_tp(heads) for heads in attended]
    tp_attended[0] = after(tp_attended[0], attended[-1])
    fc1_bundles = gather_rest(fc1_bundle, attended[-1], near=fc1_near)
    fc2_bundles = gather_rest(fc2_bundle, tp_attended[0])
    all_attended = jnp.stack(attended)
    weights = [proj_bundles, fc1_bundles, fc2_bundles]
    if block % PAIR:
        order = lax.rem(here[0] + chips - jnp.arange(chips, dtype=jnp.int32), chips)
        weights = [
            [placed_columns_plain([b[:, :-EXTRA] for b in proj_bundles], here)],
            fc1_bundles,
            [placed_columns_plain([b[order] for b in fc2_bundles], here)],
        ]
    far_attended = other_ctx(after(all_attended, fc2_bundles[-1]), 1)
    far_logs = other_ctx(after(jnp.stack(logs), fc2_bundles[-1]), 3)
    residuals, normed_two, actives, hidden_grads, feeds, backs, swapped_twos = [], [], [], [], [], [], []
    hidden_sums = 0.0
    for index in sequences:
        gate = [backs[-1], far_attended, far_logs, tp_attended[index]] if index else []
        residual, normed, active, hidden_grad, feed, back, hidden_sum, own_proj = feed_forward(
            attended[index],
            after(tp_attended[index], *backs[-1:]),
            tokens,
            out_grad,
            lines,
            bias_fc1,
            weights,
            after(here, *gate),
            index,
        )
        residuals.append(residual)
        normed_two.append(normed)
        actives.append(active)
        hidden_grads.append(hidden_grad)
        feeds.append(feed)
        backs.append(back)
        swapped_twos.append(swap_tp(back))
        hidden_sums = hidden_sums + hidden_sum[0]

    fc2_groups = [([(out_grad, s) for s in sequences], actives)]
    fc1_groups = [([(normed[None], 0) for normed in normed_two], hidden_grads)]
    branches, head_grads, far_head_grads = [], [], []
    two_sums = 0.0
    gate = backs[-1]
    for index in sequences:
        branch, head_grad, two_sum = norm_two_backward(
            backs[index],
            swapped_twos[index],
            residuals[index],
            out_grad,
            lines,
            own_proj,
            after(here, gate),
            index,
        )
        branches.append(branch)
        head_grads.append(head_grad)
        far_head_grads.append(other_ctx(head_grad, 0))
        two_sums = two_sums + two_sum
        if index == 0:
            blocks_fc2 = gradient_blocks(fc2_groups, after(here, head_grad), "grad_fc2")
            gate = blocks_fc2[1]
    cross_fc2 = cross_ctx(*blocks_fc2, head_grads[-1])
    fc1_groups.append(([(branch[None], 0) for branch in branches], attended))
    blocks_fc1 = gradient_blocks(fc1_groups, after(here, cross_fc2[1]), "grad_fc1_proj")

    grad_triples, back_ones, swapped_ones, outputs = [], [], [], []
    one_sums, triple_sums = 0.0, 0.0
    gate = (blocks_fc1[1],)
    for index in sequences:
        if index == 0:
            feed = after(feeds[0], *gate)
            swapped_feed = swap_tp(feed)
        grad_triple = attention_backward(
            (triple, attended[index], head_grads[index], logs[index]),
            (far_triple, far_attended[index], far_head_grads[index], far_logs[index]),
            after(place, *gate),
            pictures,
            index,
        )
        gate = (grad_triple,)
        if index == 0:
            gate, arrived_fc2 = cross_chips(cross_fc2, grad_triple)
            cross_fc1 = cross_ctx(*blocks_fc1, gate)
            gate = (cross_fc1[1],)
        grad_triples.append(grad_triple)
        if index == seq_count - 1:
            total_fc2 = spread_chips(after(arrived_fc2, grad_triple))
            part_fc1, arrived_fc1 = cross_chips(cross_fc1, total_fc2)
            last_groups = [([(normed_one, s) for s in sequences], grad_triples)]
            blocks_last = gradient_blocks(last_groups, after(here, part_fc1), "grad_last")
            gate = (blocks_last[1], *swapped_ones)
        back_one, one_sum, triple_sum = qkv_backward(
            grad_triple, tokens, full_qkv, after(here, *gate), index
        )
        gate = (back_one, swapped_feed)
        back_ones.append(back_one)
        swapped_ones.append(swap_tp(back_one))
        one_sums = one_sums + one_sum
        triple_sums = triple_sums + triple_sum[0]

    def finish_output(index, mine, theirs):
        total = mine.astype(jnp.float32) + theirs.astype(jnp.float32)
        outputs.append((residuals[index] + total + bias_fc2).astype(jnp.bfloat16))

    finish_output(0, feed, after(swapped_feed, back_ones[-1]))
    last_feeds = [after(feeds[index], back_ones[0]) for index in range(1, seq_count)]
    last_swapped = [swap_tp(feed) for feed in last_feeds]

    out_sums = jnp.sum(out_grad.astype(jnp.float32), axis=(0, 1))
    grad_qv = jnp.concatenate([triple_sums[:local_width], triple_sums[2 * local_width :]])
    vectors = [one_sums[0], one_sums[1], two_sums[2], two_sums[0], two_sums[1], out_sums]
    packed = jnp.concatenate(
        [vector.reshape(fsdp, block) for vector in vectors]
        + [
            grad_qv.reshape(2, local_heads, fsdp, HD // fsdp)
            .transpose(2, 0, 1, 3)
            .reshape(fsdp, -1),
            hidden_sums.reshape(-1, fsdp, HD // fsdp).transpose(1, 0, 2).reshape(fsdp, -1),
        ],
        axis=1,
    )
    def norm_one(index, *gate):
        return norm_one_backward(
            back_ones[index],
            swapped_ones[index],
            tokens,
            branches[index],
            lines,
            after(here, *gate),
            index,
        )

    total_fc1 = spread_chips(after(arrived_fc1, back_ones[-1]))
    cross_last = cross_ctx(*blocks_last, back_ones[-1])
    grad_tokens = [norm_one(0, cross_last[1])]
    part_last, arrived_last = cross_chips(cross_last, grad_tokens[0])
    for index in range(1, seq_count):
        finish_output(index, last_feeds[index - 1], after(last_swapped[index - 1], part_last))
    for index in range(1, seq_count):
        grad_tokens.append(norm_one(index, part_last, *last_swapped))
    sums_fc2 = spread_end(after(total_fc2, part_last), 2)
    sums_fc1 = spread_end(after(total_fc1, part_last), 2)
    total_last = spread_chips(arrived_last)
    sums_last = spread_end(total_last, 2)
    small = sum_lines(after(packed, part_last).reshape(chips, 2, -1), spot)
    norm_one = small[: 2 * block].astype(jnp.bfloat16)
    norm_one = norm_one.astype(jnp.float32) + swap_tp(norm_one).astype(jnp.float32)
    vectors = [norm_one[:block], norm_one[block:]]
    vectors += [small[i * block : (i + 1) * block] for i in range(2, 6)]
    shard_qv = small[6 * block : 6 * block + qv_size].reshape(qv_bias.shape)
    shard_fc1_bias = small[6 * block + qv_size :][:fc1_size].reshape(fc1_bias.shape)
    sums_last = sums_last.reshape(block, -1).astype(jnp.float32)
    sums_fc1 = sums_fc1.reshape(block, -1).astype(jnp.float32)
    return (
        jnp.stack(outputs),
        jnp.stack(grad_tokens),
        vectors[0],
        vectors[1],
        sums_last.reshape(-1, 3, local_width),
        shard_qv,
        sums_fc1[:, units:].T,
        vectors[2],
        vectors[3],
        vectors[4],
        sums_fc1[:, :units],
        shard_fc1_bias,
        sums_fc2.reshape(block, -1).astype(jnp.float32).T,
        vectors[5],
    )


def solution(mesh):
    return jax.shard_map(
        body,
        mesh=mesh,
        in_specs=(
            P("fsdp", "ctx", None),
            P("fsdp", None),
            P("fsdp"),
            P("fsdp"),
            P("fsdp", None, "tp"),
            P(None, "tp", "fsdp"),
            P("tp", "fsdp"),
            P("fsdp"),
            P("fsdp"),
            P("fsdp"),
            P("fsdp", "tp"),
            P("tp", "fsdp"),
            P("tp", "fsdp"),
            P("fsdp"),
            P("fsdp", "ctx", None),
        ),
        out_specs=(
            P("fsdp", "ctx", None),
            P("fsdp", "ctx", None),
            P("fsdp"),
            P("fsdp"),
            P("fsdp", None, "tp"),
            P(None, "tp", "fsdp"),
            P("tp", "fsdp"),
            P("fsdp"),
            P("fsdp"),
            P("fsdp"),
            P("fsdp", "tp"),
            P("tp", "fsdp"),
            P("tp", "fsdp"),
            P("fsdp"),
        ),
        check_vma=False,
    )
```

```python
import jax
import jax.numpy as jnp
from jax import lax
from jax.experimental import pallas as pl
from jax.experimental.pallas import tpu as pltpu
from jax.sharding import PartitionSpec as P

HD = 64
PAIR = 2 * HD
PIECE = 256
SCALE = HD ** (-0.5)
KERNEL_VMEM = 56 * 1024 * 1024

epsilon = 1e-05
masked_value = -1e30


def layer_norm(values, gain_vec, shift_vec):
    average = jnp.mean(values, axis=-1, keepdims=True)
    centred = values - average
    variance = jnp.mean(centred * centred, axis=-1, keepdims=True)
    return centred * lax.rsqrt(variance + epsilon) * gain_vec + shift_vec


NT = (((1,), (1,)), ((), ()))


def dot_nt(left, right):
    return lax.dot_general(left, right, NT, preferred_element_type=jnp.float32)


def dot_nn(left, right):
    return jnp.dot(left, right, preferred_element_type=jnp.float32)


def head_lanes(head):
    lanes = lax.broadcasted_iota(jnp.int32, (1, PAIR), 1)
    return (lanes >= head * HD) & (lanes < (head + 1) * HD)


def only_head(rows, head):
    return jnp.where(head_lanes(head), rows, jnp.zeros_like(rows))


def diagonal_mask(scores, joined):
    key_row = lax.broadcasted_iota(jnp.int32, scores.shape, 0)
    query_lane = lax.broadcasted_iota(jnp.int32, scores.shape, 1)
    return (key_row <= query_lane) | joined


def chunk_start(step, place, local_len, chunks):
    return 0 if chunks == 1 else pl.multiple_of(step * local_len, local_len)


SCORE_TILE = 32


def score_tiles(count):
    return [slice(start, start + SCORE_TILE) for start in range(0, count, SCORE_TILE)]


def folded(rows, combine):
    parts = [rows[start : start + 8] for start in range(0, rows.shape[0], 8)]
    while len(parts) > 1:
        parts = [
            combine(parts[i], parts[i + 1]) if i + 1 < len(parts) else parts[i]
            for i in range(0, len(parts), 2)
        ]
    return parts[0]


def attention_forward_kernel(
    place, pictures, q_ref, k_ref, v_ref, k_far, v_far, out_ref, log_ref, scores, weights, values
):
    rank = place[0]
    sequence = place[2]
    local_len = q_ref.shape[1]
    blocks = local_len // PIECE
    chunks = k_far.shape[1] // local_len
    values[...] = v_ref[0].T
    states = [(head, block) for head in range(2) for block in range(blocks)]
    scaled, peaks = [], []
    for index, (head, block) in enumerate(states):
        query = only_head(q_ref[0, block * PIECE : (block + 1) * PIECE, :] * SCALE, head)
        scaled.append(query)
        joined = pictures[sequence, rank * blocks + block] > 0
        count = (block + 1) * PIECE
        scores[index, :count] = dot_nt(k_ref[0, :count], query)
        peak = jnp.full((8, PIECE), masked_value, jnp.float32)
        for tile in score_tiles(count):
            part = scores[index, tile]
            if tile.start >= block * PIECE:
                key_row = lax.broadcasted_iota(jnp.int32, part.shape, 0) + (
                    tile.start - block * PIECE
                )
                lane = lax.broadcasted_iota(jnp.int32, part.shape, 1)
                part = jnp.where((key_row <= lane) | joined, part, masked_value)
                scores[index, tile] = part
            peak = jnp.maximum(peak, folded(part, jnp.maximum))
        peaks.append(peak)

    def far_scores(step, carried):
        keys = k_far[0, pl.ds(chunk_start(step, place, local_len, chunks), local_len), :]
        base = pl.multiple_of((step + 1) * local_len, local_len)
        after = []
        for index, peak in enumerate(carried):
            part = dot_nt(keys, scaled[index])
            scores[index, pl.ds(base, local_len)] = part
            for tile in score_tiles(local_len):
                peak = jnp.maximum(peak, folded(part[tile], jnp.maximum))
            after.append(peak)
        return after

    peaks = lax.fori_loop(0, rank, far_scores, peaks)
    peaks = [jnp.max(peak, axis=0, keepdims=True) for peak in peaks]
    gathered = []
    for index, (head, block) in enumerate(states):
        count = (block + 1) * PIECE
        total = jnp.zeros((8, PIECE), jnp.float32)
        for tile in score_tiles(count):
            weight = jnp.exp(scores[index, tile] - peaks[index])
            total = total + folded(weight, jnp.add)
            weights[index, tile] = weight.astype(jnp.bfloat16)
        gathered.append(
            (total, dot_nn(values[head * HD : (head + 1) * HD, :count], weights[index, :count]))
        )

    def far_values(step, carried):
        base = pl.multiple_of((step + 1) * local_len, local_len)
        far = v_far[0, pl.ds(chunk_start(step, place, local_len, chunks), local_len), :].T
        after = []
        for index, (total, sums) in enumerate(carried):
            head = states[index][0]
            for tile in score_tiles(local_len):
                weight = jnp.exp(
                    scores[index, pl.ds(base + tile.start, SCORE_TILE)] - peaks[index]
                )
                total = total + folded(weight, jnp.add)
                weights[index, tile] = weight.astype(jnp.bfloat16)
            sums = sums + dot_nn(far[head * HD : (head + 1) * HD], weights[index])
            after.append((total, sums))
        return after

    gathered = lax.fori_loop(0, rank, far_values, gathered)
    for block in range(blocks):
        rows = slice(block * PIECE, (block + 1) * PIECE)
        halves = []
        for head in range(2):
            index = head * blocks + block
            total = jnp.sum(gathered[index][0], axis=0, keepdims=True)
            halves.append(gathered[index][1] / total)
            log_ref[0, head : head + 1, rows] = peaks[index] + jnp.log(total)
        out_ref[rows, :] = jnp.concatenate(halves, axis=0).T.astype(out_ref.dtype)


def attention_forward(triple, far, place, pictures, index):
    place = jnp.concatenate([place, jnp.full((1,), index, jnp.int32)])
    _, local_len, triple_width = triple.shape
    far_len = far.shape[1]
    local_width = triple_width // 3
    pairs = local_width // PAIR

    def part(length, offset):
        return pl.BlockSpec(
            (1, length, PAIR), lambda p, place, pics: (index, 0, offset * pairs + p)
        )

    return pl.pallas_call(
        attention_forward_kernel,
        grid_spec=pltpu.PrefetchScalarGridSpec(
            num_scalar_prefetch=2,
            grid=(pairs,),
            in_specs=[
                part(local_len, 0),
                part(local_len, 1),
                part(local_len, 2),
                part(far_len, 1),
                part(far_len, 2),
            ],
            out_specs=[
                pl.BlockSpec((local_len, PAIR), lambda p, place, pics: (0, p)),
                pl.BlockSpec((1, 2, local_len), lambda p, place, pics: (p, 0, 0)),
            ],
            scratch_shapes=[
                pltpu.VMEM((2 * local_len // PIECE, local_len + far_len, PIECE), jnp.float32),
                pltpu.VMEM((2 * local_len // PIECE, local_len, PIECE), jnp.bfloat16),
                pltpu.VMEM((PAIR, local_len), jnp.bfloat16),
            ],
        ),
        out_shape=[
            jax.ShapeDtypeStruct((local_len, local_width), jnp.bfloat16),
            jax.ShapeDtypeStruct((pairs, 2, local_len), jnp.float32),
        ],
        compiler_params=pltpu.CompilerParams(vmem_limit_bytes=KERNEL_VMEM),
        cost_estimate=pl.CostEstimate(flops=50000000000, bytes_accessed=0, transcendentals=0),
        name="attention_forward",
    )(place, pictures, triple, triple, triple, far, far)


def attention_backward_kernel(
    place,
    pictures,
    q_ref,
    k_ref,
    v_ref,
    out_ref,
    grad_ref,
    log_ref,
    q_far,
    k_far,
    v_far,
    out_far,
    grad_far,
    log_far,
    triple_ref,
):
    rank = place[0]
    ranks = place[1]
    sequence = place[2]
    pair = pl.program_id(0)
    local_len = triple_ref.shape[0]
    local_width = triple_ref.shape[1] // 3
    blocks = local_len // PIECE
    chunks = k_far.shape[1] // local_len

    def sides_of(queries, grads, outs, logs):
        turned = (grads.astype(jnp.float32) * outs.astype(jnp.float32)).T
        queries = queries * SCALE
        sides = []
        for head in range(2):
            delta = jnp.sum(turned[head * HD : (head + 1) * HD], axis=0, keepdims=True)
            sides.append(
                (
                    only_head(queries, head),
                    only_head(grads, head),
                    logs[head : head + 1],
                    delta,
                )
            )
        return sides

    def pieces(keys, values, query, grad, log, delta, mask=None):
        scores = dot_nt(keys, query)
        probs = jnp.exp(scores - log)
        if mask is not None:
            probs = jnp.where(mask(probs), probs, 0.0)
        grad_probs = dot_nt(values, grad)
        return probs, (probs * (grad_probs - delta)).astype(jnp.bfloat16)

    key_own = k_ref[0]
    value_own = v_ref[0]
    key_turned = key_own.T
    sides = sides_of(q_ref[0], grad_ref[...], out_ref[...], log_ref[0])
    grad_keys = [None] * blocks
    grad_values = [None] * blocks
    grad_queries = []

    def add(total, part):
        return part if total is None else total + part

    for head in range(2):
        queries, grads, logs, deltas = sides[head]
        for block in range(blocks):
            rows = slice(block * PIECE, (block + 1) * PIECE)
            joined = pictures[sequence, rank * blocks + block] > 0
            grad_query = None
            for key_block in range(block + 1):
                key_rows = slice(key_block * PIECE, (key_block + 1) * PIECE)
                mask = (lambda p, j=joined: diagonal_mask(p, j)) if key_block == block else None
                probs, grad_scores = pieces(
                    key_own[key_rows],
                    value_own[key_rows],
                    queries[rows],
                    grads[rows],
                    logs[:, rows],
                    deltas[:, rows],
                    mask,
                )
                grad_values[key_block] = add(
                    grad_values[key_block], dot_nn(probs.astype(jnp.bfloat16), grads[rows])
                )
                grad_keys[key_block] = add(
                    grad_keys[key_block], dot_nn(grad_scores, queries[rows])
                )
                grad_query = add(
                    grad_query,
                    dot_nn(key_turned[head * HD : (head + 1) * HD, key_rows], grad_scores),
                )
            grad_queries.append(grad_query)

    def earlier(step, carried):
        start = chunk_start(step, place, local_len, chunks)
        keys = k_far[0, pl.ds(start, local_len), :]
        values = v_far[0, pl.ds(start, local_len), :]
        turned = keys.T
        after = []
        for index, total in enumerate(carried):
            head, block = index // blocks, index % blocks
            rows = slice(block * PIECE, (block + 1) * PIECE)
            queries, grads, logs, deltas = sides[head]
            _, grad_scores = pieces(
                keys, values, queries[rows], grads[rows], logs[:, rows], deltas[:, rows]
            )
            after.append(total + dot_nn(turned[head * HD : (head + 1) * HD], grad_scores))
        return after

    grad_queries = lax.fori_loop(0, rank, earlier, grad_queries)
    for block in range(blocks):
        rows = slice(block * PIECE, (block + 1) * PIECE)
        both = jnp.concatenate([grad_queries[head * blocks + block] for head in range(2)], axis=0)
        triple_ref[rows, pl.ds(pl.multiple_of(pair * PAIR, PAIR), PAIR)] = (
            (both * SCALE).T.astype(triple_ref.dtype)
        )

    def later(step, carried):
        start = chunk_start(step, place, local_len, chunks)
        window = pl.ds(start, local_len)
        sides = sides_of(
            q_far[0, window, :], grad_far[window, :], out_far[window, :], log_far[0, :, window]
        )
        keys_after, values_after = list(carried[0]), list(carried[1])
        for head in range(2):
            queries, grads, logs, deltas = sides[head]
            for block in range(blocks):
                rows = slice(block * PIECE, (block + 1) * PIECE)
                probs, grad_scores = pieces(
                    key_own[rows], value_own[rows], queries, grads, logs, deltas
                )
                values_after[block] = values_after[block] + dot_nn(
                    probs.astype(jnp.bfloat16), grads
                )
                keys_after[block] = keys_after[block] + dot_nn(grad_scores, queries)
        return keys_after, values_after

    grad_keys, grad_values = lax.fori_loop(rank + 1, ranks, later, (grad_keys, grad_values))
    for block in range(blocks):
        rows = slice(block * PIECE, (block + 1) * PIECE)
        for part, grads in ((1, grad_keys), (2, grad_values)):
            column = pl.multiple_of(part * local_width + pair * PAIR, PAIR)
            triple_ref[rows, pl.ds(column, PAIR)] = grads[block].astype(triple_ref.dtype)


def attention_backward(own, other, place, pictures, index):
    place = jnp.concatenate([place, jnp.full((1,), index, jnp.int32)])
    _, local_len, triple_width = own[0].shape
    pairs = triple_width // (3 * PAIR)
    specs = []
    for length in (local_len, other[0].shape[1]):
        for offset in range(3):
            specs.append(
                pl.BlockSpec(
                    (1, length, PAIR),
                    lambda p, place, pics, offset=offset: (index, 0, offset * pairs + p),
                )
            )
        specs += [pl.BlockSpec((length, PAIR), lambda p, place, pics: (0, p))] * 2
        specs.append(pl.BlockSpec((1, 2, length), lambda p, place, pics: (p, 0, 0)))
    return pl.pallas_call(
        attention_backward_kernel,
        grid_spec=pltpu.PrefetchScalarGridSpec(
            num_scalar_prefetch=2,
            grid=(pairs,),
            in_specs=specs,
            out_specs=pl.BlockSpec((local_len, triple_width), lambda p, place, pics: (0, 0)),
        ),
        out_shape=jax.ShapeDtypeStruct((local_len, triple_width), jnp.bfloat16),
        compiler_params=pltpu.CompilerParams(vmem_limit_bytes=KERNEL_VMEM),
        cost_estimate=pl.CostEstimate(flops=50000000000, bytes_accessed=0, transcendentals=0),
        name="attention_backward",
    )(place, pictures, *([own[0]] * 3), *own[1:], *([other[0]] * 3), *other[1:])


def core_swap():
    return [(place, place ^ 1) for place in range(lax.axis_size("fsdp"))]


PAIR_SWAP = [(0, 1), (1, 0)]


def swap_core(rows):
    return lax.ppermute(rows, "fsdp", core_swap())


def swap_ctx(rows):
    return lax.ppermute(rows, "ctx", PAIR_SWAP)


def swap_tp(rows):
    return lax.ppermute(rows, "tp", PAIR_SWAP)


def exchange_chips(rows):
    fsdp = lax.axis_size("fsdp")
    groups = [list(range(core, fsdp, 2)) for core in range(2)]
    return lax.all_to_all(
        rows, "fsdp", split_axis=0, concat_axis=0, tiled=True, axis_index_groups=groups
    )


def pick(array, index, axis):
    return lax.dynamic_index_in_dim(array, index, axis, keepdims=False)


def after(value, *others):
    return lax.optimization_barrier((value, *others))[0]


def halves_of(shard):
    halves = 2 if lax.axis_size("ctx") == 2 else 1
    return shard.reshape(halves, -1, shard.shape[1])


def gather_chips(halves):
    chips = lax.axis_size("fsdp") // 2
    part = pick(halves, lax.axis_index("ctx"), 0) if halves.shape[0] == 2 else halves[0]
    return exchange_chips(jnp.broadcast_to(part, (chips, *part.shape)))


def chip_shift(step):
    chips = lax.axis_size("fsdp") // 2
    return [
        (2 * chip + core, 2 * ((chip + step) % chips) + core)
        for chip in range(chips)
        for core in range(2)
    ]


def shift_chips(halves):
    part = pick(halves, lax.axis_index("ctx"), 0) if halves.shape[0] == 2 else halves[0]
    chips = lax.axis_size("fsdp") // 2
    return [part] + [lax.ppermute(part, "fsdp", chip_shift(step)) for step in range(1, chips)]


def gather_rest(bundle, *gate, near=None):
    bundles = [bundle, swap_core(bundle) if near is None else near]
    if lax.axis_size("ctx") == 2:
        across = after(swap_ctx(bundle), *gate)
        bundles += [across, swap_core(across)]
    return bundles


def kernel_call(kernel, scalars, arrays, in_specs, outs, out_specs, grid, name, scratch=(), flops=0):
    size = sum(array.size for array in arrays)
    return pl.pallas_call(
        kernel,
        grid_spec=pltpu.PrefetchScalarGridSpec(
            num_scalar_prefetch=len(scalars),
            grid=(grid,),
            in_specs=in_specs,
            out_specs=out_specs,
            scratch_shapes=list(scratch),
        ),
        out_shape=[jax.ShapeDtypeStruct(shape, dtype) for shape, dtype in outs],
        compiler_params=pltpu.CompilerParams(vmem_limit_bytes=KERNEL_VMEM),
        cost_estimate=pl.CostEstimate(flops=50000000000, bytes_accessed=0, transcendentals=0),
        name=name,
    )(*scalars, *arrays)


def owners(here, sides):
    for index in range(2 * sides):
        core = here[1] if index % 2 == 0 else 1 - here[1]
        yield core, ((here[2] if index < 2 else 1 - here[2]) if sides == 2 else 0)


def placed_rows(bundles, here, name, extra):
    fsdp = lax.axis_size("fsdp")
    sides = len(bundles) // 2
    chips, total, width = bundles[0].shape
    height = total - extra
    chunk = 512

    def kernel(here, *refs):
        for index, (core, side) in enumerate(owners(here, sides)):
            for chip in range(chips):
                refs[-1][(2 * chip + core) * sides + side] = refs[index][chip, :height]

    (result,) = kernel_call(
        kernel,
        [here],
        bundles,
        [pl.BlockSpec((chips, total, chunk), lambda i, here: (0, 0, i))] * (2 * sides),
        [((fsdp * sides, height, width), jnp.bfloat16)],
        [pl.BlockSpec((fsdp * sides, height, chunk), lambda i, here: (0, 0, i))],
        width // chunk,
        name,
    )
    return result.reshape(-1, width)


def placed_columns_plain(bundles, here):
    sides = []
    for mine, other in zip(bundles[::2], bundles[1::2]):
        first = jnp.where(here[1] == 0, mine, other)
        second = jnp.where(here[1] == 0, other, mine)
        both = jnp.stack([first, second], axis=1)
        sides.append(both.reshape(-1, *both.shape[2:]))
    if len(sides) == 2:
        sides = [
            jnp.where(here[2] == 0, sides[0], sides[1]),
            jnp.where(here[2] == 0, sides[1], sides[0]),
        ]
    fsdp, _, width = sides[0].shape
    return jnp.concatenate(sides, axis=1).transpose(1, 0, 2).reshape(-1, fsdp * width)


def weight_copies(bundles, target, here, columns, shifted=False):
    if len(bundles) == 1:
        yield bundles[0], target
        return
    sides = len(bundles) // 2
    for index, (core, side) in enumerate(owners(here, sides)):
        chips, _, width = bundles[index].shape
        height = target.shape[0] // (sides if columns else 2 * chips * sides)
        for chip in range(chips):
            source = bundles[index].at[chip, pl.ds(0, height)]
            block = 2 * (lax.rem(here[0] + chips - chip, chips) if shifted else chip) + core
            if columns:
                across = pl.ds(pl.multiple_of(block * width, width), width)
                yield source, target.at[pl.ds(pl.multiple_of(side * height, height), height), across]
            else:
                row = pl.multiple_of((block * sides + side) * height, height)
                yield source, target.at[pl.ds(row, height)]


UNITS = 1024
TILE = 16
ROOT = 0.7978845608028654
CUBIC = 0.044715


def feed_kernel(counts, here, *refs):
    own_ref, tp_ref, tokens_ref, grad_ref, vector_ref, bias_ref = refs[:6]
    at = 6
    bundles = []
    for count in counts:
        bundles.append(refs[at : at + count])
        at += count
    residual_ref, normed_ref, active_ref, hidden_ref, feed_ref, back_ref, sum_ref, proj_ref = refs[
        at : at + 8
    ]
    proj, first, second, feed, back, hidden_pre, grad_active, semaphores = refs[at + 8 :]
    step = pl.program_id(0)
    copies = [
        weight_copies(bundles[0], proj, here, True),
        weight_copies(bundles[1], first, here, False),
        weight_copies(bundles[2], second, here, True, True),
    ]
    made, number = [], 0
    for group in copies:
        made.append([])
        for source, place in group:
            made[-1].append(pltpu.make_async_copy(source, place, semaphores.at[number]))
            number += 1
    rows = proj.shape[0] // 2
    kept = pltpu.make_async_copy(
        proj.at[pl.ds(pl.multiple_of(here[3] * rows, rows), rows)],
        proj_ref,
        semaphores.at[number],
    )

    @pl.when(step == 0)
    def _():
        for group in made:
            for copy in group:
                copy.start()
        for copy in made[0]:
            copy.wait()
        kept.start()
        leading = here[3] == 0
        low = jnp.where(leading, own_ref[...], tp_ref[...])
        high = jnp.where(leading, tp_ref[...], own_ref[...])
        feed[...] = dot_nn(low, proj[:rows]) + dot_nn(high, proj[rows:])
        for start in range(0, feed.shape[0], TILE):
            lines = slice(start, start + TILE)
            residual = tokens_ref[0, lines].astype(jnp.float32) + feed[lines] + vector_ref[0:1]
            residual_ref[lines] = residual
            unit, _ = centred_rows(residual)
            normed_ref[lines] = (unit * vector_ref[1:2] + vector_ref[2:3]).astype(
                normed_ref.dtype
            )
        for copy in made[1]:
            copy.wait()

    units = pl.ds(pl.multiple_of(step * UNITS, UNITS), UNITS)
    hidden_pre[...] = dot_nn(normed_ref[...], first[:, units])

    @pl.when(step == 0)
    def _():
        for copy in made[2]:
            copy.wait()
        kept.wait()

    grad_active[...] = dot_nt(grad_ref[0], second[units])
    totals = jnp.zeros((TILE, UNITS), jnp.float32)
    for start in range(0, feed.shape[0], TILE):
        lines = slice(start, start + TILE)
        hidden = hidden_pre[lines] + bias_ref[...]
        square = hidden * hidden
        bent = jnp.tanh(hidden * (ROOT + ROOT * CUBIC * square))
        share = 0.5 + 0.5 * bent
        active_ref[lines] = (hidden * share).astype(jnp.bfloat16)
        slope = share + hidden * (1.0 - bent * bent) * (
            0.5 * ROOT + 1.5 * ROOT * CUBIC * square
        )
        grad_hidden = (grad_active[lines] * slope).astype(jnp.bfloat16)
        hidden_ref[lines] = grad_hidden
        totals = totals + grad_hidden.astype(jnp.float32)
    sum_ref[...] = jnp.sum(totals, axis=0, keepdims=True)
    active = active_ref[...]
    feed_part = dot_nn(active, second[units])
    back_part = dot_nt(hidden_ref[...], first[:, units])

    @pl.when(step == 0)
    def _():
        feed[...] = feed_part
        back[...] = back_part

    @pl.when(step > 0)
    def _():
        feed[...] += feed_part
        back[...] += back_part

    @pl.when(step == pl.num_programs(0) - 1)
    def _():
        feed_ref[...] = feed[...].astype(feed_ref.dtype)
        back_ref[...] = back[...].astype(back_ref.dtype)


def feed_forward(own, tp, tokens, out_grad, vectors, bias, weights, here, index):
    local_len, local_width = own.shape
    width = tokens.shape[2]
    units = bias.shape[1]
    counts = tuple(len(group) for group in weights)
    copies = sum(1 if len(group) == 1 else len(group) * group[0].shape[0] for group in weights)
    whole = lambda shape: pl.BlockSpec(shape, lambda j, here: (0,) * len(shape))
    row = pl.BlockSpec((1, local_len, width), lambda j, here: (index, 0, 0))
    block = pl.BlockSpec((local_len, UNITS), lambda j, here: (0, j))
    line = pl.BlockSpec((1, UNITS), lambda j, here: (0, j))
    flat = [array for group in weights for array in group]
    half, full = jnp.bfloat16, jnp.float32
    return kernel_call(
        lambda *refs: feed_kernel(counts, *refs),
        [here],
        [own, tp, tokens, out_grad, vectors, bias] + flat,
        [whole(own.shape), whole(own.shape), row, row, whole(vectors.shape), line]
        + [pl.BlockSpec(memory_space=pl.ANY)] * len(flat),
        [
            ((local_len, width), full),
            ((local_len, width), half),
            ((local_len, units), half),
            ((local_len, units), half),
            ((local_len, width), half),
            ((local_len, width), half),
            ((1, units), full),
            ((local_width, width), half),
        ],
        [whole((local_len, width)), whole((local_len, width)), block, block]
        + [whole((local_len, width)), whole((local_len, width)), line]
        + [pl.BlockSpec(memory_space=pl.ANY)],
        units // UNITS,
        "feed_forward",
        [
            pltpu.VMEM((2 * local_width, width), half),
            pltpu.VMEM((width, units), half),
            pltpu.VMEM((units, width), half),
            pltpu.VMEM((local_len, width), full),
            pltpu.VMEM((local_len, width), full),
            pltpu.VMEM((local_len, UNITS), full),
            pltpu.VMEM((local_len, UNITS), full),
            pltpu.SemaphoreType.DMA((copies + 1,)),
        ],
        flops=8 * local_len * width * units,
    )


ROWS = 256


def centred_rows(rows):
    average = jnp.mean(rows, axis=-1, keepdims=True)
    centred = rows - average
    spread = lax.rsqrt(jnp.mean(centred * centred, axis=-1, keepdims=True) + epsilon)
    return centred * spread, spread


def through_norm(grads, unit, spread, gain):
    scaled = grads * gain
    return spread * (
        scaled
        - jnp.mean(scaled, axis=-1, keepdims=True)
        - unit * jnp.mean(scaled * unit, axis=-1, keepdims=True)
    )


def accumulate(ref, totals):
    total = jnp.concatenate([jnp.sum(lines, axis=0, keepdims=True) for lines in totals])

    @pl.when(pl.program_id(0) == 0)
    def _():
        ref[...] = total

    @pl.when(pl.program_id(0) > 0)
    def _():
        ref[...] += total


def tiles_of(count):
    return [slice(start, start + TILE) for start in range(0, count, TILE)]


def norm_two_kernel(
    here, own_ref, tp_ref, residual_ref, grad_ref, vector_ref, proj_ref, branch_ref, heads_ref, sum_ref
):
    totals = [jnp.zeros((TILE, own_ref.shape[1]), jnp.float32)] * 3
    for lines in tiles_of(own_ref.shape[0]):
        grads = own_ref[lines].astype(jnp.float32) + tp_ref[lines].astype(jnp.float32)
        unit, spread = centred_rows(residual_ref[lines])
        total = grad_ref[0, lines].astype(jnp.float32) + through_norm(
            grads, unit, spread, vector_ref[1:2]
        )
        branch = total.astype(jnp.bfloat16)
        branch_ref[lines] = branch
        totals = [
            totals[0] + grads * unit,
            totals[1] + grads,
            totals[2] + branch.astype(jnp.float32),
        ]
    heads_ref[...] = dot_nt(branch_ref[...], proj_ref[...]).astype(heads_ref.dtype)
    accumulate(sum_ref, totals)


def norm_two_backward(own, tp, residual, out_grad, vectors, proj, here, index):
    local_len, width = own.shape
    local_width = proj.shape[0]
    whole = lambda shape: pl.BlockSpec(shape, lambda i, here: (0,) * len(shape))
    row = pl.BlockSpec((ROWS, width), lambda i, here: (i, 0))
    return kernel_call(
        norm_two_kernel,
        [here],
        [own, tp, residual, out_grad, vectors, proj],
        [row, row, row, pl.BlockSpec((1, ROWS, width), lambda i, here: (index, i, 0))]
        + [whole(vectors.shape), whole(proj.shape)],
        [
            ((local_len, width), jnp.bfloat16),
            ((local_len, local_width), jnp.bfloat16),
            ((3, width), jnp.float32),
        ],
        [row, pl.BlockSpec((ROWS, local_width), lambda i, here: (i, 0)), whole((3, width))],
        local_len // ROWS,
        "norm_two_backward",
        flops=2 * local_len * width * local_width,
    )


def qkv_back_kernel(here, grad_ref, tokens_ref, weight_ref, back_ref, sum_ref, triple_ref, back):
    back[...] = dot_nt(grad_ref[...], weight_ref[...])
    totals = [jnp.zeros((TILE, back.shape[1]), jnp.float32)] * 2
    triple = jnp.zeros((TILE, grad_ref.shape[1]), jnp.float32)
    for lines in tiles_of(back.shape[0]):
        part = back[lines]
        back_ref[lines] = part.astype(back_ref.dtype)
        unit, _ = centred_rows(tokens_ref[0, lines].astype(jnp.float32))
        totals = [totals[0] + part * unit, totals[1] + part]
        triple = triple + grad_ref[lines].astype(jnp.float32)
    accumulate(sum_ref, totals)
    accumulate(triple_ref, [triple])


def qkv_backward(grad_triple, tokens, weight, here, index):
    local_len, triple_width = grad_triple.shape
    width = tokens.shape[2]
    whole = lambda shape: pl.BlockSpec(shape, lambda i, here: (0,) * len(shape))
    return kernel_call(
        qkv_back_kernel,
        [here],
        [grad_triple, tokens, weight],
        [
            pl.BlockSpec((ROWS, triple_width), lambda i, here: (i, 0)),
            pl.BlockSpec((1, ROWS, width), lambda i, here: (index, i, 0)),
            whole(weight.shape),
        ],
        [
            ((local_len, width), jnp.bfloat16),
            ((2, width), jnp.float32),
            ((1, triple_width), jnp.float32),
        ],
        [
            pl.BlockSpec((ROWS, width), lambda i, here: (i, 0)),
            whole((2, width)),
            whole((1, triple_width)),
        ],
        local_len // ROWS,
        "qkv_backward",
        [pltpu.VMEM((ROWS, width), jnp.float32)],
        flops=2 * local_len * width * triple_width,
    )


def norm_one_kernel(here, own_ref, tp_ref, tokens_ref, residual_ref, vector_ref, out_ref):
    for lines in tiles_of(own_ref.shape[0]):
        grads = own_ref[lines].astype(jnp.float32) + tp_ref[lines].astype(jnp.float32)
        unit, spread = centred_rows(tokens_ref[0, lines].astype(jnp.float32))
        out_ref[lines] = (
            residual_ref[lines].astype(jnp.float32)
            + through_norm(grads, unit, spread, vector_ref[3:4])
        ).astype(out_ref.dtype)


def norm_one_backward(own, tp, tokens, residual, vectors, here, index):
    local_len, width = own.shape
    row = pl.BlockSpec((ROWS, width), lambda i, here: (i, 0))
    return kernel_call(
        norm_one_kernel,
        [here],
        [own, tp, tokens, residual, vectors],
        [row, row, pl.BlockSpec((1, ROWS, width), lambda i, here: (index, i, 0)), row]
        + [pl.BlockSpec(vectors.shape, lambda i, here: (0, 0))],
        [((local_len, width), jnp.bfloat16)],
        [row],
        local_len // ROWS,
        "norm_one_backward",
    )[0]


CHUNK = 512


def gradient_kernel(plan, here, *refs):
    chips, groups = plan
    step = pl.program_id(0)
    refs = list(refs)
    turned = refs.pop()
    outs = [refs.pop(-2), refs.pop()]
    rows = outs[0].shape[2]
    at = 0
    for first, last, sequences in groups:
        lefts = refs[at : at + 2 * sequences * chips]
        rights = refs[at + 2 * sequences * chips : at + sequences * (2 * chips + 1)]
        at += sequences * (2 * chips + 1)

        @pl.when(step == first)
        def _():
            for index, left in enumerate(lefts):
                which, rest = divmod(index, sequences * chips)
                sequence, chip = divmod(rest, chips)
                block = left.shape[2]
                turned[which, sequence, chip * block : (chip + 1) * block] = left[0].T

        @pl.when((step >= first) & (step < last))
        def _():
            for which in range(2):
                total = dot_nn(turned[which, 0], rights[0][...])
                for sequence in range(1, sequences):
                    total += dot_nn(turned[which, sequence], rights[sequence][...])
                total = total.astype(jnp.bfloat16).reshape(chips, 2, rows, -1)
                for half in range(2):
                    outs[which][half] = total[:, half]


def gradient_plain(groups, here):
    chips = lax.axis_size("fsdp") // 2
    columns = []
    for lefts, rights in groups:
        total = 0.0
        for (array, lead), right in zip(lefts, rights):
            total = total + lax.dot_general(
                array[lead], right, (((0,), (0,)), ((), ())), preferred_element_type=jnp.float32
            )
        columns.append(total)
    whole = jnp.concatenate(columns, axis=1)
    whole = whole.astype(jnp.bfloat16).reshape(chips, 2, 2, -1, whole.shape[1])
    whole = whole.transpose(2, 1, 0, 3, 4)
    return pick(whole, 1 - here[1], 1), pick(whole, here[1], 1)


def gradient_blocks(groups, here, name):
    chips = lax.axis_size("fsdp") // 2
    if groups[0][0][0][0].shape[2] % (2 * chips * PAIR):
        return gradient_plain(groups, here)
    arrays, specs, plan = [], [], []
    at = 0
    for lefts, rights in groups:
        first, last = at, at + rights[0].shape[1] // CHUNK
        at = last
        plan.append((first, last, len(rights)))
        tokens = rights[0].shape[0]
        for own in (0, 1):
            for array, lead in lefts:
                block = array.shape[2] // (2 * chips)
                for chip in range(chips):
                    arrays.append(array)
                    specs.append(
                        pl.BlockSpec(
                            (1, tokens, block),
                            lambda i, here, lead=lead, chip=chip, own=own: (
                                lead,
                                0,
                                2 * chip + (here[1] if own else 1 - here[1]),
                            ),
                        )
                    )
        for right in rights:
            arrays.append(right)
            specs.append(
                pl.BlockSpec(
                    (tokens, CHUNK),
                    lambda i, here, first=first, last=last: (
                        0,
                        jnp.clip(i, first, last - 1) - first,
                    ),
                )
            )
    half = block // 2
    whole = pl.BlockSpec((2, chips, half, CHUNK), lambda i, here: (0, 0, 0, i))
    plan = (chips, plan)
    return kernel_call(
        lambda *refs: gradient_kernel(plan, *refs),
        [here],
        arrays,
        specs,
        [((2, chips, half, at * CHUNK), jnp.bfloat16)] * 2,
        [whole, whole],
        at,
        name,
        [pltpu.VMEM((2, len(groups[0][1]), chips * block, tokens), jnp.bfloat16)],
    )


def cross_ctx(sent, kept, gate):
    received = after(swap_core(sent), gate)
    halves = [None, None]
    side = lax.axis_index("ctx")
    for which in range(2):
        index = (which + side) % 2
        total = pick(kept, index, 0).astype(jnp.float32) + pick(received, index, 0).astype(
            jnp.float32
        )
        halves[which] = total
    if lax.axis_size("ctx") != 2:
        low = jnp.where(side % 2 == 0, halves[0], halves[1])
        high = jnp.where(side % 2 == 0, halves[1], halves[0])
        return jnp.concatenate([low, high], axis=1), sent, None
    away = halves[1].astype(jnp.bfloat16)
    return halves[0], away, swap_ctx(away)


def cross_chips(crossing, gate):
    mine, _, coming = crossing
    if coming is not None:
        mine = mine + after(coming, gate).astype(jnp.float32)
    mine = mine.astype(jnp.bfloat16)
    return mine, exchange_chips(mine)


def sum_lines(lines, spot):
    chips = lines.shape[0]
    chip, core = spot // 2, spot % 2
    lines = lines.astype(jnp.bfloat16)
    near = swap_core(pick(lines, 1 - core, 1)).astype(jnp.float32)
    lines = (pick(lines, core, 1).astype(jnp.float32) + near).astype(jnp.bfloat16)
    if lax.axis_size("ctx") == 2:
        both = lines.astype(jnp.float32) + swap_ctx(lines).astype(jnp.float32)
    else:
        both = lax.psum(lines, "ctx").astype(jnp.float32)
    lines = both.astype(jnp.bfloat16)
    total = pick(lines, chip, 0).astype(jnp.float32)
    for step in range(1, chips):
        sent = pick(lines, (chip + step) % chips, 0)
        total = total + lax.ppermute(sent, "fsdp", chip_shift(step)).astype(jnp.float32)
    return total


def spread_chips(parts):
    return jnp.sum(parts.astype(jnp.float32), axis=0).astype(jnp.bfloat16)


def spread_end(total, halves):
    if lax.axis_size("ctx") != 2:
        return lax.psum(total, "ctx").reshape(halves, -1, total.shape[1])
    other = swap_ctx(total)
    leading = lax.axis_index("ctx") == 0
    return jnp.stack([jnp.where(leading, total, other), jnp.where(leading, other, total)])


def other_ctx(rows, axis):
    if lax.axis_size("ctx") != 2:
        return lax.all_gather(rows, "ctx", axis=axis, tiled=True)
    return swap_ctx(rows)


def other_tokens(tokens, gate):
    seq_count = tokens.shape[0]
    if lax.axis_size("ctx") != 2 or lax.axis_size("tp") != 2 or seq_count % 2:
        return other_ctx(tokens, 1)
    side = lax.axis_index("tp")
    halves = tokens.reshape(2, seq_count // 2, *tokens.shape[1:])
    mine = after(swap_ctx(pick(halves, side, 0)), gate)
    theirs = swap_tp(mine)
    return jnp.concatenate(
        [jnp.where(side == 0, mine, theirs), jnp.where(side == 0, theirs, mine)]
    )


EXTRA = 16


def body(
    tokens,
    picture_starts,
    ln1_gain,
    ln1_shift,
    w_qkv,
    qv_bias,
    w_proj,
    proj_bias,
    ln2_gain,
    ln2_shift,
    w_fc1,
    fc1_bias,
    w_fc2,
    fc2_bias,
    out_grad,
):
    seq_count, local_len, width = tokens.shape
    fsdp = lax.axis_size("fsdp")
    chips = fsdp // 2
    ranks = lax.axis_size("ctx")
    rank = lax.axis_index("ctx")
    full_len = ranks * local_len
    local_width = w_qkv.shape[2]
    local_heads = local_width // HD
    units = w_fc1.shape[1]
    sequences = range(seq_count)
    spot = lax.axis_index("fsdp")
    side = lax.axis_index("tp")
    here = jnp.stack([spot // 2, spot % 2, rank, side]).astype(jnp.int32)
    place = jnp.stack([rank, jnp.int32(ranks)]).astype(jnp.int32)
    piece_ids = jnp.arange(full_len // PIECE, dtype=jnp.int32)
    pictures = jnp.any(
        piece_ids[None, :, None] == (picture_starts // PIECE)[:, None, :], axis=2
    ).astype(jnp.int32)

    block = ln1_gain.shape[0]
    qv_size, fc1_size = qv_bias.size, fc1_bias.size
    qv_lines = qv_size // block
    small = jnp.concatenate(
        [
            jnp.stack([ln1_gain, ln1_shift, proj_bias, ln2_gain, ln2_shift, fc2_bias]),
            qv_bias.reshape(-1, block),
            fc1_bias.reshape(-1, block),
        ]
    )
    small = jnp.pad(small, ((0, EXTRA - small.shape[0]), (0, 0)))
    qkv_bundle = gather_chips(halves_of(w_qkv.reshape(-1, 3 * local_width)))
    far_proj = swap_tp(w_proj)
    proj_halves = halves_of(
        jnp.concatenate(
            [jnp.where(side == 0, w_proj, far_proj), jnp.where(side == 0, far_proj, w_proj)]
        )
    )
    small = jnp.broadcast_to(small, (proj_halves.shape[0], *small.shape))
    proj_halves = jnp.concatenate([proj_halves, small], axis=1)
    proj_bundle = gather_chips(after(proj_halves, qkv_bundle))
    fc2_pieces = shift_chips(after(halves_of(w_fc2), qkv_bundle))
    fc1_bundle = gather_chips(after(w_fc1[None], proj_bundle))
    far_tokens = other_tokens(tokens, proj_bundle)
    full_qkv = placed_rows(gather_rest(qkv_bundle), here, "place_qkv", 0)
    mine = swap_core(proj_bundle)

    first = jnp.where(spot % 2 == 0, proj_bundle, mine)[:, -EXTRA:]
    second = jnp.where(spot % 2 == 0, mine, proj_bundle)[:, -EXTRA:]
    smalls = jnp.stack([first, second], axis=1).reshape(fsdp, EXTRA, block).astype(jnp.float32)
    vectors = [smalls[:, i].reshape(-1) for i in range(6)]
    gain_one, shift_one, bias_proj, gain_two, shift_two, bias_fc2 = vectors
    qv_rows = smalls[:, 6 : 6 + qv_lines].reshape(fsdp, 2, local_heads, HD // fsdp)
    qv_rows = qv_rows.transpose(1, 2, 0, 3).reshape(2, local_width)
    bias_fc1 = smalls[:, 6 + qv_lines : 6 + qv_lines + fc1_size // block]
    bias_fc1 = bias_fc1.reshape(fsdp, units // HD, HD // fsdp).transpose(1, 0, 2).reshape(1, -1)
    bias_qkv = jnp.concatenate([qv_rows[0], jnp.zeros_like(qv_rows[0]), qv_rows[1]])
    lines = jnp.stack([bias_proj, gain_two, shift_two, gain_one])

    def project(rows):
        normed = layer_norm(rows.astype(jnp.float32), gain_one, shift_one).astype(jnp.bfloat16)
        result = jnp.einsum("sld,de->sle", normed, full_qkv, preferred_element_type=jnp.float32)
        return normed, (result + bias_qkv).astype(jnp.bfloat16)

    normed_one, triple = project(tokens)
    _, far_triple = project(far_tokens)
    proj_bundles = gather_rest(proj_bundle, triple, near=mine)
    fc2_bundle = jnp.stack(after(tuple(fc2_pieces), full_qkv))
    fc2_near = swap_core(fc2_bundle)
    attended, logs = [], []
    for index in sequences:
        gate = [attended[-1], fc2_near] if index else [fc2_bundle, proj_bundles[-1]]
        heads, log = attention_forward(triple, far_triple, after(place, *gate), pictures, index)
        attended.append(heads)
        logs.append(log)
    tp_attended = [swap_tp(heads) for heads in attended]
    tp_attended[0] = after(tp_attended[0], attended[-1])
    fc1_bundle = after(fc1_bundle, attended[0])
    fc1_bundles = [fc1_bundle, swap_core(fc1_bundle)]
    fc2_bundles = gather_rest(fc2_bundle, tp_attended[0], near=fc2_near)
    all_attended = jnp.stack(attended)
    weights = [proj_bundles, fc1_bundles, fc2_bundles]
    if block % PAIR:
        order = lax.rem(here[0] + chips - jnp.arange(chips, dtype=jnp.int32), chips)
        weights = [
            [placed_columns_plain([b[:, :-EXTRA] for b in proj_bundles], here)],
            fc1_bundles,
            [placed_columns_plain([b[order] for b in fc2_bundles], here)],
        ]
    all_logs = jnp.stack(logs)
    residuals, normed_two, actives, hidden_grads, feeds, backs, swapped_twos = [], [], [], [], [], [], []
    hidden_sums = 0.0
    for index in sequences:
        gate = [backs[-1], tp_attended[index]] if index else []
        residual, normed, active, hidden_grad, feed, back, hidden_sum, own_proj = feed_forward(
            attended[index],
            after(tp_attended[index], *backs[-1:]),
            tokens,
            out_grad,
            lines,
            bias_fc1,
            weights,
            after(here, *gate),
            index,
        )
        residuals.append(residual)
        normed_two.append(normed)
        actives.append(active)
        hidden_grads.append(hidden_grad)
        feeds.append(feed)
        backs.append(back)
        swapped_twos.append(swap_tp(back))
        hidden_sums = hidden_sums + hidden_sum[0]
        if index == 0:
            far_logs = other_ctx(after(all_logs, back), 3)
            far_attended = other_ctx(after(all_attended, far_logs), 1)

    fc2_groups = [([(out_grad, s) for s in sequences], actives)]
    fc1_groups = [([(normed[None], 0) for normed in normed_two], hidden_grads)]
    branches, head_grads, far_head_grads = [], [], []
    two_sums = 0.0
    gate = backs[-1]
    for index in sequences:
        branch, head_grad, two_sum = norm_two_backward(
            backs[index],
            swapped_twos[index],
            residuals[index],
            out_grad,
            lines,
            own_proj,
            after(here, gate),
            index,
        )
        branches.append(branch)
        head_grads.append(head_grad)
        far_head_grads.append(other_ctx(head_grad, 0))
        two_sums = two_sums + two_sum
        if index == 0:
            blocks_fc2 = gradient_blocks(fc2_groups, after(here, head_grad), "grad_fc2")
            gate = blocks_fc2[1]
    cross_fc2 = cross_ctx(*blocks_fc2, head_grads[-1])
    fc1_groups.append(([(branch[None], 0) for branch in branches], attended))
    blocks_fc1 = gradient_blocks(
        fc1_groups, after(here, cross_fc2[1], far_attended, far_logs), "grad_fc1_proj"
    )

    grad_triples, back_ones, swapped_ones, outputs = [], [], [], []
    one_sums, triple_sums = 0.0, 0.0
    gate = (blocks_fc1[1],)
    for index in sequences:
        if index == 0:
            feed = after(feeds[0], *gate)
            swapped_feed = swap_tp(feed)
        grad_triple = attention_backward(
            (triple, attended[index], head_grads[index], logs[index]),
            (far_triple, far_attended[index], far_head_grads[index], far_logs[index]),
            after(place, *gate),
            pictures,
            index,
        )
        gate = (grad_triple,)
        if index == 0:
            gate, arrived_fc2 = cross_chips(cross_fc2, grad_triple)
            cross_fc1 = cross_ctx(*blocks_fc1, gate)
            gate = (cross_fc1[1],)
        grad_triples.append(grad_triple)
        if index == seq_count - 1:
            total_fc2 = spread_chips(after(arrived_fc2, grad_triple))
            part_fc1, arrived_fc1 = cross_chips(cross_fc1, total_fc2)
            last_groups = [([(normed_one, s) for s in sequences], grad_triples)]
            blocks_last = gradient_blocks(last_groups, after(here, part_fc1), "grad_last")
            gate = (blocks_last[1], *swapped_ones)
        back_one, one_sum, triple_sum = qkv_backward(
            grad_triple, tokens, full_qkv, after(here, *gate), index
        )
        gate = (back_one, swapped_feed)
        back_ones.append(back_one)
        swapped_ones.append(swap_tp(back_one))
        one_sums = one_sums + one_sum
        triple_sums = triple_sums + triple_sum[0]

    def finish_output(index, mine, theirs):
        total = mine.astype(jnp.float32) + theirs.astype(jnp.float32)
        outputs.append((residuals[index] + total + bias_fc2).astype(jnp.bfloat16))

    finish_output(0, feed, after(swapped_feed, back_ones[-1]))
    last_feeds = [after(feeds[index], back_ones[0]) for index in range(1, seq_count)]
    last_swapped = [swap_tp(feed) for feed in last_feeds]

    out_sums = jnp.sum(out_grad.astype(jnp.float32), axis=(0, 1))
    grad_qv = jnp.concatenate([triple_sums[:local_width], triple_sums[2 * local_width :]])
    vectors = [one_sums[0], one_sums[1], two_sums[2], two_sums[0], two_sums[1], out_sums]
    packed = jnp.concatenate(
        [vector.reshape(fsdp, block) for vector in vectors]
        + [
            grad_qv.reshape(2, local_heads, fsdp, HD // fsdp)
            .transpose(2, 0, 1, 3)
            .reshape(fsdp, -1),
            hidden_sums.reshape(-1, fsdp, HD // fsdp).transpose(1, 0, 2).reshape(fsdp, -1),
        ],
        axis=1,
    )
    def norm_one(index, *gate):
        return norm_one_backward(
            back_ones[index],
            swapped_ones[index],
            tokens,
            branches[index],
            lines,
            after(here, *gate),
            index,
        )

    total_fc1 = spread_chips(after(arrived_fc1, back_ones[-1]))
    cross_last = cross_ctx(*blocks_last, back_ones[-1])
    grad_tokens = [norm_one(0, cross_last[1])]
    part_last, arrived_last = cross_chips(cross_last, grad_tokens[0])
    for index in range(1, seq_count):
        finish_output(index, last_feeds[index - 1], after(last_swapped[index - 1], part_last))
    for index in range(1, seq_count):
        grad_tokens.append(norm_one(index, part_last, *last_swapped))
    sums_fc2 = spread_end(after(total_fc2, part_last), 2)
    sums_fc1 = spread_end(after(total_fc1, part_last), 2)
    total_last = spread_chips(arrived_last)
    sums_last = spread_end(total_last, 2)
    small = sum_lines(after(packed, part_last).reshape(chips, 2, -1), spot)
    norm_one = small[: 2 * block].astype(jnp.bfloat16)
    norm_one = norm_one.astype(jnp.float32) + swap_tp(norm_one).astype(jnp.float32)
    vectors = [norm_one[:block], norm_one[block:]]
    vectors += [small[i * block : (i + 1) * block] for i in range(2, 6)]
    shard_qv = small[6 * block : 6 * block + qv_size].reshape(qv_bias.shape)
    shard_fc1_bias = small[6 * block + qv_size :][:fc1_size].reshape(fc1_bias.shape)
    sums_last = sums_last.reshape(block, -1).astype(jnp.float32)
    sums_fc1 = sums_fc1.reshape(block, -1).astype(jnp.float32)
    return (
        jnp.stack(outputs),
        jnp.stack(grad_tokens),
        vectors[0],
        vectors[1],
        sums_last.reshape(-1, 3, local_width),
        shard_qv,
        sums_fc1[:, units:].T,
        vectors[2],
        vectors[3],
        vectors[4],
        sums_fc1[:, :units],
        shard_fc1_bias,
        sums_fc2.reshape(block, -1).astype(jnp.float32).T,
        vectors[5],
    )


def solution(mesh):
    return jax.shard_map(
        body,
        mesh=mesh,
        in_specs=(
            P("fsdp", "ctx", None),
            P("fsdp", None),
            P("fsdp"),
            P("fsdp"),
            P("fsdp", None, "tp"),
            P(None, "tp", "fsdp"),
            P("tp", "fsdp"),
            P("fsdp"),
            P("fsdp"),
            P("fsdp"),
            P("fsdp", "tp"),
            P("tp", "fsdp"),
            P("tp", "fsdp"),
            P("fsdp"),
            P("fsdp", "ctx", None),
        ),
        out_specs=(
            P("fsdp", "ctx", None),
            P("fsdp", "ctx", None),
            P("fsdp"),
            P("fsdp"),
            P("fsdp", None, "tp"),
            P(None, "tp", "fsdp"),
            P("tp", "fsdp"),
            P("fsdp"),
            P("fsdp"),
            P("fsdp"),
            P("fsdp", "tp"),
            P("tp", "fsdp"),
            P("tp", "fsdp"),
            P("fsdp"),
        ),
        check_vma=False,
    )
```

```python
import jax
import jax.numpy as jnp
from jax import lax
from jax.experimental import pallas as pl
from jax.experimental.pallas import tpu as pltpu
from jax.sharding import PartitionSpec as P

HD = 64
PAIR = 2 * HD
PIECE = 256
SCALE = HD ** (-0.5)
KERNEL_VMEM = 56 * 1024 * 1024

epsilon = 1e-05
masked_value = -1e30


def layer_norm(values, gain_vec, shift_vec):
    average = jnp.mean(values, axis=-1, keepdims=True)
    centred = values - average
    variance = jnp.mean(centred * centred, axis=-1, keepdims=True)
    return centred * lax.rsqrt(variance + epsilon) * gain_vec + shift_vec


NT = (((1,), (1,)), ((), ()))


def dot_nt(left, right):
    return lax.dot_general(left, right, NT, preferred_element_type=jnp.float32)


def dot_nn(left, right):
    return jnp.dot(left, right, preferred_element_type=jnp.float32)


def head_lanes(head):
    lanes = lax.broadcasted_iota(jnp.int32, (1, PAIR), 1)
    return (lanes >= head * HD) & (lanes < (head + 1) * HD)


def only_head(rows, head):
    return jnp.where(head_lanes(head), rows, jnp.zeros_like(rows))


def diagonal_mask(scores, joined):
    key_row = lax.broadcasted_iota(jnp.int32, scores.shape, 0)
    query_lane = lax.broadcasted_iota(jnp.int32, scores.shape, 1)
    return (key_row <= query_lane) | joined


def chunk_start(step, place, local_len, chunks):
    return 0 if chunks == 1 else pl.multiple_of(step * local_len, local_len)


SCORE_TILE = 32


def score_tiles(count):
    return [slice(start, start + SCORE_TILE) for start in range(0, count, SCORE_TILE)]


def folded(rows, combine):
    parts = [rows[start : start + 8] for start in range(0, rows.shape[0], 8)]
    while len(parts) > 1:
        parts = [
            combine(parts[i], parts[i + 1]) if i + 1 < len(parts) else parts[i]
            for i in range(0, len(parts), 2)
        ]
    return parts[0]


def attention_forward_kernel(
    place, pictures, q_ref, k_ref, v_ref, k_far, v_far, out_ref, log_ref, scores, weights, values
):
    rank = place[0]
    sequence = place[2]
    local_len = q_ref.shape[1]
    blocks = local_len // PIECE
    chunks = k_far.shape[1] // local_len
    values[...] = v_ref[0].T
    states = [(head, block) for head in range(2) for block in range(blocks)]
    scaled, peaks = [], []
    for index, (head, block) in enumerate(states):
        query = only_head(q_ref[0, block * PIECE : (block + 1) * PIECE, :] * SCALE, head)
        scaled.append(query)
        joined = pictures[sequence, rank * blocks + block] > 0
        count = (block + 1) * PIECE
        scores[index, :count] = dot_nt(k_ref[0, :count], query)
        peak = jnp.full((8, PIECE), masked_value, jnp.float32)
        for tile in score_tiles(count):
            part = scores[index, tile]
            if tile.start >= block * PIECE:
                key_row = lax.broadcasted_iota(jnp.int32, part.shape, 0) + (
                    tile.start - block * PIECE
                )
                lane = lax.broadcasted_iota(jnp.int32, part.shape, 1)
                part = jnp.where((key_row <= lane) | joined, part, masked_value)
                scores[index, tile] = part
            peak = jnp.maximum(peak, folded(part, jnp.maximum))
        peaks.append(peak)

    def far_scores(step, carried):
        keys = k_far[0, pl.ds(chunk_start(step, place, local_len, chunks), local_len), :]
        base = pl.multiple_of((step + 1) * local_len, local_len)
        after = []
        for index, peak in enumerate(carried):
            part = dot_nt(keys, scaled[index])
            scores[index, pl.ds(base, local_len)] = part
            for tile in score_tiles(local_len):
                peak = jnp.maximum(peak, folded(part[tile], jnp.maximum))
            after.append(peak)
        return after

    peaks = lax.fori_loop(0, rank, far_scores, peaks)
    peaks = [jnp.max(peak, axis=0, keepdims=True) for peak in peaks]
    gathered = []
    for index, (head, block) in enumerate(states):
        count = (block + 1) * PIECE
        total = jnp.zeros((8, PIECE), jnp.float32)
        for tile in score_tiles(count):
            weight = jnp.exp(scores[index, tile] - peaks[index])
            total = total + folded(weight, jnp.add)
            weights[index, tile] = weight.astype(jnp.bfloat16)
        gathered.append(
            (total, dot_nn(values[head * HD : (head + 1) * HD, :count], weights[index, :count]))
        )

    def far_values(step, carried):
        base = pl.multiple_of((step + 1) * local_len, local_len)
        far = v_far[0, pl.ds(chunk_start(step, place, local_len, chunks), local_len), :].T
        after = []
        for index, (total, sums) in enumerate(carried):
            head = states[index][0]
            for tile in score_tiles(local_len):
                weight = jnp.exp(
                    scores[index, pl.ds(base + tile.start, SCORE_TILE)] - peaks[index]
                )
                total = total + folded(weight, jnp.add)
                weights[index, tile] = weight.astype(jnp.bfloat16)
            sums = sums + dot_nn(far[head * HD : (head + 1) * HD], weights[index])
            after.append((total, sums))
        return after

    gathered = lax.fori_loop(0, rank, far_values, gathered)
    for block in range(blocks):
        rows = slice(block * PIECE, (block + 1) * PIECE)
        halves = []
        for head in range(2):
            index = head * blocks + block
            total = jnp.sum(gathered[index][0], axis=0, keepdims=True)
            halves.append(gathered[index][1] / total)
            log_ref[0, head : head + 1, rows] = peaks[index] + jnp.log(total)
        out_ref[rows, :] = jnp.concatenate(halves, axis=0).T.astype(out_ref.dtype)


def attention_forward(triple, far, place, pictures, index):
    place = jnp.concatenate([place, jnp.full((1,), index, jnp.int32)])
    _, local_len, triple_width = triple.shape
    far_len = far.shape[1]
    local_width = triple_width // 3
    pairs = local_width // PAIR

    def part(length, offset):
        return pl.BlockSpec(
            (1, length, PAIR), lambda p, place, pics: (index, 0, offset * pairs + p)
        )

    return pl.pallas_call(
        attention_forward_kernel,
        grid_spec=pltpu.PrefetchScalarGridSpec(
            num_scalar_prefetch=2,
            grid=(pairs,),
            in_specs=[
                part(local_len, 0),
                part(local_len, 1),
                part(local_len, 2),
                part(far_len, 1),
                part(far_len, 2),
            ],
            out_specs=[
                pl.BlockSpec((local_len, PAIR), lambda p, place, pics: (0, p)),
                pl.BlockSpec((1, 2, local_len), lambda p, place, pics: (p, 0, 0)),
            ],
            scratch_shapes=[
                pltpu.VMEM((2 * local_len // PIECE, local_len + far_len, PIECE), jnp.float32),
                pltpu.VMEM((2 * local_len // PIECE, local_len, PIECE), jnp.bfloat16),
                pltpu.VMEM((PAIR, local_len), jnp.bfloat16),
            ],
        ),
        out_shape=[
            jax.ShapeDtypeStruct((local_len, local_width), jnp.bfloat16),
            jax.ShapeDtypeStruct((pairs, 2, local_len), jnp.float32),
        ],
        compiler_params=pltpu.CompilerParams(vmem_limit_bytes=KERNEL_VMEM),
        cost_estimate=pl.CostEstimate(flops=50000000000, bytes_accessed=0, transcendentals=0),
        name="attention_forward",
    )(place, pictures, triple, triple, triple, far, far)


def attention_backward_kernel(
    place,
    pictures,
    q_ref,
    k_ref,
    v_ref,
    out_ref,
    grad_ref,
    log_ref,
    q_far,
    k_far,
    v_far,
    out_far,
    grad_far,
    log_far,
    triple_ref,
):
    rank = place[0]
    ranks = place[1]
    sequence = place[2]
    pair = pl.program_id(0)
    local_len = triple_ref.shape[0]
    local_width = triple_ref.shape[1] // 3
    blocks = local_len // PIECE
    chunks = k_far.shape[1] // local_len

    def sides_of(queries, grads, outs, logs):
        turned = (grads.astype(jnp.float32) * outs.astype(jnp.float32)).T
        queries = queries * SCALE
        sides = []
        for head in range(2):
            delta = jnp.sum(turned[head * HD : (head + 1) * HD], axis=0, keepdims=True)
            sides.append(
                (
                    only_head(queries, head),
                    only_head(grads, head),
                    logs[head : head + 1],
                    delta,
                )
            )
        return sides

    def pieces(keys, values, query, grad, log, delta, mask=None):
        scores = dot_nt(keys, query)
        probs = jnp.exp(scores - log)
        if mask is not None:
            probs = jnp.where(mask(probs), probs, 0.0)
        grad_probs = dot_nt(values, grad)
        return probs, (probs * (grad_probs - delta)).astype(jnp.bfloat16)

    key_own = k_ref[0]
    value_own = v_ref[0]
    key_turned = key_own.T
    sides = sides_of(q_ref[0], grad_ref[...], out_ref[...], log_ref[0])
    grad_keys = [None] * blocks
    grad_values = [None] * blocks
    grad_queries = []

    def add(total, part):
        return part if total is None else total + part

    for head in range(2):
        queries, grads, logs, deltas = sides[head]
        for block in range(blocks):
            rows = slice(block * PIECE, (block + 1) * PIECE)
            joined = pictures[sequence, rank * blocks + block] > 0
            grad_query = None
            for key_block in range(block + 1):
                key_rows = slice(key_block * PIECE, (key_block + 1) * PIECE)
                mask = (lambda p, j=joined: diagonal_mask(p, j)) if key_block == block else None
                probs, grad_scores = pieces(
                    key_own[key_rows],
                    value_own[key_rows],
                    queries[rows],
                    grads[rows],
                    logs[:, rows],
                    deltas[:, rows],
                    mask,
                )
                grad_values[key_block] = add(
                    grad_values[key_block], dot_nn(probs.astype(jnp.bfloat16), grads[rows])
                )
                grad_keys[key_block] = add(
                    grad_keys[key_block], dot_nn(grad_scores, queries[rows])
                )
                grad_query = add(
                    grad_query,
                    dot_nn(key_turned[head * HD : (head + 1) * HD, key_rows], grad_scores),
                )
            grad_queries.append(grad_query)

    def earlier(step, carried):
        start = chunk_start(step, place, local_len, chunks)
        keys = k_far[0, pl.ds(start, local_len), :]
        values = v_far[0, pl.ds(start, local_len), :]
        turned = keys.T
        after = []
        for index, total in enumerate(carried):
            head, block = index // blocks, index % blocks
            rows = slice(block * PIECE, (block + 1) * PIECE)
            queries, grads, logs, deltas = sides[head]
            _, grad_scores = pieces(
                keys, values, queries[rows], grads[rows], logs[:, rows], deltas[:, rows]
            )
            after.append(total + dot_nn(turned[head * HD : (head + 1) * HD], grad_scores))
        return after

    grad_queries = lax.fori_loop(0, rank, earlier, grad_queries)
    for block in range(blocks):
        rows = slice(block * PIECE, (block + 1) * PIECE)
        both = jnp.concatenate([grad_queries[head * blocks + block] for head in range(2)], axis=0)
        triple_ref[rows, pl.ds(pl.multiple_of(pair * PAIR, PAIR), PAIR)] = (
            (both * SCALE).T.astype(triple_ref.dtype)
        )

    def later(step, carried):
        start = chunk_start(step, place, local_len, chunks)
        window = pl.ds(start, local_len)
        sides = sides_of(
            q_far[0, window, :], grad_far[window, :], out_far[window, :], log_far[0, :, window]
        )
        keys_after, values_after = list(carried[0]), list(carried[1])
        for head in range(2):
            queries, grads, logs, deltas = sides[head]
            for block in range(blocks):
                rows = slice(block * PIECE, (block + 1) * PIECE)
                probs, grad_scores = pieces(
                    key_own[rows], value_own[rows], queries, grads, logs, deltas
                )
                values_after[block] = values_after[block] + dot_nn(
                    probs.astype(jnp.bfloat16), grads
                )
                keys_after[block] = keys_after[block] + dot_nn(grad_scores, queries)
        return keys_after, values_after

    grad_keys, grad_values = lax.fori_loop(rank + 1, ranks, later, (grad_keys, grad_values))
    for block in range(blocks):
        rows = slice(block * PIECE, (block + 1) * PIECE)
        for part, grads in ((1, grad_keys), (2, grad_values)):
            column = pl.multiple_of(part * local_width + pair * PAIR, PAIR)
            triple_ref[rows, pl.ds(column, PAIR)] = grads[block].astype(triple_ref.dtype)


def attention_backward(own, other, place, pictures, index):
    place = jnp.concatenate([place, jnp.full((1,), index, jnp.int32)])
    _, local_len, triple_width = own[0].shape
    pairs = triple_width // (3 * PAIR)
    specs = []
    for length in (local_len, other[0].shape[1]):
        for offset in range(3):
            specs.append(
                pl.BlockSpec(
                    (1, length, PAIR),
                    lambda p, place, pics, offset=offset: (index, 0, offset * pairs + p),
                )
            )
        specs += [pl.BlockSpec((length, PAIR), lambda p, place, pics: (0, p))] * 2
        specs.append(pl.BlockSpec((1, 2, length), lambda p, place, pics: (p, 0, 0)))
    return pl.pallas_call(
        attention_backward_kernel,
        grid_spec=pltpu.PrefetchScalarGridSpec(
            num_scalar_prefetch=2,
            grid=(pairs,),
            in_specs=specs,
            out_specs=pl.BlockSpec((local_len, triple_width), lambda p, place, pics: (0, 0)),
        ),
        out_shape=jax.ShapeDtypeStruct((local_len, triple_width), jnp.bfloat16),
        compiler_params=pltpu.CompilerParams(vmem_limit_bytes=KERNEL_VMEM),
        cost_estimate=pl.CostEstimate(flops=50000000000, bytes_accessed=0, transcendentals=0),
        name="attention_backward",
    )(place, pictures, *([own[0]] * 3), *own[1:], *([other[0]] * 3), *other[1:])


def core_swap():
    return [(place, place ^ 1) for place in range(lax.axis_size("fsdp"))]


PAIR_SWAP = [(0, 1), (1, 0)]


def swap_core(rows):
    return lax.ppermute(rows, "fsdp", core_swap())


def swap_ctx(rows):
    return lax.ppermute(rows, "ctx", PAIR_SWAP)


def swap_tp(rows):
    return lax.ppermute(rows, "tp", PAIR_SWAP)


def exchange_chips(rows):
    fsdp = lax.axis_size("fsdp")
    groups = [list(range(core, fsdp, 2)) for core in range(2)]
    return lax.all_to_all(
        rows, "fsdp", split_axis=0, concat_axis=0, tiled=True, axis_index_groups=groups
    )


def pick(array, index, axis):
    return lax.dynamic_index_in_dim(array, index, axis, keepdims=False)


def after(value, *others):
    return lax.optimization_barrier((value, *others))[0]


def halves_of(shard):
    halves = 2 if lax.axis_size("ctx") == 2 else 1
    return shard.reshape(halves, -1, shard.shape[1])


def gather_chips(halves):
    chips = lax.axis_size("fsdp") // 2
    part = pick(halves, lax.axis_index("ctx"), 0) if halves.shape[0] == 2 else halves[0]
    return exchange_chips(jnp.broadcast_to(part, (chips, *part.shape)))


def chip_shift(step):
    chips = lax.axis_size("fsdp") // 2
    return [
        (2 * chip + core, 2 * ((chip + step) % chips) + core)
        for chip in range(chips)
        for core in range(2)
    ]


def shift_chips(halves):
    part = pick(halves, lax.axis_index("ctx"), 0) if halves.shape[0] == 2 else halves[0]
    chips = lax.axis_size("fsdp") // 2
    return [part] + [lax.ppermute(part, "fsdp", chip_shift(step)) for step in range(1, chips)]


def gather_rest(bundle, *gate, near=None):
    bundles = [bundle, swap_core(bundle) if near is None else near]
    if lax.axis_size("ctx") == 2:
        across = after(swap_ctx(bundle), *gate)
        bundles += [across, swap_core(across)]
    return bundles


def kernel_call(kernel, scalars, arrays, in_specs, outs, out_specs, grid, name, scratch=(), flops=0):
    size = sum(array.size for array in arrays)
    return pl.pallas_call(
        kernel,
        grid_spec=pltpu.PrefetchScalarGridSpec(
            num_scalar_prefetch=len(scalars),
            grid=(grid,),
            in_specs=in_specs,
            out_specs=out_specs,
            scratch_shapes=list(scratch),
        ),
        out_shape=[jax.ShapeDtypeStruct(shape, dtype) for shape, dtype in outs],
        compiler_params=pltpu.CompilerParams(vmem_limit_bytes=KERNEL_VMEM),
        cost_estimate=pl.CostEstimate(flops=50000000000, bytes_accessed=0, transcendentals=0),
        name=name,
    )(*scalars, *arrays)


def owners(here, sides):
    for index in range(2 * sides):
        core = here[1] if index % 2 == 0 else 1 - here[1]
        yield core, ((here[2] if index < 2 else 1 - here[2]) if sides == 2 else 0)


def placed_rows(bundles, here, name, extra):
    fsdp = lax.axis_size("fsdp")
    sides = len(bundles) // 2
    chips, total, width = bundles[0].shape
    height = total - extra
    chunk = 512

    def kernel(here, *refs):
        for index, (core, side) in enumerate(owners(here, sides)):
            for chip in range(chips):
                refs[-1][(2 * chip + core) * sides + side] = refs[index][chip, :height]

    (result,) = kernel_call(
        kernel,
        [here],
        bundles,
        [pl.BlockSpec((chips, total, chunk), lambda i, here: (0, 0, i))] * (2 * sides),
        [((fsdp * sides, height, width), jnp.bfloat16)],
        [pl.BlockSpec((fsdp * sides, height, chunk), lambda i, here: (0, 0, i))],
        width // chunk,
        name,
    )
    return result.reshape(-1, width)


def placed_columns_plain(bundles, here):
    sides = []
    for mine, other in zip(bundles[::2], bundles[1::2]):
        first = jnp.where(here[1] == 0, mine, other)
        second = jnp.where(here[1] == 0, other, mine)
        both = jnp.stack([first, second], axis=1)
        sides.append(both.reshape(-1, *both.shape[2:]))
    if len(sides) == 2:
        sides = [
            jnp.where(here[2] == 0, sides[0], sides[1]),
            jnp.where(here[2] == 0, sides[1], sides[0]),
        ]
    fsdp, _, width = sides[0].shape
    return jnp.concatenate(sides, axis=1).transpose(1, 0, 2).reshape(-1, fsdp * width)


def weight_copies(bundles, target, here, columns, shifted=False):
    if len(bundles) == 1:
        yield bundles[0], target
        return
    sides = len(bundles) // 2
    for index, (core, side) in enumerate(owners(here, sides)):
        chips, _, width = bundles[index].shape
        height = target.shape[0] // (sides if columns else 2 * chips * sides)
        for chip in range(chips):
            source = bundles[index].at[chip, pl.ds(0, height)]
            block = 2 * (lax.rem(here[0] + chips - chip, chips) if shifted else chip) + core
            if columns:
                across = pl.ds(pl.multiple_of(block * width, width), width)
                yield source, target.at[pl.ds(pl.multiple_of(side * height, height), height), across]
            else:
                row = pl.multiple_of((block * sides + side) * height, height)
                yield source, target.at[pl.ds(row, height)]


UNITS = 1024
TILE = 16
ROOT = 0.7978845608028654
CUBIC = 0.044715


def feed_kernel(counts, here, *refs):
    own_ref, tp_ref, tokens_ref, grad_ref, vector_ref, bias_ref = refs[:6]
    at = 6
    bundles = []
    for count in counts:
        bundles.append(refs[at : at + count])
        at += count
    residual_ref, normed_ref, active_ref, hidden_ref, feed_ref, back_ref, sum_ref, proj_ref = refs[
        at : at + 8
    ]
    proj, first, second, feed, back, hidden_pre, grad_active, semaphores = refs[at + 8 :]
    step = pl.program_id(0)
    copies = [
        weight_copies(bundles[0], proj, here, True),
        weight_copies(bundles[1], first, here, False),
        weight_copies(bundles[2], second, here, True, True),
    ]
    made, number = [], 0
    for group in copies:
        made.append([])
        for source, place in group:
            made[-1].append(pltpu.make_async_copy(source, place, semaphores.at[number]))
            number += 1
    rows = proj.shape[0] // 2
    kept = pltpu.make_async_copy(
        proj.at[pl.ds(pl.multiple_of(here[3] * rows, rows), rows)],
        proj_ref,
        semaphores.at[number],
    )

    @pl.when(step == 0)
    def _():
        for group in made:
            for copy in group:
                copy.start()
        for copy in made[0]:
            copy.wait()
        kept.start()
        leading = here[3] == 0
        low = jnp.where(leading, own_ref[...], tp_ref[...])
        high = jnp.where(leading, tp_ref[...], own_ref[...])
        feed[...] = dot_nn(low, proj[:rows]) + dot_nn(high, proj[rows:])
        for start in range(0, feed.shape[0], TILE):
            lines = slice(start, start + TILE)
            residual = tokens_ref[0, lines].astype(jnp.float32) + feed[lines] + vector_ref[0:1]
            residual_ref[lines] = residual
            unit, _ = centred_rows(residual)
            normed_ref[lines] = (unit * vector_ref[1:2] + vector_ref[2:3]).astype(
                normed_ref.dtype
            )
        for copy in made[1]:
            copy.wait()

    units = pl.ds(pl.multiple_of(step * UNITS, UNITS), UNITS)
    hidden_pre[...] = dot_nn(normed_ref[...], first[:, units])

    @pl.when(step == 0)
    def _():
        for copy in made[2]:
            copy.wait()
        kept.wait()

    grad_active[...] = dot_nt(grad_ref[0], second[units])
    totals = jnp.zeros((TILE, UNITS), jnp.float32)
    for start in range(0, feed.shape[0], TILE):
        lines = slice(start, start + TILE)
        hidden = hidden_pre[lines] + bias_ref[...]
        square = hidden * hidden
        bent = jnp.tanh(hidden * (ROOT + ROOT * CUBIC * square))
        share = 0.5 + 0.5 * bent
        active_ref[lines] = (hidden * share).astype(jnp.bfloat16)
        slope = share + hidden * (1.0 - bent * bent) * (
            0.5 * ROOT + 1.5 * ROOT * CUBIC * square
        )
        grad_hidden = (grad_active[lines] * slope).astype(jnp.bfloat16)
        hidden_ref[lines] = grad_hidden
        totals = totals + grad_hidden.astype(jnp.float32)
    sum_ref[...] = jnp.sum(totals, axis=0, keepdims=True)
    active = active_ref[...]
    feed_part = dot_nn(active, second[units])
    back_part = dot_nt(hidden_ref[...], first[:, units])

    @pl.when(step == 0)
    def _():
        feed[...] = feed_part
        back[...] = back_part

    @pl.when(step > 0)
    def _():
        feed[...] += feed_part
        back[...] += back_part

    @pl.when(step == pl.num_programs(0) - 1)
    def _():
        feed_ref[...] = feed[...].astype(feed_ref.dtype)
        back_ref[...] = back[...].astype(back_ref.dtype)


def feed_forward(own, tp, tokens, out_grad, vectors, bias, weights, here, index):
    local_len, local_width = own.shape
    width = tokens.shape[2]
    units = bias.shape[1]
    counts = tuple(len(group) for group in weights)
    copies = sum(1 if len(group) == 1 else len(group) * group[0].shape[0] for group in weights)
    whole = lambda shape: pl.BlockSpec(shape, lambda j, here: (0,) * len(shape))
    row = pl.BlockSpec((1, local_len, width), lambda j, here: (index, 0, 0))
    block = pl.BlockSpec((local_len, UNITS), lambda j, here: (0, j))
    line = pl.BlockSpec((1, UNITS), lambda j, here: (0, j))
    flat = [array for group in weights for array in group]
    half, full = jnp.bfloat16, jnp.float32
    return kernel_call(
        lambda *refs: feed_kernel(counts, *refs),
        [here],
        [own, tp, tokens, out_grad, vectors, bias] + flat,
        [whole(own.shape), whole(own.shape), row, row, whole(vectors.shape), line]
        + [pl.BlockSpec(memory_space=pl.ANY)] * len(flat),
        [
            ((local_len, width), full),
            ((local_len, width), half),
            ((local_len, units), half),
            ((local_len, units), half),
            ((local_len, width), half),
            ((local_len, width), half),
            ((1, units), full),
            ((local_width, width), half),
        ],
        [whole((local_len, width)), whole((local_len, width)), block, block]
        + [whole((local_len, width)), whole((local_len, width)), line]
        + [pl.BlockSpec(memory_space=pl.ANY)],
        units // UNITS,
        "feed_forward",
        [
            pltpu.VMEM((2 * local_width, width), half),
            pltpu.VMEM((width, units), half),
            pltpu.VMEM((units, width), half),
            pltpu.VMEM((local_len, width), full),
            pltpu.VMEM((local_len, width), full),
            pltpu.VMEM((local_len, UNITS), full),
            pltpu.VMEM((local_len, UNITS), full),
            pltpu.SemaphoreType.DMA((copies + 1,)),
        ],
        flops=8 * local_len * width * units,
    )


ROWS = 256


def centred_rows(rows):
    average = jnp.mean(rows, axis=-1, keepdims=True)
    centred = rows - average
    spread = lax.rsqrt(jnp.mean(centred * centred, axis=-1, keepdims=True) + epsilon)
    return centred * spread, spread


def through_norm(grads, unit, spread, gain):
    scaled = grads * gain
    return spread * (
        scaled
        - jnp.mean(scaled, axis=-1, keepdims=True)
        - unit * jnp.mean(scaled * unit, axis=-1, keepdims=True)
    )


def accumulate(ref, totals):
    total = jnp.concatenate([jnp.sum(lines, axis=0, keepdims=True) for lines in totals])

    @pl.when(pl.program_id(0) == 0)
    def _():
        ref[...] = total

    @pl.when(pl.program_id(0) > 0)
    def _():
        ref[...] += total


def tiles_of(count):
    return [slice(start, start + TILE) for start in range(0, count, TILE)]


def norm_two_kernel(
    here, own_ref, tp_ref, residual_ref, grad_ref, vector_ref, proj_ref, branch_ref, heads_ref, sum_ref
):
    totals = [jnp.zeros((TILE, own_ref.shape[1]), jnp.float32)] * 3
    for lines in tiles_of(own_ref.shape[0]):
        grads = own_ref[lines].astype(jnp.float32) + tp_ref[lines].astype(jnp.float32)
        unit, spread = centred_rows(residual_ref[lines])
        total = grad_ref[0, lines].astype(jnp.float32) + through_norm(
            grads, unit, spread, vector_ref[1:2]
        )
        branch = total.astype(jnp.bfloat16)
        branch_ref[lines] = branch
        totals = [
            totals[0] + grads * unit,
            totals[1] + grads,
            totals[2] + branch.astype(jnp.float32),
        ]
    heads_ref[...] = dot_nt(branch_ref[...], proj_ref[...]).astype(heads_ref.dtype)
    accumulate(sum_ref, totals)


def norm_two_backward(own, tp, residual, out_grad, vectors, proj, here, index):
    local_len, width = own.shape
    local_width = proj.shape[0]
    whole = lambda shape: pl.BlockSpec(shape, lambda i, here: (0,) * len(shape))
    row = pl.BlockSpec((ROWS, width), lambda i, here: (i, 0))
    return kernel_call(
        norm_two_kernel,
        [here],
        [own, tp, residual, out_grad, vectors, proj],
        [row, row, row, pl.BlockSpec((1, ROWS, width), lambda i, here: (index, i, 0))]
        + [whole(vectors.shape), whole(proj.shape)],
        [
            ((local_len, width), jnp.bfloat16),
            ((local_len, local_width), jnp.bfloat16),
            ((3, width), jnp.float32),
        ],
        [row, pl.BlockSpec((ROWS, local_width), lambda i, here: (i, 0)), whole((3, width))],
        local_len // ROWS,
        "norm_two_backward",
        flops=2 * local_len * width * local_width,
    )


def qkv_back_kernel(here, grad_ref, tokens_ref, weight_ref, back_ref, sum_ref, triple_ref, back):
    back[...] = dot_nt(grad_ref[...], weight_ref[...])
    totals = [jnp.zeros((TILE, back.shape[1]), jnp.float32)] * 2
    triple = jnp.zeros((TILE, grad_ref.shape[1]), jnp.float32)
    for lines in tiles_of(back.shape[0]):
        part = back[lines]
        back_ref[lines] = part.astype(back_ref.dtype)
        unit, _ = centred_rows(tokens_ref[0, lines].astype(jnp.float32))
        totals = [totals[0] + part * unit, totals[1] + part]
        triple = triple + grad_ref[lines].astype(jnp.float32)
    accumulate(sum_ref, totals)
    accumulate(triple_ref, [triple])


def qkv_backward(grad_triple, tokens, weight, here, index):
    local_len, triple_width = grad_triple.shape
    width = tokens.shape[2]
    whole = lambda shape: pl.BlockSpec(shape, lambda i, here: (0,) * len(shape))
    return kernel_call(
        qkv_back_kernel,
        [here],
        [grad_triple, tokens, weight],
        [
            pl.BlockSpec((ROWS, triple_width), lambda i, here: (i, 0)),
            pl.BlockSpec((1, ROWS, width), lambda i, here: (index, i, 0)),
            whole(weight.shape),
        ],
        [
            ((local_len, width), jnp.bfloat16),
            ((2, width), jnp.float32),
            ((1, triple_width), jnp.float32),
        ],
        [
            pl.BlockSpec((ROWS, width), lambda i, here: (i, 0)),
            whole((2, width)),
            whole((1, triple_width)),
        ],
        local_len // ROWS,
        "qkv_backward",
        [pltpu.VMEM((ROWS, width), jnp.float32)],
        flops=2 * local_len * width * triple_width,
    )


def norm_one_kernel(here, own_ref, tp_ref, tokens_ref, residual_ref, vector_ref, out_ref):
    for lines in tiles_of(own_ref.shape[0]):
        grads = own_ref[lines].astype(jnp.float32) + tp_ref[lines].astype(jnp.float32)
        unit, spread = centred_rows(tokens_ref[0, lines].astype(jnp.float32))
        out_ref[lines] = (
            residual_ref[lines].astype(jnp.float32)
            + through_norm(grads, unit, spread, vector_ref[3:4])
        ).astype(out_ref.dtype)


def norm_one_backward(own, tp, tokens, residual, vectors, here, index):
    local_len, width = own.shape
    row = pl.BlockSpec((ROWS, width), lambda i, here: (i, 0))
    return kernel_call(
        norm_one_kernel,
        [here],
        [own, tp, tokens, residual, vectors],
        [row, row, pl.BlockSpec((1, ROWS, width), lambda i, here: (index, i, 0)), row]
        + [pl.BlockSpec(vectors.shape, lambda i, here: (0, 0))],
        [((local_len, width), jnp.bfloat16)],
        [row],
        local_len // ROWS,
        "norm_one_backward",
    )[0]


CHUNK = 512


def gradient_kernel(plan, here, *refs):
    chips, groups = plan
    step = pl.program_id(0)
    refs = list(refs)
    turned = refs.pop()
    outs = [refs.pop(-2), refs.pop()]
    rows = outs[0].shape[2]
    at = 0
    for first, last, sequences in groups:
        lefts = refs[at : at + 2 * sequences * chips]
        rights = refs[at + 2 * sequences * chips : at + sequences * (2 * chips + 1)]
        at += sequences * (2 * chips + 1)

        @pl.when(step == first)
        def _():
            for index, left in enumerate(lefts):
                which, rest = divmod(index, sequences * chips)
                sequence, chip = divmod(rest, chips)
                block = left.shape[2]
                turned[which, sequence, chip * block : (chip + 1) * block] = left[0].T

        @pl.when((step >= first) & (step < last))
        def _():
            for which in range(2):
                total = dot_nn(turned[which, 0], rights[0][...])
                for sequence in range(1, sequences):
                    total += dot_nn(turned[which, sequence], rights[sequence][...])
                total = total.astype(jnp.bfloat16).reshape(chips, 2, rows, -1)
                for half in range(2):
                    outs[which][half] = total[:, half]


def gradient_plain(groups, here):
    chips = lax.axis_size("fsdp") // 2
    columns = []
    for lefts, rights in groups:
        total = 0.0
        for (array, lead), right in zip(lefts, rights):
            total = total + lax.dot_general(
                array[lead], right, (((0,), (0,)), ((), ())), preferred_element_type=jnp.float32
            )
        columns.append(total)
    whole = jnp.concatenate(columns, axis=1)
    whole = whole.astype(jnp.bfloat16).reshape(chips, 2, 2, -1, whole.shape[1])
    whole = whole.transpose(2, 1, 0, 3, 4)
    return pick(whole, 1 - here[1], 1), pick(whole, here[1], 1)


def gradient_blocks(groups, here, name):
    chips = lax.axis_size("fsdp") // 2
    if groups[0][0][0][0].shape[2] % (2 * chips * PAIR):
        return gradient_plain(groups, here)
    arrays, specs, plan = [], [], []
    at = 0
    for lefts, rights in groups:
        first, last = at, at + rights[0].shape[1] // CHUNK
        at = last
        plan.append((first, last, len(rights)))
        tokens = rights[0].shape[0]
        for own in (0, 1):
            for array, lead in lefts:
                block = array.shape[2] // (2 * chips)
                for chip in range(chips):
                    arrays.append(array)
                    specs.append(
                        pl.BlockSpec(
                            (1, tokens, block),
                            lambda i, here, lead=lead, chip=chip, own=own: (
                                lead,
                                0,
                                2 * chip + (here[1] if own else 1 - here[1]),
                            ),
                        )
                    )
        for right in rights:
            arrays.append(right)
            specs.append(
                pl.BlockSpec(
                    (tokens, CHUNK),
                    lambda i, here, first=first, last=last: (
                        0,
                        jnp.clip(i, first, last - 1) - first,
                    ),
                )
            )
    half = block // 2
    whole = pl.BlockSpec((2, chips, half, CHUNK), lambda i, here: (0, 0, 0, i))
    plan = (chips, plan)
    return kernel_call(
        lambda *refs: gradient_kernel(plan, *refs),
        [here],
        arrays,
        specs,
        [((2, chips, half, at * CHUNK), jnp.bfloat16)] * 2,
        [whole, whole],
        at,
        name,
        [pltpu.VMEM((2, len(groups[0][1]), chips * block, tokens), jnp.bfloat16)],
    )


def cross_ctx(sent, kept, gate):
    received = after(swap_core(sent), gate)
    halves = [None, None]
    side = lax.axis_index("ctx")
    for which in range(2):
        index = (which + side) % 2
        total = pick(kept, index, 0).astype(jnp.float32) + pick(received, index, 0).astype(
            jnp.float32
        )
        halves[which] = total
    if lax.axis_size("ctx") != 2:
        low = jnp.where(side % 2 == 0, halves[0], halves[1])
        high = jnp.where(side % 2 == 0, halves[1], halves[0])
        return jnp.concatenate([low, high], axis=1), sent, None
    away = halves[1].astype(jnp.bfloat16)
    return halves[0], away, swap_ctx(away)


def cross_chips(crossing, gate):
    mine, _, coming = crossing
    if coming is not None:
        mine = mine + after(coming, gate).astype(jnp.float32)
    mine = mine.astype(jnp.bfloat16)
    return mine, exchange_chips(mine)


def rounded(values):
    return lax.reduce_precision(values, exponent_bits=8, mantissa_bits=7)


def sum_lines(lines, spot):
    chips = lines.shape[0]
    chip, core = spot // 2, spot % 2
    near = swap_core(pick(lines, 1 - core, 1).astype(jnp.bfloat16)).astype(jnp.float32)
    lines = rounded(pick(lines, core, 1) + near)
    if lax.axis_size("ctx") == 2:
        both = lines + swap_ctx(lines.astype(jnp.bfloat16)).astype(jnp.float32)
    else:
        both = lax.psum(lines.astype(jnp.bfloat16), "ctx").astype(jnp.float32)
    lines = both.astype(jnp.bfloat16)
    total = pick(lines, chip, 0).astype(jnp.float32)
    for step in range(1, chips):
        sent = pick(lines, (chip + step) % chips, 0)
        total = total + lax.ppermute(sent, "fsdp", chip_shift(step)).astype(jnp.float32)
    return total


def spread_chips(parts):
    return jnp.sum(parts.astype(jnp.float32), axis=0).astype(jnp.bfloat16)


def spread_end(total, halves, *gate):
    if lax.axis_size("ctx") != 2:
        return lax.psum(total, "ctx").reshape(halves, -1, total.shape[1])
    other = after(swap_ctx(total), *gate)
    leading = lax.axis_index("ctx") == 0
    return jnp.stack([jnp.where(leading, total, other), jnp.where(leading, other, total)])


def other_ctx(rows, axis):
    if lax.axis_size("ctx") != 2:
        return lax.all_gather(rows, "ctx", axis=axis, tiled=True)
    return swap_ctx(rows)


def other_tokens(tokens, gate):
    seq_count = tokens.shape[0]
    if lax.axis_size("ctx") != 2 or lax.axis_size("tp") != 2 or seq_count % 2:
        return other_ctx(tokens, 1)
    side = lax.axis_index("tp")
    halves = tokens.reshape(2, seq_count // 2, *tokens.shape[1:])
    mine = after(swap_ctx(pick(halves, side, 0)), gate)
    theirs = swap_tp(mine)
    return jnp.concatenate(
        [jnp.where(side == 0, mine, theirs), jnp.where(side == 0, theirs, mine)]
    )


EXTRA = 16


def body(
    tokens,
    picture_starts,
    ln1_gain,
    ln1_shift,
    w_qkv,
    qv_bias,
    w_proj,
    proj_bias,
    ln2_gain,
    ln2_shift,
    w_fc1,
    fc1_bias,
    w_fc2,
    fc2_bias,
    out_grad,
):
    seq_count, local_len, width = tokens.shape
    fsdp = lax.axis_size("fsdp")
    chips = fsdp // 2
    ranks = lax.axis_size("ctx")
    rank = lax.axis_index("ctx")
    full_len = ranks * local_len
    local_width = w_qkv.shape[2]
    local_heads = local_width // HD
    units = w_fc1.shape[1]
    sequences = range(seq_count)
    spot = lax.axis_index("fsdp")
    side = lax.axis_index("tp")
    here = jnp.stack([spot // 2, spot % 2, rank, side]).astype(jnp.int32)
    place = jnp.stack([rank, jnp.int32(ranks)]).astype(jnp.int32)
    piece_ids = jnp.arange(full_len // PIECE, dtype=jnp.int32)
    pictures = jnp.any(
        piece_ids[None, :, None] == (picture_starts // PIECE)[:, None, :], axis=2
    ).astype(jnp.int32)

    block = ln1_gain.shape[0]
    qv_size, fc1_size = qv_bias.size, fc1_bias.size
    qv_lines = qv_size // block
    small = jnp.concatenate(
        [
            jnp.stack([ln1_gain, ln1_shift, proj_bias, ln2_gain, ln2_shift, fc2_bias]),
            qv_bias.reshape(-1, block),
            fc1_bias.reshape(-1, block),
        ]
    )
    small = jnp.pad(small, ((0, EXTRA - small.shape[0]), (0, 0)))
    qkv_bundle = gather_chips(halves_of(w_qkv.reshape(-1, 3 * local_width)))
    far_proj = swap_tp(w_proj)
    proj_halves = halves_of(
        jnp.concatenate(
            [jnp.where(side == 0, w_proj, far_proj), jnp.where(side == 0, far_proj, w_proj)]
        )
    )
    small = jnp.broadcast_to(small, (proj_halves.shape[0], *small.shape))
    proj_halves = jnp.concatenate([proj_halves, small], axis=1)
    proj_bundle = gather_chips(after(proj_halves, qkv_bundle))
    fc2_pieces = shift_chips(after(halves_of(w_fc2), qkv_bundle))
    fc1_bundle = gather_chips(after(w_fc1[None], proj_bundle))
    far_tokens = other_tokens(tokens, proj_bundle)
    full_qkv = placed_rows(gather_rest(qkv_bundle), here, "place_qkv", 0)
    mine = swap_core(proj_bundle)

    first = jnp.where(spot % 2 == 0, proj_bundle, mine)[:, -EXTRA:]
    second = jnp.where(spot % 2 == 0, mine, proj_bundle)[:, -EXTRA:]
    smalls = jnp.stack([first, second], axis=1).reshape(fsdp, EXTRA, block).astype(jnp.float32)
    vectors = [smalls[:, i].reshape(-1) for i in range(6)]
    gain_one, shift_one, bias_proj, gain_two, shift_two, bias_fc2 = vectors
    qv_rows = smalls[:, 6 : 6 + qv_lines].reshape(fsdp, 2, local_heads, HD // fsdp)
    qv_rows = qv_rows.transpose(1, 2, 0, 3).reshape(2, local_width)
    bias_fc1 = smalls[:, 6 + qv_lines : 6 + qv_lines + fc1_size // block]
    bias_fc1 = bias_fc1.reshape(fsdp, units // HD, HD // fsdp).transpose(1, 0, 2).reshape(1, -1)
    bias_qkv = jnp.concatenate([qv_rows[0], jnp.zeros_like(qv_rows[0]), qv_rows[1]])
    lines = jnp.stack([bias_proj, gain_two, shift_two, gain_one])

    def project(rows):
        normed = layer_norm(rows.astype(jnp.float32), gain_one, shift_one).astype(jnp.bfloat16)
        result = jnp.einsum("sld,de->sle", normed, full_qkv, preferred_element_type=jnp.float32)
        return normed, (result + bias_qkv).astype(jnp.bfloat16)

    normed_one, triple = project(tokens)
    _, far_triple = project(far_tokens)
    proj_bundles = gather_rest(proj_bundle, triple, near=mine)
    fc2_bundle = jnp.stack(after(tuple(fc2_pieces), full_qkv))
    fc2_near = swap_core(fc2_bundle)
    attended, logs = [], []
    for index in sequences:
        gate = [attended[-1], fc2_near] if index else [fc2_bundle, proj_bundles[-1]]
        heads, log = attention_forward(triple, far_triple, after(place, *gate), pictures, index)
        attended.append(heads)
        logs.append(log)
    tp_attended = [swap_tp(heads) for heads in attended]
    tp_attended[0] = after(tp_attended[0], attended[-1])
    fc1_bundle = after(fc1_bundle, attended[0])
    fc1_bundles = [fc1_bundle, swap_core(fc1_bundle)]
    fc2_bundles = gather_rest(fc2_bundle, tp_attended[0], near=fc2_near)
    all_attended = jnp.stack(attended)
    weights = [proj_bundles, fc1_bundles, fc2_bundles]
    if block % PAIR:
        order = lax.rem(here[0] + chips - jnp.arange(chips, dtype=jnp.int32), chips)
        weights = [
            [placed_columns_plain([b[:, :-EXTRA] for b in proj_bundles], here)],
            fc1_bundles,
            [placed_columns_plain([b[order] for b in fc2_bundles], here)],
        ]
    all_logs = jnp.stack(logs)
    residuals, normed_two, actives, hidden_grads, feeds, backs, swapped_twos = [], [], [], [], [], [], []
    hidden_sums = 0.0
    for index in sequences:
        gate = [backs[-1], tp_attended[index]] if index else []
        residual, normed, active, hidden_grad, feed, back, hidden_sum, own_proj = feed_forward(
            attended[index],
            after(tp_attended[index], *backs[-1:]),
            tokens,
            out_grad,
            lines,
            bias_fc1,
            weights,
            after(here, *gate),
            index,
        )
        residuals.append(residual)
        normed_two.append(normed)
        actives.append(active)
        hidden_grads.append(hidden_grad)
        feeds.append(feed)
        backs.append(back)
        swapped_twos.append(swap_tp(back))
        hidden_sums = hidden_sums + hidden_sum[0]
        if index == 0:
            far_logs = other_ctx(after(all_logs, back), 3)
            far_attended = other_ctx(after(all_attended, far_logs), 1)

    fc2_groups = [([(out_grad, s) for s in sequences], actives)]
    fc1_groups = [([(normed[None], 0) for normed in normed_two], hidden_grads)]
    branches, head_grads, far_head_grads = [], [], []
    two_sums = 0.0
    gate = backs[-1]
    for index in sequences:
        branch, head_grad, two_sum = norm_two_backward(
            backs[index],
            swapped_twos[index],
            residuals[index],
            out_grad,
            lines,
            own_proj,
            after(here, gate),
            index,
        )
        branches.append(branch)
        head_grads.append(head_grad)
        far_head_grads.append(other_ctx(head_grad, 0))
        two_sums = two_sums + two_sum
        if index == 0:
            blocks_fc2 = gradient_blocks(fc2_groups, after(here, head_grad), "grad_fc2")
            gate = blocks_fc2[1]
    cross_fc2 = cross_ctx(*blocks_fc2, head_grads[-1])
    fc1_groups.append(([(branch[None], 0) for branch in branches], attended))
    blocks_fc1 = gradient_blocks(
        fc1_groups, after(here, cross_fc2[1], far_attended, far_logs), "grad_fc1_proj"
    )

    grad_triples, back_ones, swapped_ones, outputs = [], [], [], []
    one_sums, triple_sums = 0.0, 0.0
    gate = (blocks_fc1[1],)
    for index in sequences:
        if index == 0:
            feed = after(feeds[0], *gate)
            swapped_feed = swap_tp(feed)
        grad_triple = attention_backward(
            (triple, attended[index], head_grads[index], logs[index]),
            (far_triple, far_attended[index], far_head_grads[index], far_logs[index]),
            after(place, *gate),
            pictures,
            index,
        )
        gate = (grad_triple,)
        if index == 0:
            gate, arrived_fc2 = cross_chips(cross_fc2, grad_triple)
            cross_fc1 = cross_ctx(*blocks_fc1, gate)
            gate = (cross_fc1[1],)
        grad_triples.append(grad_triple)
        if index == seq_count - 1:
            total_fc2 = spread_chips(after(arrived_fc2, grad_triple))
            part_fc1, arrived_fc1 = cross_chips(cross_fc1, total_fc2)
            last_groups = [([(normed_one, s) for s in sequences], grad_triples)]
            blocks_last = gradient_blocks(last_groups, after(here, part_fc1), "grad_last")
            gate = (blocks_last[1], *swapped_ones)
        back_one, one_sum, triple_sum = qkv_backward(
            grad_triple, tokens, full_qkv, after(here, *gate), index
        )
        gate = (back_one, swapped_feed)
        back_ones.append(back_one)
        swapped_ones.append(swap_tp(back_one))
        one_sums = one_sums + one_sum
        triple_sums = triple_sums + triple_sum[0]

    def finish_output(index, mine, theirs):
        total = mine.astype(jnp.float32) + theirs.astype(jnp.float32)
        outputs.append((residuals[index] + total + bias_fc2).astype(jnp.bfloat16))

    finish_output(0, feed, after(swapped_feed, back_ones[-1]))
    last_feeds = [after(feeds[index], back_ones[0]) for index in range(1, seq_count)]
    last_swapped = [swap_tp(feed) for feed in last_feeds]

    out_sums = jnp.sum(out_grad.astype(jnp.float32), axis=(0, 1))
    grad_qv = jnp.concatenate([triple_sums[:local_width], triple_sums[2 * local_width :]])
    vectors = [one_sums[0], one_sums[1], two_sums[2], two_sums[0], two_sums[1], out_sums]
    packed = jnp.concatenate(
        [vector.reshape(fsdp, block) for vector in vectors]
        + [
            grad_qv.reshape(2, local_heads, fsdp, HD // fsdp)
            .transpose(2, 0, 1, 3)
            .reshape(fsdp, -1),
            hidden_sums.reshape(-1, fsdp, HD // fsdp).transpose(1, 0, 2).reshape(fsdp, -1),
        ],
        axis=1,
    )
    def norm_one(index, *gate):
        return norm_one_backward(
            back_ones[index],
            swapped_ones[index],
            tokens,
            branches[index],
            lines,
            after(here, *gate),
            index,
        )

    total_fc1 = spread_chips(after(arrived_fc1, back_ones[-1]))
    cross_last = cross_ctx(*blocks_last, back_ones[-1])
    grad_tokens = [norm_one(0, cross_last[1])]
    part_last, arrived_last = cross_chips(cross_last, grad_tokens[0])
    for index in range(1, seq_count):
        finish_output(index, last_feeds[index - 1], after(last_swapped[index - 1], part_last))
    for index in range(1, seq_count):
        grad_tokens.append(norm_one(index, part_last, *last_swapped))
    total_last = spread_chips(arrived_last)
    sums_fc2 = spread_end(after(total_fc2, part_last), 2, total_last)
    sums_fc1 = spread_end(after(total_fc1, part_last), 2, total_last)
    sums_last = spread_end(total_last, 2)
    small = sum_lines(after(packed, part_last).reshape(chips, 2, -1), spot)
    norm_one = rounded(after(small[: 2 * block], total_last))
    norm_one = norm_one + swap_tp(norm_one.astype(jnp.bfloat16)).astype(jnp.float32)
    small = small.astype(jnp.float32)
    vectors = [norm_one[:block], norm_one[block:]]
    vectors += [small[i * block : (i + 1) * block] for i in range(2, 6)]
    shard_qv = small[6 * block : 6 * block + qv_size].reshape(qv_bias.shape)
    shard_fc1_bias = small[6 * block + qv_size :][:fc1_size].reshape(fc1_bias.shape)
    sums_last = sums_last.reshape(block, -1).astype(jnp.float32)
    sums_fc1 = sums_fc1.reshape(block, -1).astype(jnp.float32)
    return (
        jnp.stack(outputs),
        jnp.stack(grad_tokens),
        vectors[0],
        vectors[1],
        sums_last.reshape(-1, 3, local_width),
        shard_qv,
        sums_fc1[:, units:].T,
        vectors[2],
        vectors[3],
        vectors[4],
        sums_fc1[:, :units],
        shard_fc1_bias,
        sums_fc2.reshape(block, -1).astype(jnp.float32).T,
        vectors[5],
    )


def solution(mesh):
    return jax.shard_map(
        body,
        mesh=mesh,
        in_specs=(
            P("fsdp", "ctx", None),
            P("fsdp", None),
            P("fsdp"),
            P("fsdp"),
            P("fsdp", None, "tp"),
            P(None, "tp", "fsdp"),
            P("tp", "fsdp"),
            P("fsdp"),
            P("fsdp"),
            P("fsdp"),
            P("fsdp", "tp"),
            P("tp", "fsdp"),
            P("tp", "fsdp"),
            P("fsdp"),
            P("fsdp", "ctx", None),
        ),
        out_specs=(
            P("fsdp", "ctx", None),
            P("fsdp", "ctx", None),
            P("fsdp"),
            P("fsdp"),
            P("fsdp", None, "tp"),
            P(None, "tp", "fsdp"),
            P("tp", "fsdp"),
            P("fsdp"),
            P("fsdp"),
            P("fsdp"),
            P("fsdp", "tp"),
            P("tp", "fsdp"),
            P("tp", "fsdp"),
            P("fsdp"),
        ),
        check_vma=False,
    )
```

```python
import jax
import jax.numpy as jnp
from jax import lax
from jax.experimental import pallas as pl
from jax.experimental.pallas import tpu as pltpu
from jax.sharding import PartitionSpec as P

HD = 64
PAIR = 2 * HD
PIECE = 256
SCALE = HD ** (-0.5)
KERNEL_VMEM = 56 * 1024 * 1024

epsilon = 1e-05
masked_value = -1e30


def layer_norm(values, gain_vec, shift_vec):
    average = jnp.mean(values, axis=-1, keepdims=True)
    centred = values - average
    variance = jnp.mean(centred * centred, axis=-1, keepdims=True)
    return centred * lax.rsqrt(variance + epsilon) * gain_vec + shift_vec


NT = (((1,), (1,)), ((), ()))


def dot_nt(left, right):
    return lax.dot_general(left, right, NT, preferred_element_type=jnp.float32)


def dot_nn(left, right):
    return jnp.dot(left, right, preferred_element_type=jnp.float32)


def head_lanes(head):
    lanes = lax.broadcasted_iota(jnp.int32, (1, PAIR), 1)
    return (lanes >= head * HD) & (lanes < (head + 1) * HD)


def only_head(rows, head):
    return jnp.where(head_lanes(head), rows, jnp.zeros_like(rows))


def diagonal_mask(scores, joined):
    key_row = lax.broadcasted_iota(jnp.int32, scores.shape, 0)
    query_lane = lax.broadcasted_iota(jnp.int32, scores.shape, 1)
    return (key_row <= query_lane) | joined


def chunk_start(step, place, local_len, chunks):
    return 0 if chunks == 1 else pl.multiple_of(step * local_len, local_len)


SCORE_TILE = 32


def score_tiles(count):
    return [slice(start, start + SCORE_TILE) for start in range(0, count, SCORE_TILE)]


def folded(rows, combine):
    parts = [rows[start : start + 8] for start in range(0, rows.shape[0], 8)]
    while len(parts) > 1:
        parts = [
            combine(parts[i], parts[i + 1]) if i + 1 < len(parts) else parts[i]
            for i in range(0, len(parts), 2)
        ]
    return parts[0]


def attention_forward_kernel(
    place, pictures, q_ref, k_ref, v_ref, k_far, v_far, out_ref, log_ref, scores, weights, values
):
    rank = place[0]
    sequence = place[2]
    local_len = q_ref.shape[1]
    blocks = local_len // PIECE
    chunks = k_far.shape[1] // local_len
    values[...] = v_ref[0].T
    states = [(head, block) for head in range(2) for block in range(blocks)]
    scaled, peaks = [], []
    for index, (head, block) in enumerate(states):
        query = only_head(q_ref[0, block * PIECE : (block + 1) * PIECE, :] * SCALE, head)
        scaled.append(query)
        joined = pictures[sequence, rank * blocks + block] > 0
        count = (block + 1) * PIECE
        scores[index, :count] = dot_nt(k_ref[0, :count], query)
        peak = jnp.full((8, PIECE), masked_value, jnp.float32)
        for tile in score_tiles(count):
            part = scores[index, tile]
            if tile.start >= block * PIECE:
                key_row = lax.broadcasted_iota(jnp.int32, part.shape, 0) + (
                    tile.start - block * PIECE
                )
                lane = lax.broadcasted_iota(jnp.int32, part.shape, 1)
                part = jnp.where((key_row <= lane) | joined, part, masked_value)
                scores[index, tile] = part
            peak = jnp.maximum(peak, folded(part, jnp.maximum))
        peaks.append(peak)

    def far_scores(step, carried):
        keys = k_far[0, pl.ds(chunk_start(step, place, local_len, chunks), local_len), :]
        base = pl.multiple_of((step + 1) * local_len, local_len)
        after = []
        for index, peak in enumerate(carried):
            part = dot_nt(keys, scaled[index])
            scores[index, pl.ds(base, local_len)] = part
            for tile in score_tiles(local_len):
                peak = jnp.maximum(peak, folded(part[tile], jnp.maximum))
            after.append(peak)
        return after

    peaks = lax.fori_loop(0, rank, far_scores, peaks)
    peaks = [jnp.max(peak, axis=0, keepdims=True) for peak in peaks]
    gathered = []
    for index, (head, block) in enumerate(states):
        count = (block + 1) * PIECE
        total = jnp.zeros((8, PIECE), jnp.float32)
        for tile in score_tiles(count):
            weight = jnp.exp(scores[index, tile] - peaks[index])
            total = total + folded(weight, jnp.add)
            weights[index, tile] = weight.astype(jnp.bfloat16)
        gathered.append(
            (total, dot_nn(values[head * HD : (head + 1) * HD, :count], weights[index, :count]))
        )

    def far_values(step, carried):
        base = pl.multiple_of((step + 1) * local_len, local_len)
        far = v_far[0, pl.ds(chunk_start(step, place, local_len, chunks), local_len), :].T
        after = []
        for index, (total, sums) in enumerate(carried):
            head = states[index][0]
            for tile in score_tiles(local_len):
                weight = jnp.exp(
                    scores[index, pl.ds(base + tile.start, SCORE_TILE)] - peaks[index]
                )
                total = total + folded(weight, jnp.add)
                weights[index, tile] = weight.astype(jnp.bfloat16)
            sums = sums + dot_nn(far[head * HD : (head + 1) * HD], weights[index])
            after.append((total, sums))
        return after

    gathered = lax.fori_loop(0, rank, far_values, gathered)
    for block in range(blocks):
        rows = slice(block * PIECE, (block + 1) * PIECE)
        halves = []
        for head in range(2):
            index = head * blocks + block
            total = jnp.sum(gathered[index][0], axis=0, keepdims=True)
            halves.append(gathered[index][1] / total)
            log_ref[0, head : head + 1, rows] = peaks[index] + jnp.log(total)
        out_ref[rows, :] = jnp.concatenate(halves, axis=0).T.astype(out_ref.dtype)


def attention_forward(triple, far, place, pictures, index):
    place = jnp.concatenate([place, jnp.full((1,), index, jnp.int32)])
    _, local_len, triple_width = triple.shape
    far_len = far.shape[1]
    local_width = triple_width // 3
    pairs = local_width // PAIR

    def part(length, offset):
        return pl.BlockSpec(
            (1, length, PAIR), lambda p, place, pics: (index, 0, offset * pairs + p)
        )

    return pl.pallas_call(
        attention_forward_kernel,
        grid_spec=pltpu.PrefetchScalarGridSpec(
            num_scalar_prefetch=2,
            grid=(pairs,),
            in_specs=[
                part(local_len, 0),
                part(local_len, 1),
                part(local_len, 2),
                part(far_len, 1),
                part(far_len, 2),
            ],
            out_specs=[
                pl.BlockSpec((local_len, PAIR), lambda p, place, pics: (0, p)),
                pl.BlockSpec((1, 2, local_len), lambda p, place, pics: (p, 0, 0)),
            ],
            scratch_shapes=[
                pltpu.VMEM((2 * local_len // PIECE, local_len + far_len, PIECE), jnp.float32),
                pltpu.VMEM((2 * local_len // PIECE, local_len, PIECE), jnp.bfloat16),
                pltpu.VMEM((PAIR, local_len), jnp.bfloat16),
            ],
        ),
        out_shape=[
            jax.ShapeDtypeStruct((local_len, local_width), jnp.bfloat16),
            jax.ShapeDtypeStruct((pairs, 2, local_len), jnp.float32),
        ],
        compiler_params=pltpu.CompilerParams(vmem_limit_bytes=KERNEL_VMEM),
        cost_estimate=pl.CostEstimate(flops=50000000000, bytes_accessed=0, transcendentals=0),
        name="attention_forward",
    )(place, pictures, triple, triple, triple, far, far)


def attention_backward_kernel(
    place,
    pictures,
    q_ref,
    k_ref,
    v_ref,
    out_ref,
    grad_ref,
    log_ref,
    q_far,
    k_far,
    v_far,
    out_far,
    grad_far,
    log_far,
    triple_ref,
):
    rank = place[0]
    ranks = place[1]
    sequence = place[2]
    pair = pl.program_id(0)
    local_len = triple_ref.shape[0]
    local_width = triple_ref.shape[1] // 3
    blocks = local_len // PIECE
    chunks = k_far.shape[1] // local_len

    def sides_of(queries, grads, outs, logs):
        turned = (grads.astype(jnp.float32) * outs.astype(jnp.float32)).T
        queries = queries * SCALE
        sides = []
        for head in range(2):
            delta = jnp.sum(turned[head * HD : (head + 1) * HD], axis=0, keepdims=True)
            sides.append(
                (
                    only_head(queries, head),
                    only_head(grads, head),
                    logs[head : head + 1],
                    delta,
                )
            )
        return sides

    def pieces(keys, values, query, grad, log, delta, mask=None):
        scores = dot_nt(keys, query)
        probs = jnp.exp(scores - log)
        if mask is not None:
            probs = jnp.where(mask(probs), probs, 0.0)
        grad_probs = dot_nt(values, grad)
        return probs, (probs * (grad_probs - delta)).astype(jnp.bfloat16)

    key_own = k_ref[0]
    value_own = v_ref[0]
    key_turned = key_own.T
    sides = sides_of(q_ref[0], grad_ref[...], out_ref[...], log_ref[0])
    grad_keys = [None] * blocks
    grad_values = [None] * blocks
    grad_queries = []

    def add(total, part):
        return part if total is None else total + part

    for head in range(2):
        queries, grads, logs, deltas = sides[head]
        for block in range(blocks):
            rows = slice(block * PIECE, (block + 1) * PIECE)
            joined = pictures[sequence, rank * blocks + block] > 0
            grad_query = None
            for key_block in range(block + 1):
                key_rows = slice(key_block * PIECE, (key_block + 1) * PIECE)
                mask = (lambda p, j=joined: diagonal_mask(p, j)) if key_block == block else None
                probs, grad_scores = pieces(
                    key_own[key_rows],
                    value_own[key_rows],
                    queries[rows],
                    grads[rows],
                    logs[:, rows],
                    deltas[:, rows],
                    mask,
                )
                grad_values[key_block] = add(
                    grad_values[key_block], dot_nn(probs.astype(jnp.bfloat16), grads[rows])
                )
                grad_keys[key_block] = add(
                    grad_keys[key_block], dot_nn(grad_scores, queries[rows])
                )
                grad_query = add(
                    grad_query,
                    dot_nn(key_turned[head * HD : (head + 1) * HD, key_rows], grad_scores),
                )
            grad_queries.append(grad_query)

    def earlier(step, carried):
        start = chunk_start(step, place, local_len, chunks)
        keys = k_far[0, pl.ds(start, local_len), :]
        values = v_far[0, pl.ds(start, local_len), :]
        turned = keys.T
        after = []
        for index, total in enumerate(carried):
            head, block = index // blocks, index % blocks
            rows = slice(block * PIECE, (block + 1) * PIECE)
            queries, grads, logs, deltas = sides[head]
            _, grad_scores = pieces(
                keys, values, queries[rows], grads[rows], logs[:, rows], deltas[:, rows]
            )
            after.append(total + dot_nn(turned[head * HD : (head + 1) * HD], grad_scores))
        return after

    grad_queries = lax.fori_loop(0, rank, earlier, grad_queries)
    for block in range(blocks):
        rows = slice(block * PIECE, (block + 1) * PIECE)
        both = jnp.concatenate([grad_queries[head * blocks + block] for head in range(2)], axis=0)
        triple_ref[rows, pl.ds(pl.multiple_of(pair * PAIR, PAIR), PAIR)] = (
            (both * SCALE).T.astype(triple_ref.dtype)
        )

    def later(step, carried):
        start = chunk_start(step, place, local_len, chunks)
        window = pl.ds(start, local_len)
        sides = sides_of(
            q_far[0, window, :], grad_far[window, :], out_far[window, :], log_far[0, :, window]
        )
        keys_after, values_after = list(carried[0]), list(carried[1])
        for head in range(2):
            queries, grads, logs, deltas = sides[head]
            for block in range(blocks):
                rows = slice(block * PIECE, (block + 1) * PIECE)
                probs, grad_scores = pieces(
                    key_own[rows], value_own[rows], queries, grads, logs, deltas
                )
                values_after[block] = values_after[block] + dot_nn(
                    probs.astype(jnp.bfloat16), grads
                )
                keys_after[block] = keys_after[block] + dot_nn(grad_scores, queries)
        return keys_after, values_after

    grad_keys, grad_values = lax.fori_loop(rank + 1, ranks, later, (grad_keys, grad_values))
    for block in range(blocks):
        rows = slice(block * PIECE, (block + 1) * PIECE)
        for part, grads in ((1, grad_keys), (2, grad_values)):
            column = pl.multiple_of(part * local_width + pair * PAIR, PAIR)
            triple_ref[rows, pl.ds(column, PAIR)] = grads[block].astype(triple_ref.dtype)


def attention_backward(own, other, place, pictures, index):
    place = jnp.concatenate([place, jnp.full((1,), index, jnp.int32)])
    _, local_len, triple_width = own[0].shape
    pairs = triple_width // (3 * PAIR)
    specs = []
    for length in (local_len, other[0].shape[1]):
        for offset in range(3):
            specs.append(
                pl.BlockSpec(
                    (1, length, PAIR),
                    lambda p, place, pics, offset=offset: (index, 0, offset * pairs + p),
                )
            )
        specs += [pl.BlockSpec((length, PAIR), lambda p, place, pics: (0, p))] * 2
        specs.append(pl.BlockSpec((1, 2, length), lambda p, place, pics: (p, 0, 0)))
    return pl.pallas_call(
        attention_backward_kernel,
        grid_spec=pltpu.PrefetchScalarGridSpec(
            num_scalar_prefetch=2,
            grid=(pairs,),
            in_specs=specs,
            out_specs=pl.BlockSpec((local_len, triple_width), lambda p, place, pics: (0, 0)),
        ),
        out_shape=jax.ShapeDtypeStruct((local_len, triple_width), jnp.bfloat16),
        compiler_params=pltpu.CompilerParams(vmem_limit_bytes=KERNEL_VMEM),
        cost_estimate=pl.CostEstimate(flops=50000000000, bytes_accessed=0, transcendentals=0),
        name="attention_backward",
    )(place, pictures, *([own[0]] * 3), *own[1:], *([other[0]] * 3), *other[1:])


def core_swap():
    return [(place, place ^ 1) for place in range(lax.axis_size("fsdp"))]


PAIR_SWAP = [(0, 1), (1, 0)]


def swap_core(rows):
    return lax.ppermute(rows, "fsdp", core_swap())


def swap_ctx(rows):
    return lax.ppermute(rows, "ctx", PAIR_SWAP)


def swap_tp(rows):
    return lax.ppermute(rows, "tp", PAIR_SWAP)


def exchange_chips(rows):
    fsdp = lax.axis_size("fsdp")
    groups = [list(range(core, fsdp, 2)) for core in range(2)]
    return lax.all_to_all(
        rows, "fsdp", split_axis=0, concat_axis=0, tiled=True, axis_index_groups=groups
    )


def pick(array, index, axis):
    return lax.dynamic_index_in_dim(array, index, axis, keepdims=False)


def after(value, *others):
    return lax.optimization_barrier((value, *others))[0]


def halves_of(shard):
    halves = 2 if lax.axis_size("ctx") == 2 else 1
    return shard.reshape(halves, -1, shard.shape[1])


def gather_chips(halves):
    chips = lax.axis_size("fsdp") // 2
    part = pick(halves, lax.axis_index("ctx"), 0) if halves.shape[0] == 2 else halves[0]
    return exchange_chips(jnp.broadcast_to(part, (chips, *part.shape)))


def chip_shift(step):
    chips = lax.axis_size("fsdp") // 2
    return [
        (2 * chip + core, 2 * ((chip + step) % chips) + core)
        for chip in range(chips)
        for core in range(2)
    ]


def shift_chips(halves):
    part = pick(halves, lax.axis_index("ctx"), 0) if halves.shape[0] == 2 else halves[0]
    chips = lax.axis_size("fsdp") // 2
    return [part] + [lax.ppermute(part, "fsdp", chip_shift(step)) for step in range(1, chips)]


def gather_rest(bundle, *gate, near=None):
    bundles = [bundle, swap_core(bundle) if near is None else near]
    if lax.axis_size("ctx") == 2:
        across = after(swap_ctx(bundle), *gate)
        bundles += [across, swap_core(across)]
    return bundles


def kernel_call(kernel, scalars, arrays, in_specs, outs, out_specs, grid, name, scratch=(), flops=0):
    size = sum(array.size for array in arrays)
    return pl.pallas_call(
        kernel,
        grid_spec=pltpu.PrefetchScalarGridSpec(
            num_scalar_prefetch=len(scalars),
            grid=(grid,),
            in_specs=in_specs,
            out_specs=out_specs,
            scratch_shapes=list(scratch),
        ),
        out_shape=[jax.ShapeDtypeStruct(shape, dtype) for shape, dtype in outs],
        compiler_params=pltpu.CompilerParams(vmem_limit_bytes=KERNEL_VMEM),
        cost_estimate=pl.CostEstimate(flops=50000000000, bytes_accessed=0, transcendentals=0),
        name=name,
    )(*scalars, *arrays)


def owners(here, sides):
    for index in range(2 * sides):
        core = here[1] if index % 2 == 0 else 1 - here[1]
        yield core, ((here[2] if index < 2 else 1 - here[2]) if sides == 2 else 0)


def placed_rows(bundles, here, name, extra):
    fsdp = lax.axis_size("fsdp")
    sides = len(bundles) // 2
    chips, total, width = bundles[0].shape
    height = total - extra
    chunk = 512

    def kernel(here, *refs):
        for index, (core, side) in enumerate(owners(here, sides)):
            for chip in range(chips):
                refs[-1][(2 * chip + core) * sides + side] = refs[index][chip, :height]

    (result,) = kernel_call(
        kernel,
        [here],
        bundles,
        [pl.BlockSpec((chips, total, chunk), lambda i, here: (0, 0, i))] * (2 * sides),
        [((fsdp * sides, height, width), jnp.bfloat16)],
        [pl.BlockSpec((fsdp * sides, height, chunk), lambda i, here: (0, 0, i))],
        width // chunk,
        name,
    )
    return result.reshape(-1, width)


def placed_columns_plain(bundles, here):
    sides = []
    for mine, other in zip(bundles[::2], bundles[1::2]):
        first = jnp.where(here[1] == 0, mine, other)
        second = jnp.where(here[1] == 0, other, mine)
        both = jnp.stack([first, second], axis=1)
        sides.append(both.reshape(-1, *both.shape[2:]))
    if len(sides) == 2:
        sides = [
            jnp.where(here[2] == 0, sides[0], sides[1]),
            jnp.where(here[2] == 0, sides[1], sides[0]),
        ]
    fsdp, _, width = sides[0].shape
    return jnp.concatenate(sides, axis=1).transpose(1, 0, 2).reshape(-1, fsdp * width)


def weight_copies(bundles, target, here, columns, shifted=False):
    if len(bundles) == 1:
        yield bundles[0], target
        return
    sides = len(bundles) // 2
    for index, (core, side) in enumerate(owners(here, sides)):
        chips, _, width = bundles[index].shape
        height = target.shape[0] // (sides if columns else 2 * chips * sides)
        for chip in range(chips):
            source = bundles[index].at[chip, pl.ds(0, height)]
            block = 2 * (lax.rem(here[0] + chips - chip, chips) if shifted else chip) + core
            if columns:
                across = pl.ds(pl.multiple_of(block * width, width), width)
                yield source, target.at[pl.ds(pl.multiple_of(side * height, height), height), across]
            else:
                row = pl.multiple_of((block * sides + side) * height, height)
                yield source, target.at[pl.ds(row, height)]


UNITS = 1024
TILE = 16
ROOT = 0.7978845608028654
CUBIC = 0.044715


def feed_kernel(counts, here, *refs):
    own_ref, tp_ref, tokens_ref, grad_ref, vector_ref, bias_ref = refs[:6]
    at = 6
    bundles = []
    for count in counts:
        bundles.append(refs[at : at + count])
        at += count
    residual_out, normed_out, active_ref, hidden_ref, feed_ref, back_ref, sum_ref, proj_ref = refs[
        at : at + 8
    ]
    (
        proj,
        first,
        second,
        feed,
        back,
        hidden_pre,
        grad_active,
        residual_ref,
        normed_ref,
        semaphores,
    ) = refs[at + 8 :]
    step = pl.program_id(0)
    copies = [
        weight_copies(bundles[0], proj, here, True),
        weight_copies(bundles[1], first, here, False),
        weight_copies(bundles[2], second, here, True, True),
    ]
    made, number = [], 0
    for group in copies:
        made.append([])
        for source, place in group:
            made[-1].append(pltpu.make_async_copy(source, place, semaphores.at[number]))
            number += 1
    rows = proj.shape[0] // 2
    kept = pltpu.make_async_copy(
        proj.at[pl.ds(pl.multiple_of(here[3] * rows, rows), rows)],
        proj_ref,
        semaphores.at[number],
    )
    saved = [
        pltpu.make_async_copy(residual_ref, residual_out, semaphores.at[number + 1]),
        pltpu.make_async_copy(normed_ref, normed_out, semaphores.at[number + 2]),
    ]

    @pl.when(step == 0)
    def _():
        for group in made:
            for copy in group:
                copy.start()
        for copy in made[0]:
            copy.wait()
        kept.start()
        leading = here[3] == 0
        low = jnp.where(leading, own_ref[...], tp_ref[...])
        high = jnp.where(leading, tp_ref[...], own_ref[...])
        feed[...] = dot_nn(low, proj[:rows]) + dot_nn(high, proj[rows:])
        for start in range(0, feed.shape[0], TILE):
            lines = slice(start, start + TILE)
            residual = tokens_ref[0, lines].astype(jnp.float32) + feed[lines] + vector_ref[0:1]
            residual_ref[lines] = residual
            unit, _ = centred_rows(residual)
            normed_ref[lines] = (unit * vector_ref[1:2] + vector_ref[2:3]).astype(
                normed_ref.dtype
            )
        for copy in saved:
            copy.start()
        for copy in made[1]:
            copy.wait()

    units = pl.ds(pl.multiple_of(step * UNITS, UNITS), UNITS)
    hidden_pre[...] = dot_nn(normed_ref[...], first[:, units])

    @pl.when(step == 0)
    def _():
        for copy in made[2]:
            copy.wait()
        kept.wait()

    grad_active[...] = dot_nt(grad_ref[0], second[units])
    totals = jnp.zeros((TILE, UNITS), jnp.float32)
    for start in range(0, feed.shape[0], TILE):
        lines = slice(start, start + TILE)
        hidden = hidden_pre[lines] + bias_ref[...]
        square = hidden * hidden
        bent = jnp.tanh(hidden * (ROOT + ROOT * CUBIC * square))
        share = 0.5 + 0.5 * bent
        active_ref[lines] = (hidden * share).astype(jnp.bfloat16)
        slope = share + hidden * (1.0 - bent * bent) * (
            0.5 * ROOT + 1.5 * ROOT * CUBIC * square
        )
        grad_hidden = (grad_active[lines] * slope).astype(jnp.bfloat16)
        hidden_ref[lines] = grad_hidden
        totals = totals + grad_hidden.astype(jnp.float32)
    sum_ref[...] = jnp.sum(totals, axis=0, keepdims=True)
    active = active_ref[...]
    feed_part = dot_nn(active, second[units])
    back_part = dot_nt(hidden_ref[...], first[:, units])

    @pl.when(step == 0)
    def _():
        feed[...] = feed_part
        back[...] = back_part

    @pl.when(step > 0)
    def _():
        feed[...] += feed_part
        back[...] += back_part

    @pl.when(step == pl.num_programs(0) - 1)
    def _():
        feed_ref[...] = feed[...].astype(feed_ref.dtype)
        back_ref[...] = back[...].astype(back_ref.dtype)
        for copy in saved:
            copy.wait()


def feed_forward(own, tp, tokens, out_grad, vectors, bias, weights, here, index):
    local_len, local_width = own.shape
    width = tokens.shape[2]
    units = bias.shape[1]
    counts = tuple(len(group) for group in weights)
    copies = sum(1 if len(group) == 1 else len(group) * group[0].shape[0] for group in weights)
    whole = lambda shape: pl.BlockSpec(shape, lambda j, here: (0,) * len(shape))
    row = pl.BlockSpec((1, local_len, width), lambda j, here: (index, 0, 0))
    block = pl.BlockSpec((local_len, UNITS), lambda j, here: (0, j))
    line = pl.BlockSpec((1, UNITS), lambda j, here: (0, j))
    flat = [array for group in weights for array in group]
    half, full = jnp.bfloat16, jnp.float32
    return kernel_call(
        lambda *refs: feed_kernel(counts, *refs),
        [here],
        [own, tp, tokens, out_grad, vectors, bias] + flat,
        [whole(own.shape), whole(own.shape), row, row, whole(vectors.shape), line]
        + [pl.BlockSpec(memory_space=pl.ANY)] * len(flat),
        [
            ((local_len, width), full),
            ((local_len, width), half),
            ((local_len, units), half),
            ((local_len, units), half),
            ((local_len, width), half),
            ((local_len, width), half),
            ((1, units), full),
            ((local_width, width), half),
        ],
        [pl.BlockSpec(memory_space=pl.ANY)] * 2
        + [block, block]
        + [whole((local_len, width)), whole((local_len, width)), line]
        + [pl.BlockSpec(memory_space=pl.ANY)],
        units // UNITS,
        "feed_forward",
        [
            pltpu.VMEM((2 * local_width, width), half),
            pltpu.VMEM((width, units), half),
            pltpu.VMEM((units, width), half),
            pltpu.VMEM((local_len, width), full),
            pltpu.VMEM((local_len, width), full),
            pltpu.VMEM((local_len, UNITS), full),
            pltpu.VMEM((local_len, UNITS), full),
            pltpu.VMEM((local_len, width), full),
            pltpu.VMEM((local_len, width), half),
            pltpu.SemaphoreType.DMA((copies + 3,)),
        ],
        flops=8 * local_len * width * units,
    )


ROWS = 256


def centred_rows(rows):
    average = jnp.mean(rows, axis=-1, keepdims=True)
    centred = rows - average
    spread = lax.rsqrt(jnp.mean(centred * centred, axis=-1, keepdims=True) + epsilon)
    return centred * spread, spread


def through_norm(grads, unit, spread, gain):
    scaled = grads * gain
    return spread * (
        scaled
        - jnp.mean(scaled, axis=-1, keepdims=True)
        - unit * jnp.mean(scaled * unit, axis=-1, keepdims=True)
    )


def accumulate(ref, totals):
    total = jnp.concatenate([jnp.sum(lines, axis=0, keepdims=True) for lines in totals])

    @pl.when(pl.program_id(0) == 0)
    def _():
        ref[...] = total

    @pl.when(pl.program_id(0) > 0)
    def _():
        ref[...] += total


def tiles_of(count):
    return [slice(start, start + TILE) for start in range(0, count, TILE)]


def norm_two_kernel(
    here, own_ref, tp_ref, residual_ref, grad_ref, vector_ref, proj_ref, branch_ref, heads_ref, sum_ref
):
    totals = [jnp.zeros((TILE, own_ref.shape[1]), jnp.float32)] * 3
    for lines in tiles_of(own_ref.shape[0]):
        grads = own_ref[lines].astype(jnp.float32) + tp_ref[lines].astype(jnp.float32)
        unit, spread = centred_rows(residual_ref[lines])
        total = grad_ref[0, lines].astype(jnp.float32) + through_norm(
            grads, unit, spread, vector_ref[1:2]
        )
        branch = total.astype(jnp.bfloat16)
        branch_ref[lines] = branch
        totals = [
            totals[0] + grads * unit,
            totals[1] + grads,
            totals[2] + branch.astype(jnp.float32),
        ]
    heads_ref[...] = dot_nt(branch_ref[...], proj_ref[...]).astype(heads_ref.dtype)
    accumulate(sum_ref, totals)


def norm_two_backward(own, tp, residual, out_grad, vectors, proj, here, index):
    local_len, width = own.shape
    local_width = proj.shape[0]
    whole = lambda shape: pl.BlockSpec(shape, lambda i, here: (0,) * len(shape))
    row = pl.BlockSpec((ROWS, width), lambda i, here: (i, 0))
    return kernel_call(
        norm_two_kernel,
        [here],
        [own, tp, residual, out_grad, vectors, proj],
        [row, row, row, pl.BlockSpec((1, ROWS, width), lambda i, here: (index, i, 0))]
        + [whole(vectors.shape), whole(proj.shape)],
        [
            ((local_len, width), jnp.bfloat16),
            ((local_len, local_width), jnp.bfloat16),
            ((3, width), jnp.float32),
        ],
        [row, pl.BlockSpec((ROWS, local_width), lambda i, here: (i, 0)), whole((3, width))],
        local_len // ROWS,
        "norm_two_backward",
        flops=2 * local_len * width * local_width,
    )


def qkv_back_kernel(here, grad_ref, tokens_ref, weight_ref, back_ref, sum_ref, triple_ref, back):
    back[...] = dot_nt(grad_ref[...], weight_ref[...])
    totals = [jnp.zeros((TILE, back.shape[1]), jnp.float32)] * 2
    triple = jnp.zeros((TILE, grad_ref.shape[1]), jnp.float32)
    for lines in tiles_of(back.shape[0]):
        part = back[lines]
        back_ref[lines] = part.astype(back_ref.dtype)
        unit, _ = centred_rows(tokens_ref[0, lines].astype(jnp.float32))
        totals = [totals[0] + part * unit, totals[1] + part]
        triple = triple + grad_ref[lines].astype(jnp.float32)
    accumulate(sum_ref, totals)
    accumulate(triple_ref, [triple])


def qkv_backward(grad_triple, tokens, weight, here, index):
    local_len, triple_width = grad_triple.shape
    width = tokens.shape[2]
    whole = lambda shape: pl.BlockSpec(shape, lambda i, here: (0,) * len(shape))
    return kernel_call(
        qkv_back_kernel,
        [here],
        [grad_triple, tokens, weight],
        [
            pl.BlockSpec((ROWS, triple_width), lambda i, here: (i, 0)),
            pl.BlockSpec((1, ROWS, width), lambda i, here: (index, i, 0)),
            whole(weight.shape),
        ],
        [
            ((local_len, width), jnp.bfloat16),
            ((2, width), jnp.float32),
            ((1, triple_width), jnp.float32),
        ],
        [
            pl.BlockSpec((ROWS, width), lambda i, here: (i, 0)),
            whole((2, width)),
            whole((1, triple_width)),
        ],
        local_len // ROWS,
        "qkv_backward",
        [pltpu.VMEM((ROWS, width), jnp.float32)],
        flops=2 * local_len * width * triple_width,
    )


def norm_one_kernel(here, own_ref, tp_ref, tokens_ref, residual_ref, vector_ref, out_ref):
    for lines in tiles_of(own_ref.shape[0]):
        grads = own_ref[lines].astype(jnp.float32) + tp_ref[lines].astype(jnp.float32)
        unit, spread = centred_rows(tokens_ref[0, lines].astype(jnp.float32))
        out_ref[lines] = (
            residual_ref[lines].astype(jnp.float32)
            + through_norm(grads, unit, spread, vector_ref[3:4])
        ).astype(out_ref.dtype)


def norm_one_backward(own, tp, tokens, residual, vectors, here, index):
    local_len, width = own.shape
    row = pl.BlockSpec((ROWS, width), lambda i, here: (i, 0))
    return kernel_call(
        norm_one_kernel,
        [here],
        [own, tp, tokens, residual, vectors],
        [row, row, pl.BlockSpec((1, ROWS, width), lambda i, here: (index, i, 0)), row]
        + [pl.BlockSpec(vectors.shape, lambda i, here: (0, 0))],
        [((local_len, width), jnp.bfloat16)],
        [row],
        local_len // ROWS,
        "norm_one_backward",
    )[0]


CHUNK = 512


def gradient_kernel(plan, here, *refs):
    chips, groups = plan
    step = pl.program_id(0)
    refs = list(refs)
    turned = refs.pop()
    outs = [refs.pop(-2), refs.pop()]
    rows = outs[0].shape[2]
    at = 0
    for first, last, sequences in groups:
        lefts = refs[at : at + 2 * sequences * chips]
        rights = refs[at + 2 * sequences * chips : at + sequences * (2 * chips + 1)]
        at += sequences * (2 * chips + 1)

        @pl.when(step == first)
        def _():
            for index, left in enumerate(lefts):
                which, rest = divmod(index, sequences * chips)
                sequence, chip = divmod(rest, chips)
                block = left.shape[2]
                turned[which, sequence, chip * block : (chip + 1) * block] = left[0].T

        @pl.when((step >= first) & (step < last))
        def _():
            for which in range(2):
                total = dot_nn(turned[which, 0], rights[0][...])
                for sequence in range(1, sequences):
                    total += dot_nn(turned[which, sequence], rights[sequence][...])
                total = total.astype(jnp.bfloat16).reshape(chips, 2, rows, -1)
                for half in range(2):
                    outs[which][half] = total[:, half]


def gradient_plain(groups, here):
    chips = lax.axis_size("fsdp") // 2
    columns = []
    for lefts, rights in groups:
        total = 0.0
        for (array, lead), right in zip(lefts, rights):
            total = total + lax.dot_general(
                array[lead], right, (((0,), (0,)), ((), ())), preferred_element_type=jnp.float32
            )
        columns.append(total)
    whole = jnp.concatenate(columns, axis=1)
    whole = whole.astype(jnp.bfloat16).reshape(chips, 2, 2, -1, whole.shape[1])
    whole = whole.transpose(2, 1, 0, 3, 4)
    return pick(whole, 1 - here[1], 1), pick(whole, here[1], 1)


def gradient_blocks(groups, here, name):
    chips = lax.axis_size("fsdp") // 2
    if groups[0][0][0][0].shape[2] % (2 * chips * PAIR):
        return gradient_plain(groups, here)
    arrays, specs, plan = [], [], []
    at = 0
    for lefts, rights in groups:
        first, last = at, at + rights[0].shape[1] // CHUNK
        at = last
        plan.append((first, last, len(rights)))
        tokens = rights[0].shape[0]
        for own in (0, 1):
            for array, lead in lefts:
                block = array.shape[2] // (2 * chips)
                for chip in range(chips):
                    arrays.append(array)
                    specs.append(
                        pl.BlockSpec(
                            (1, tokens, block),
                            lambda i, here, lead=lead, chip=chip, own=own: (
                                lead,
                                0,
                                2 * chip + (here[1] if own else 1 - here[1]),
                            ),
                        )
                    )
        for right in rights:
            arrays.append(right)
            specs.append(
                pl.BlockSpec(
                    (tokens, CHUNK),
                    lambda i, here, first=first, last=last: (
                        0,
                        jnp.clip(i, first, last - 1) - first,
                    ),
                )
            )
    half = block // 2
    whole = pl.BlockSpec((2, chips, half, CHUNK), lambda i, here: (0, 0, 0, i))
    plan = (chips, plan)
    return kernel_call(
        lambda *refs: gradient_kernel(plan, *refs),
        [here],
        arrays,
        specs,
        [((2, chips, half, at * CHUNK), jnp.bfloat16)] * 2,
        [whole, whole],
        at,
        name,
        [pltpu.VMEM((2, len(groups[0][1]), chips * block, tokens), jnp.bfloat16)],
    )


def cross_ctx(sent, kept, gate):
    received = after(swap_core(sent), gate)
    halves = [None, None]
    side = lax.axis_index("ctx")
    for which in range(2):
        index = (which + side) % 2
        total = pick(kept, index, 0).astype(jnp.float32) + pick(received, index, 0).astype(
            jnp.float32
        )
        halves[which] = total
    if lax.axis_size("ctx") != 2:
        low = jnp.where(side % 2 == 0, halves[0], halves[1])
        high = jnp.where(side % 2 == 0, halves[1], halves[0])
        return jnp.concatenate([low, high], axis=1), sent, None
    away = halves[1].astype(jnp.bfloat16)
    return halves[0], away, swap_ctx(away)


def cross_chips(crossing, gate):
    mine, _, coming = crossing
    if coming is not None:
        mine = mine + after(coming, gate).astype(jnp.float32)
    mine = mine.astype(jnp.bfloat16)
    return mine, exchange_chips(mine)


def rounded(values):
    return lax.reduce_precision(values, exponent_bits=8, mantissa_bits=7)


def sum_lines(lines, spot):
    chips = lines.shape[0]
    chip, core = spot // 2, spot % 2
    near = swap_core(pick(lines, 1 - core, 1).astype(jnp.bfloat16)).astype(jnp.float32)
    lines = rounded(pick(lines, core, 1) + near)
    if lax.axis_size("ctx") == 2:
        both = lines + swap_ctx(lines.astype(jnp.bfloat16)).astype(jnp.float32)
    else:
        both = lax.psum(lines.astype(jnp.bfloat16), "ctx").astype(jnp.float32)
    lines = both.astype(jnp.bfloat16)
    total = pick(lines, chip, 0).astype(jnp.float32)
    for step in range(1, chips):
        sent = pick(lines, (chip + step) % chips, 0)
        total = total + lax.ppermute(sent, "fsdp", chip_shift(step)).astype(jnp.float32)
    return total


def spread_chips(parts):
    return jnp.sum(parts.astype(jnp.float32), axis=0).astype(jnp.bfloat16)


def spread_end(total, halves, *gate):
    if lax.axis_size("ctx") != 2:
        return lax.psum(total, "ctx").reshape(halves, -1, total.shape[1])
    other = after(swap_ctx(total), *gate)
    leading = lax.axis_index("ctx") == 0
    return jnp.stack([jnp.where(leading, total, other), jnp.where(leading, other, total)])


def other_ctx(rows, axis):
    if lax.axis_size("ctx") != 2:
        return lax.all_gather(rows, "ctx", axis=axis, tiled=True)
    return swap_ctx(rows)


def other_tokens(tokens, gate):
    seq_count = tokens.shape[0]
    if lax.axis_size("ctx") != 2 or lax.axis_size("tp") != 2 or seq_count % 2:
        return other_ctx(tokens, 1)
    side = lax.axis_index("tp")
    halves = tokens.reshape(2, seq_count // 2, *tokens.shape[1:])
    mine = after(swap_ctx(pick(halves, side, 0)), gate)
    theirs = swap_tp(mine)
    return jnp.concatenate(
        [jnp.where(side == 0, mine, theirs), jnp.where(side == 0, theirs, mine)]
    )


EXTRA = 16


def body(
    tokens,
    picture_starts,
    ln1_gain,
    ln1_shift,
    w_qkv,
    qv_bias,
    w_proj,
    proj_bias,
    ln2_gain,
    ln2_shift,
    w_fc1,
    fc1_bias,
    w_fc2,
    fc2_bias,
    out_grad,
):
    seq_count, local_len, width = tokens.shape
    fsdp = lax.axis_size("fsdp")
    chips = fsdp // 2
    ranks = lax.axis_size("ctx")
    rank = lax.axis_index("ctx")
    full_len = ranks * local_len
    local_width = w_qkv.shape[2]
    local_heads = local_width // HD
    units = w_fc1.shape[1]
    sequences = range(seq_count)
    spot = lax.axis_index("fsdp")
    side = lax.axis_index("tp")
    here = jnp.stack([spot // 2, spot % 2, rank, side]).astype(jnp.int32)
    place = jnp.stack([rank, jnp.int32(ranks)]).astype(jnp.int32)
    piece_ids = jnp.arange(full_len // PIECE, dtype=jnp.int32)
    pictures = jnp.any(
        piece_ids[None, :, None] == (picture_starts // PIECE)[:, None, :], axis=2
    ).astype(jnp.int32)

    block = ln1_gain.shape[0]
    qv_size, fc1_size = qv_bias.size, fc1_bias.size
    qv_lines = qv_size // block
    small = jnp.concatenate(
        [
            jnp.stack([ln1_gain, ln1_shift, proj_bias, ln2_gain, ln2_shift, fc2_bias]),
            qv_bias.reshape(-1, block),
            fc1_bias.reshape(-1, block),
        ]
    )
    small = jnp.pad(small, ((0, EXTRA - small.shape[0]), (0, 0)))
    qkv_bundle = gather_chips(halves_of(w_qkv.reshape(-1, 3 * local_width)))
    far_proj = swap_tp(w_proj)
    proj_halves = halves_of(
        jnp.concatenate(
            [jnp.where(side == 0, w_proj, far_proj), jnp.where(side == 0, far_proj, w_proj)]
        )
    )
    small = jnp.broadcast_to(small, (proj_halves.shape[0], *small.shape))
    proj_halves = jnp.concatenate([proj_halves, small], axis=1)
    proj_bundle = gather_chips(after(proj_halves, qkv_bundle))
    fc2_pieces = shift_chips(after(halves_of(w_fc2), qkv_bundle))
    fc1_bundle = gather_chips(after(w_fc1[None], proj_bundle))
    far_tokens = other_tokens(tokens, proj_bundle)
    full_qkv = placed_rows(gather_rest(qkv_bundle), here, "place_qkv", 0)
    mine = swap_core(proj_bundle)

    first = jnp.where(spot % 2 == 0, proj_bundle, mine)[:, -EXTRA:]
    second = jnp.where(spot % 2 == 0, mine, proj_bundle)[:, -EXTRA:]
    smalls = jnp.stack([first, second], axis=1).reshape(fsdp, EXTRA, block).astype(jnp.float32)
    vectors = [smalls[:, i].reshape(-1) for i in range(6)]
    gain_one, shift_one, bias_proj, gain_two, shift_two, bias_fc2 = vectors
    qv_rows = smalls[:, 6 : 6 + qv_lines].reshape(fsdp, 2, local_heads, HD // fsdp)
    qv_rows = qv_rows.transpose(1, 2, 0, 3).reshape(2, local_width)
    bias_fc1 = smalls[:, 6 + qv_lines : 6 + qv_lines + fc1_size // block]
    bias_fc1 = bias_fc1.reshape(fsdp, units // HD, HD // fsdp).transpose(1, 0, 2).reshape(1, -1)
    bias_qkv = jnp.concatenate([qv_rows[0], jnp.zeros_like(qv_rows[0]), qv_rows[1]])
    lines = jnp.stack([bias_proj, gain_two, shift_two, gain_one])

    def project(rows):
        normed = layer_norm(rows.astype(jnp.float32), gain_one, shift_one).astype(jnp.bfloat16)
        result = jnp.einsum("sld,de->sle", normed, full_qkv, preferred_element_type=jnp.float32)
        return normed, (result + bias_qkv).astype(jnp.bfloat16)

    normed_one, triple = project(tokens)
    _, far_triple = project(far_tokens)
    proj_bundles = gather_rest(proj_bundle, triple, near=mine)
    fc2_bundle = jnp.stack(after(tuple(fc2_pieces), full_qkv))
    fc2_near = swap_core(fc2_bundle)
    attended, logs = [], []
    for index in sequences:
        gate = [attended[-1], fc2_near] if index else [fc2_bundle, proj_bundles[-1]]
        heads, log = attention_forward(triple, far_triple, after(place, *gate), pictures, index)
        attended.append(heads)
        logs.append(log)
    tp_attended = [swap_tp(heads) for heads in attended]
    tp_attended[0] = after(tp_attended[0], attended[-1])
    fc1_bundle = after(fc1_bundle, attended[0])
    fc1_bundles = [fc1_bundle, swap_core(fc1_bundle)]
    fc2_bundles = gather_rest(fc2_bundle, tp_attended[0], near=fc2_near)
    all_attended = jnp.stack(attended)
    weights = [proj_bundles, fc1_bundles, fc2_bundles]
    if block % PAIR:
        order = lax.rem(here[0] + chips - jnp.arange(chips, dtype=jnp.int32), chips)
        weights = [
            [placed_columns_plain([b[:, :-EXTRA] for b in proj_bundles], here)],
            fc1_bundles,
            [placed_columns_plain([b[order] for b in fc2_bundles], here)],
        ]
    all_logs = jnp.stack(logs)
    residuals, normed_two, actives, hidden_grads, feeds, backs, swapped_twos = [], [], [], [], [], [], []
    hidden_sums = 0.0
    for index in sequences:
        gate = [backs[-1], tp_attended[index]] if index else []
        residual, normed, active, hidden_grad, feed, back, hidden_sum, own_proj = feed_forward(
            attended[index],
            after(tp_attended[index], *backs[-1:]),
            tokens,
            out_grad,
            lines,
            bias_fc1,
            weights,
            after(here, *gate),
            index,
        )
        residuals.append(residual)
        normed_two.append(normed)
        actives.append(active)
        hidden_grads.append(hidden_grad)
        feeds.append(feed)
        backs.append(back)
        swapped_twos.append(swap_tp(back))
        hidden_sums = hidden_sums + hidden_sum[0]
        if index == 0:
            far_logs = other_ctx(after(all_logs, back), 3)
            far_attended = other_ctx(after(all_attended, far_logs), 1)

    fc2_groups = [([(out_grad, s) for s in sequences], actives)]
    fc1_groups = [([(normed[None], 0) for normed in normed_two], hidden_grads)]
    branches, head_grads, far_head_grads = [], [], []
    two_sums = 0.0
    gate = backs[-1]
    for index in sequences:
        branch, head_grad, two_sum = norm_two_backward(
            backs[index],
            swapped_twos[index],
            residuals[index],
            out_grad,
            lines,
            own_proj,
            after(here, gate),
            index,
        )
        branches.append(branch)
        head_grads.append(head_grad)
        far_head_grads.append(other_ctx(head_grad, 0))
        two_sums = two_sums + two_sum
        if index == 0:
            blocks_fc2 = gradient_blocks(fc2_groups, after(here, head_grad), "grad_fc2")
            gate = blocks_fc2[1]
    cross_fc2 = cross_ctx(*blocks_fc2, head_grads[-1])
    fc1_groups.append(([(branch[None], 0) for branch in branches], attended))
    blocks_fc1 = gradient_blocks(
        fc1_groups, after(here, cross_fc2[1], far_attended, far_logs), "grad_fc1_proj"
    )

    grad_triples, back_ones, swapped_ones, outputs = [], [], [], []
    one_sums, triple_sums = 0.0, 0.0
    gate = (blocks_fc1[1],)
    for index in sequences:
        if index == 0:
            feed = after(feeds[0], *gate)
            swapped_feed = swap_tp(feed)
        grad_triple = attention_backward(
            (triple, attended[index], head_grads[index], logs[index]),
            (far_triple, far_attended[index], far_head_grads[index], far_logs[index]),
            after(place, *gate),
            pictures,
            index,
        )
        gate = (grad_triple,)
        if index == 0:
            gate, arrived_fc2 = cross_chips(cross_fc2, grad_triple)
            cross_fc1 = cross_ctx(*blocks_fc1, gate)
            gate = (cross_fc1[1],)
        grad_triples.append(grad_triple)
        if index == seq_count - 1:
            total_fc2 = spread_chips(after(arrived_fc2, grad_triple))
            part_fc1, arrived_fc1 = cross_chips(cross_fc1, total_fc2)
            last_groups = [([(normed_one, s) for s in sequences], grad_triples)]
            blocks_last = gradient_blocks(last_groups, after(here, part_fc1), "grad_last")
            gate = (blocks_last[1], *swapped_ones)
        back_one, one_sum, triple_sum = qkv_backward(
            grad_triple, tokens, full_qkv, after(here, *gate), index
        )
        gate = (back_one, swapped_feed)
        back_ones.append(back_one)
        swapped_ones.append(swap_tp(back_one))
        one_sums = one_sums + one_sum
        triple_sums = triple_sums + triple_sum[0]

    def finish_output(index, mine, theirs):
        total = mine.astype(jnp.float32) + theirs.astype(jnp.float32)
        outputs.append((residuals[index] + total + bias_fc2).astype(jnp.bfloat16))

    finish_output(0, feed, after(swapped_feed, back_ones[-1]))
    last_feeds = [after(feeds[index], back_ones[0]) for index in range(1, seq_count)]
    last_swapped = [swap_tp(feed) for feed in last_feeds]

    out_sums = jnp.sum(out_grad.astype(jnp.float32), axis=(0, 1))
    grad_qv = jnp.concatenate([triple_sums[:local_width], triple_sums[2 * local_width :]])
    vectors = [one_sums[0], one_sums[1], two_sums[2], two_sums[0], two_sums[1], out_sums]
    packed = jnp.concatenate(
        [vector.reshape(fsdp, block) for vector in vectors]
        + [
            grad_qv.reshape(2, local_heads, fsdp, HD // fsdp)
            .transpose(2, 0, 1, 3)
            .reshape(fsdp, -1),
            hidden_sums.reshape(-1, fsdp, HD // fsdp).transpose(1, 0, 2).reshape(fsdp, -1),
        ],
        axis=1,
    )
    def norm_one(index, *gate):
        return norm_one_backward(
            back_ones[index],
            swapped_ones[index],
            tokens,
            branches[index],
            lines,
            after(here, *gate),
            index,
        )

    total_fc1 = spread_chips(after(arrived_fc1, back_ones[-1]))
    cross_last = cross_ctx(*blocks_last, back_ones[-1])
    grad_tokens = [norm_one(0, cross_last[1])]
    part_last, arrived_last = cross_chips(cross_last, grad_tokens[0])
    for index in range(1, seq_count):
        finish_output(index, last_feeds[index - 1], after(last_swapped[index - 1], part_last))
    for index in range(1, seq_count):
        grad_tokens.append(norm_one(index, part_last, *last_swapped))
    total_last = spread_chips(arrived_last)
    sums_fc2 = spread_end(after(total_fc2, part_last), 2, total_last)
    sums_fc1 = spread_end(after(total_fc1, part_last), 2, total_last)
    sums_last = spread_end(total_last, 2)
    small = sum_lines(after(packed, part_last).reshape(chips, 2, -1), spot)
    norm_one = rounded(after(small[: 2 * block], total_last))
    norm_one = norm_one + swap_tp(norm_one.astype(jnp.bfloat16)).astype(jnp.float32)
    small = small.astype(jnp.float32)
    vectors = [norm_one[:block], norm_one[block:]]
    vectors += [small[i * block : (i + 1) * block] for i in range(2, 6)]
    shard_qv = small[6 * block : 6 * block + qv_size].reshape(qv_bias.shape)
    shard_fc1_bias = small[6 * block + qv_size :][:fc1_size].reshape(fc1_bias.shape)
    sums_last = sums_last.reshape(block, -1).astype(jnp.float32)
    sums_fc1 = sums_fc1.reshape(block, -1).astype(jnp.float32)
    return (
        jnp.stack(outputs),
        jnp.stack(grad_tokens),
        vectors[0],
        vectors[1],
        sums_last.reshape(-1, 3, local_width),
        shard_qv,
        sums_fc1[:, units:].T,
        vectors[2],
        vectors[3],
        vectors[4],
        sums_fc1[:, :units],
        shard_fc1_bias,
        sums_fc2.reshape(block, -1).astype(jnp.float32).T,
        vectors[5],
    )


def solution(mesh):
    return jax.shard_map(
        body,
        mesh=mesh,
        in_specs=(
            P("fsdp", "ctx", None),
            P("fsdp", None),
            P("fsdp"),
            P("fsdp"),
            P("fsdp", None, "tp"),
            P(None, "tp", "fsdp"),
            P("tp", "fsdp"),
            P("fsdp"),
            P("fsdp"),
            P("fsdp"),
            P("fsdp", "tp"),
            P("tp", "fsdp"),
            P("tp", "fsdp"),
            P("fsdp"),
            P("fsdp", "ctx", None),
        ),
        out_specs=(
            P("fsdp", "ctx", None),
            P("fsdp", "ctx", None),
            P("fsdp"),
            P("fsdp"),
            P("fsdp", None, "tp"),
            P(None, "tp", "fsdp"),
            P("tp", "fsdp"),
            P("fsdp"),
            P("fsdp"),
            P("fsdp"),
            P("fsdp", "tp"),
            P("tp", "fsdp"),
            P("tp", "fsdp"),
            P("fsdp"),
        ),
        check_vma=False,
    )
```
